32 devices in a mesh: row: 8 (over y, x, core), col: 4 (over z).
Axes of the slice: x: 2, y: 2, z: 4, core: 2. Of those that a mesh axis runs over, the one named last changes fastest.
Arguments:
- tiles: bfloat16 [8192, 128, 128], P(('row', 'col'))
- tile_src: int32 [8192], P(('row', 'col')), may hold values from 0 to 15
- tile_slot: int32 [8192], P(('row', 'col')), may hold values from 0 to 127
- slot_block: int32 [4096], P(('row', 'col')), may hold values from 0 to 15
- out_degree: int32 [65536], P(('row', 'col')), may hold values from 512 to 2047
- good_seeds: int32 [128, 4096], P(None, ('row', 'col')), may hold values from 0 to 65535, as said below
- spam_cores: int32 [128, 2048], P(None, ('row', 'col')), may hold values from 0 to 65535, as said below
Outputs:
- trust: float32 [65536, 128], P(('row', 'col'))
- distrust: float32 [65536, 128], P(('row', 'col'))
The draws below stay inside these ranges and needn't reach their ends.
Inputs may be any that keep to these rules, and one draw needn't show every extreme that they name: `tile_slot`: slot s of a device belongs to the peer with index s // 4 along row+col. `slot_block`: entry p * 128 + s is the local index, among the 16 blocks held by peer s // 4, of the target block of slot s of device p. `good_seeds`: entries j * 128 to (j + 1) * 128 - 1 of each column's list are hosts of device j, from j * 2048 to (j + 1) * 2048 - 1. `spam_cores`: entries j * 64 to (j + 1) * 64 - 1 of each column's list are hosts of device j, from j * 2048 to (j + 1) * 2048 - 1.
All inputs are finite; a program needn't handle non-finite values.
Results may differ from the reference program's by a relative error of at most 0.0003.
Values may be sent and summed in bfloat16 or wider, within the bound.
A program may use at most 128 MiB of HBM per device.

```python
import math
import jax
import jax.numpy as jnp
import numpy as np
from jax import lax

BS = 128
S = 128
BLK_DEV = 16
TILES_DEV = 256
SLOTS_DEV = 128
TRUST_ITERS = 2
ANTI_ITERS = 2
CAP = 4
HOSTS_DEV = 2048
NB = 512
HOSTS = 65536
NTILES = 8192
SLOTS = 4096
GOOD_DEV = 128
K_GOOD = 4096
SPAM_DEV = 64
K_SPAM = 2048
N_ROW = 8
N_COL = 4


def draw_tiles(key, part):
    first, second, third = jax.random.split(key, 3)
    base = 4.6 * jnp.exp(jax.random.uniform(first, (NTILES, BS, BS), jnp.float32, math.log(0.0001), 0.0))
    lower, upper = (0.3, 3.0)
    row_scale = jnp.exp(jax.random.uniform(second, (NTILES, BS, 1), jnp.float32, math.log(lower), math.log(upper)))
    column_scale = jnp.exp(jax.random.uniform(third, (NTILES, 1, BS), jnp.float32, math.log(lower), math.log(upper)))
    return (base * row_scale * column_scale).astype(jnp.bfloat16)


def local_hosts(key, per_device, total):
    local = jax.random.randint(key, (S, total), 0, HOSTS_DEV, dtype=jnp.int32)
    owner = (jnp.arange(total, dtype=jnp.int32) // per_device).astype(jnp.int32)
    return (local + owner[None, :] * HOSTS_DEV).astype(jnp.int32)


def draw_good_seeds(key, part):
    return local_hosts(jax.random.fold_in(key, 11), GOOD_DEV, K_GOOD)


def draw_spam_cores(key, part):
    return local_hosts(jax.random.fold_in(key, 23), SPAM_DEV, K_SPAM)


def plant(values, key, least, high):
    longest = values.shape.index(max(values.shape))
    spots = []
    for shift in (0, 1):
        where = [jax.random.randint(jax.random.fold_in(key, axis), (), 0, length) for axis, length in enumerate(values.shape)]
        where[longest] = (where[longest] + shift) % values.shape[longest]
        spots.append(tuple(where))
    return values.at[spots[0]].set(least).at[spots[1]].set(high)


def rank_table(count, lean):
    loads = [(1 << 20) // math.isqrt(grade ** lean) + 1 for grade in range(1, count + 1)]
    deviation = 1 + sum(loads) // (1 << 30)
    return np.cumsum(np.array([max(1, weight // deviation) for weight in loads]))


def ranked_ids(stream_key, shape, amount, slope):
    grid = rank_table(amount, slope)
    pick = jax.random.randint(jax.random.fold_in(stream_key, 1), shape, 0, int(grid[amount - 1]))
    standing = jnp.searchsorted(jnp.asarray(grid, jnp.int32), pick, side="right")
    return jax.random.permutation(jax.random.fold_in(stream_key, 2), amount)[standing].astype(jnp.int32)


def setup_inputs(seed: int = 0) -> dict:
    key_list = jax.random.split(jax.random.key(seed), 8)
    tiles = draw_tiles(jax.random.fold_in(key_list[7], 71), 0)
    tile_src = plant(jax.random.randint(key_list[1], (NTILES,), 0, BLK_DEV), jax.random.fold_in(key_list[1], 1), 0, BLK_DEV - 1).astype(jnp.int32)
    tile_slot = plant(jax.random.randint(key_list[2], (NTILES,), 0, SLOTS_DEV), jax.random.fold_in(key_list[2], 1), 0, SLOTS_DEV - 1).astype(jnp.int32)
    slot_block = plant(ranked_ids(key_list[3], (SLOTS,), BLK_DEV, 1), jax.random.fold_in(key_list[3], 3), 0, BLK_DEV - 1).astype(jnp.int32)
    out_degree = plant(jax.random.randint(key_list[4], (HOSTS,), TILES_DEV * BS // (4 * BLK_DEV), TILES_DEV * BS // BLK_DEV), jax.random.fold_in(key_list[4], 1), TILES_DEV * BS // (4 * BLK_DEV), (TILES_DEV * BS // BLK_DEV) - 1).astype(jnp.int32)
    good_seeds = draw_good_seeds(jax.random.fold_in(key_list[7], 71), 0)
    spam_cores = draw_spam_cores(jax.random.fold_in(key_list[7], 71), 0)
    return dict(tiles=tiles, tile_src=tile_src, tile_slot=tile_slot, slot_block=slot_block, out_degree=out_degree, good_seeds=good_seeds, spam_cores=spam_cores)


def teleport(seeds, factor):
    column_index = jnp.broadcast_to(jnp.arange(S, dtype=jnp.int32)[:, None], seeds.shape)
    counts = jnp.zeros((HOSTS, S), jnp.float32).at[seeds, column_index].add(jnp.float32(1.0))
    return counts * jnp.float32(factor)


def reference(tiles, tile_src, tile_slot, slot_block, out_degree, good_seeds, spam_cores):
    devices = N_ROW * N_COL
    owner = (jnp.arange(NTILES, dtype=jnp.int32) // TILES_DEV).astype(jnp.int32)
    source_block = (owner * BLK_DEV + tile_src).astype(jnp.int32)
    global_slot = (owner * SLOTS_DEV + tile_slot).astype(jnp.int32)
    target_block = ((tile_slot // CAP) * BLK_DEV + slot_block[global_slot]).astype(jnp.int32)
    column_sums = jnp.sum(tiles, axis=1, dtype=jnp.float32)
    in_weight = 1.0 + jax.ops.segment_sum(column_sums, target_block, num_segments=NB).reshape(HOSTS)
    good_start = teleport(good_seeds, HOSTS_DEV / GOOD_DEV)
    spam_start = teleport(spam_cores, HOSTS_DEV / SPAM_DEV)
    grouped = tiles.reshape(devices, TILES_DEV, BS, BS)
    source_groups = source_block.reshape(devices, TILES_DEV)
    target_groups = target_block.reshape(devices, TILES_DEV)

    def forward(scaled):
        blocks = scaled.reshape(NB, BS, S)

        def one_group(total, group):
            weights, sources, targets = group
            products = jnp.einsum("kij,kis->kjs", weights.astype(jnp.float32), blocks[sources].astype(jnp.float32), precision=lax.Precision.HIGHEST)
            return total + jax.ops.segment_sum(products, targets, num_segments=NB), None

        total, _ = lax.scan(one_group, jnp.zeros((NB, BS, S), jnp.float32), (grouped, source_groups, target_groups))
        return total.reshape(HOSTS, S)

    def backward(share):
        blocks = share.reshape(NB, BS, S)

        def one_group(total, group):
            weights, sources, targets = group
            products = jnp.einsum("kij,kjs->kis", weights.astype(jnp.float32), blocks[targets].astype(jnp.float32), precision=lax.Precision.HIGHEST)
            return total + jax.ops.segment_sum(products, sources, num_segments=NB), None

        total, _ = lax.scan(one_group, jnp.zeros((NB, BS, S), jnp.float32), (grouped, source_groups, target_groups))
        return total.reshape(HOSTS, S)

    degree = out_degree.astype(jnp.float32)[:, None]
    trust = good_start
    for iteration in range(TRUST_ITERS):
        scaled = (trust / degree).astype(jnp.bfloat16)
        trust = 0.85 * forward(scaled) + 0.15 * good_start
    shield = 1.0 / (1.0 + trust)
    distrust = spam_start
    for iteration in range(ANTI_ITERS):
        share = (shield * distrust / in_weight[:, None]).astype(jnp.bfloat16)
        distrust = 0.85 * backward(share) + 0.15 * spam_start
    return trust, distrust
```

```python
import functools

import jax
import jax.numpy as jnp
from jax import lax
from jax.experimental import pallas as pl
from jax.experimental.pallas import tpu as pltpu
from jax.sharding import PartitionSpec as P

AXES = ("row", "col")
VM = pl.BlockSpec(memory_space=pltpu.VMEM)
SM = pl.BlockSpec(memory_space=pltpu.SMEM)
ANY = pl.BlockSpec(memory_space=pl.ANY)
F32 = jnp.float32
BF16 = jnp.bfloat16
WORD = 15
GROUP = 16
HALVES = 2
MESH = pl.DeviceIdType.MESH


def count_seeds(columns, source, target, step=0, pieces=1):
    blocks, seeds, size = target.shape
    hosts = blocks * size
    base = (lax.axis_index("row") * columns + lax.axis_index("col")) * hosts
    count = source.shape[1]
    factor = F32(hosts / count)
    block_iota = lax.broadcasted_iota(jnp.int32, (blocks, count), 0) * size
    lane_iota = lax.broadcasted_iota(jnp.int32, (size, count), 0)

    def one(s, _):
        local = source[pl.ds(s, 1), :] - base
        shifted = local - block_iota
        inside = jnp.where((shifted >= 0) & (shifted < size), F32(1), F32(0)).astype(BF16)
        start = jnp.max(jnp.where(local >= block_iota, block_iota, 0), axis=0, keepdims=True)
        lane = jnp.where(lane_iota == local - start, F32(1), F32(0)).astype(BF16)
        counts = lax.dot_general(
            inside, lane, (((1,), (1,)), ((), ())), preferred_element_type=F32
        )
        for b in range(blocks):
            target[b, pl.ds(s, 1), :] = counts[b : b + 1, :] * factor
        return 0

    share = seeds // pieces
    lax.fori_loop(step * share, (step + 1) * share, one, 0, unroll=4)


def exponent_of(peak):
    return jnp.floor(jnp.log2(jnp.maximum(peak, F32(2.0**-100)))) + F32(1)


def to_words(value):
    return jnp.clip(jnp.floor(value + F32(0.5)), F32(-32767), F32(32767))


def pack(first, cap, part, bits, acc, block_ref, out_ref):
    peers = out_ref.shape[0]
    size = acc.shape[2]
    halves = size // part
    tail = out_ref.shape[1] - cap * size

    def one(p, _):
        exps, cols = [], []
        for c in range(cap):
            n = p * cap + c
            value = acc[n, :size, :]
            e = exponent_of(jnp.max(jnp.abs(value), axis=0, keepdims=True))
            words = to_words(value * jnp.exp2(WORD - e)).astype(jnp.int32).astype(jnp.int16)
            for h in range(halves):
                at = (h * cap + c) * part + (tail if h else 0)
                out_ref[p, at : at + part, :] = words[h * part : (h + 1) * part, :]
            exps.append(e * F32(2**bits) + block_ref[n].astype(F32))
            if first:
                col = acc[n, size : size + 8, :][:1, :]
                f = exponent_of(jnp.abs(col))
                scaled = col * jnp.exp2(WORD - f)
                high = to_words(scaled)
                cols += [f, high, to_words((scaled - high) * F32(2.0**WORD))]
        rows = exps + cols
        if tail > len(rows):
            rows.append(jnp.zeros((tail - len(rows), size), F32))
        at = cap * part
        out_ref[p, at : at + tail, :] = jnp.concatenate(rows, axis=0).astype(jnp.int32).astype(jnp.int16)
        return 0

    lax.fori_loop(0, peers, one, 0)


def push_kernel(first, cap, part, *refs):
    if first:
        src_ref, slot_ref, block_ref, good_ref, degree_ref, tiles_ref, out_ref, acc, scaled = refs
    else:
        src_ref, slot_ref, block_ref, inflow, good_ref, degree_ref, tiles_ref, out_ref, acc, scaled = refs
    step = pl.program_id(0)
    blocks, seeds, size = good_ref.shape
    per_step = tiles_ref.shape[0]

    @pl.when(step == 0)
    def _():
        acc[...] = jnp.zeros_like(acc)
        def one(b, _):
            degree = degree_ref[b].astype(F32)
            trust = good_ref[b]
            if not first:
                trust = F32(0.85) * inflow[b] + F32(0.15) * trust
            scaled[b, :seeds, :] = (trust / degree).astype(BF16)
            if first:
                scaled[b, seeds:, :] = jnp.ones((scaled.shape[1] - seeds, size), BF16)
            return 0

        lax.fori_loop(0, blocks, one, 0)

    def some(g, _):
        products = []
        for k in range(GROUP):
            n = step * per_step + g * GROUP + k
            products.append(
                jnp.dot(scaled[src_ref[n]], tiles_ref[g * GROUP + k], preferred_element_type=F32)
            )
        for k in range(GROUP):
            acc[slot_ref[step * per_step + g * GROUP + k]] += products[k]
        return 0

    lax.fori_loop(0, per_step // GROUP, some, 0)

    @pl.when(step == pl.num_programs(0) - 1)
    def _():
        pack(first, cap, part, blocks.bit_length() - 1, acc, block_ref, out_ref)


def shares(shield_ref, weight_ref, start_of, share_ref):
    def one(b, _):
        weight = weight_ref[pl.ds(b, 1), :]
        share_ref[b] = (shield_ref[b] * start_of(b) / weight).astype(BF16)
        return 0

    lax.fori_loop(0, share_ref.shape[0], one, 0)


def greet(devices):
    barrier = pltpu.get_barrier_semaphore()
    for device, there in devices:
        @pl.when(there)
        def _():
            pl.semaphore_signal(barrier, inc=1, device_id=device, device_id_type=MESH)
    pl.semaphore_wait(barrier, sum(jnp.where(there, 1, 0) for _, there in devices))


def fetch_kernel(rows, columns, cap, want_ref, share_ref, fetched_ref, *scratch):
    line = 2 * (columns - 1)
    held, (picked, line_send, line_recv, send, recv) = scratch[:line], scratch[line:]
    r, z = lax.axis_index("row"), lax.axis_index("col")
    others = [lax.rem(r + d, rows) for d in range(1, rows)]
    sides = (-1, 1)
    inside = {side: (z + side >= 0) & (z + side < columns) for side in sides}
    greet([((t, z), t >= 0) for t in others] + [((r, z + side), inside[side]) for side in sides])

    def place(side, d):
        return 2 * (d - 1) + (0 if side < 0 else 1)

    def pass_on(source, d, side):
        slot = place(-side, d)
        return pltpu.make_async_remote_copy(
            src_ref=source, dst_ref=held[slot],
            send_sem=line_send.at[slot], recv_sem=line_recv.at[slot],
            device_id=(r, z + side), device_id_type=MESH,
        )

    def serve(t, origin):
        return pltpu.make_async_remote_copy(
            src_ref=picked.at[t, pl.ds(origin * cap, cap)],
            dst_ref=fetched_ref.at[pl.ds((r * columns + origin) * cap, cap)],
            send_sem=send.at[t, origin], recv_sem=recv.at[r, origin],
            device_id=(t, z), device_id_type=MESH,
        )

    def spread(source, origin):
        before = None
        for t in others:
            for j in range(cap):
                picked[t, origin * cap + j] = source[want_ref[t, 0, (r * columns + origin) * cap + j]]
            if before is not None:
                serve(before, origin).start()
            before = t
        for j in range(cap):
            fetched_ref[(r * columns + origin) * cap + j] = source[want_ref[r, 0, (r * columns + origin) * cap + j]]
        serve(before, origin).start()

    for side in sides:
        @pl.when(inside[side])
        def _():
            pass_on(share_ref, 1, side).start()
    spread(share_ref, z)
    for d in range(1, columns):
        for side in sides:
            origin = z + side * d

            @pl.when((origin >= 0) & (origin < columns))
            def _():
                here = held[place(side, d)]
                pass_on(share_ref, d, -side).wait_recv()

                if d < columns - 1:
                    @pl.when(inside[-side])
                    def _():
                        pass_on(here, d + 1, -side).start()

                spread(here, origin)
    for origin in range(columns):
        for t in others:
            serve(t, origin).wait_send()
            pltpu.make_async_remote_copy(
                src_ref=picked.at[t, pl.ds(origin * cap, cap)],
                dst_ref=fetched_ref.at[pl.ds((t * columns + origin) * cap, cap)],
                send_sem=send.at[t, origin], recv_sem=recv.at[t, origin],
                device_id=(t, z), device_id_type=MESH,
            ).wait_recv()
    for d in range(columns - 1):
        for side in sides:
            origin = z - side * d

            @pl.when((origin >= 0) & (origin < columns) & inside[side])
            def _():
                pass_on(share_ref, d + 1, side).wait_send()


def order_of(z, columns):
    table = []
    for plane in range(columns):
        line = []
        for k in range(columns):
            if columns - 1 - k > plane:
                line.append(columns - 1 - k)
            if k < plane:
                line.append(k)
        table.append(line + [plane])
    picks = []
    for i in range(columns):
        pick = z * 0
        for plane in range(columns):
            pick = pick + jnp.where(z == plane, table[plane][i], 0)
        picks.append(pick)
    return picks


def reduce_kernel(first, rows, columns, cap, words_ref, *refs):
    if first:
        cores_ref, mine_ref, inflow_ref, weight_ref, spam_ref, want_ref, *refs = refs
    else:
        inflow_ref, *refs = refs
    landed, table, partial, exps, packed, inbox, own, send, recv, chain_send, chain_recv, *refs = refs
    r, z = lax.axis_index("row"), lax.axis_index("col")
    blocks, part, size = partial.shape
    seeds = inflow_ref.shape[1]
    halves = seeds // part
    bits = blocks.bit_length() - 1
    tail_at = cap * part
    spans = []
    for h in range(halves):
        start = spans[-1][0] + spans[-1][1] if spans else 0
        spans.append((start, cap * part + (landed.shape[2] - cap * seeds if h == 0 else 0)))
    data = blocks * part
    longs = [data + blocks * (4 if first and h == 0 else 1) for h in range(halves)]
    others = [lax.rem(r + d, rows) for d in range(1, rows)]
    targets = order_of(z, columns)
    block_iota = lax.broadcasted_iota(jnp.int32, (blocks, size), 0)
    greet(
        [((t, z), t >= 0) for t in others]
        + [((r, z - 1), z > 0), ((r, z + 1), z < columns - 1)]
    )

    def across(i, h, t, origin):
        at = pl.ds(*spans[h])
        return pltpu.make_async_remote_copy(
            src_ref=words_ref.at[t * columns + targets[i], at], dst_ref=landed.at[i, origin, at],
            send_sem=send.at[i, h, t], recv_sem=recv.at[i, h, origin],
            device_id=(t, z), device_id_type=MESH,
        )

    def mine(i):
        return pltpu.make_async_copy(
            words_ref.at[r * columns + targets[i]], landed.at[i, r], own.at[i]
        )

    def chain(i, h, side):
        at = pl.ds(0, longs[h])
        return pltpu.make_async_remote_copy(
            src_ref=packed.at[min(i, columns - 2), h, at], dst_ref=inbox.at[side, targets[i], h, at],
            send_sem=chain_send.at[min(i, columns - 2), h], recv_sem=chain_recv.at[side, targets[i], h],
            device_id=(r, z + 1 - 2 * side), device_id_type=MESH,
        )

    def to_int16(value):
        return value.astype(jnp.int32).astype(jnp.int16)

    def to_float(value):
        return value.astype(jnp.int32).astype(F32)

    if first:
        known_send, known_recv = refs

        def know(t, origin):
            return pltpu.make_async_remote_copy(
                src_ref=mine_ref, dst_ref=want_ref.at[origin],
                send_sem=known_send.at[t], recv_sem=known_recv.at[origin],
                device_id=(t, z), device_id_type=MESH,
            )

        for t in others:
            know(t, r).start()
        want_ref[r] = mine_ref[...]
    for i in range(columns):
        for h in range(halves):
            for t in others:
                across(i, h, t, r).start()
        mine(i).start()

    pieces = min(4, (columns - 1) * halves)
    for i in range(columns):
        mine(i).wait()
        side = jnp.where(targets[i] > z, 0, 1)
        joined = jnp.where(targets[i] > z, z > 0, z < columns - 1)
        cols = jnp.zeros((blocks, size), F32)
        for h in range(halves):
            for t in others:
                across(i, h, t, t).wait_recv()
            if h == 0:
                def weigh(q, cols):
                    tail = landed[i, q, tail_at : spans[0][1], :].astype(jnp.int32)
                    for c in range(cap):
                        word = tail[c : c + 1, :]
                        hit = block_iota == (word & (blocks - 1))
                        scale = jnp.exp2((word >> bits).astype(F32) - WORD)
                        table[q * cap + c] = jnp.where(
                            hit, jnp.broadcast_to(scale, (blocks, size)), F32(0)
                        )
                        if first:
                            f, high, low = (
                                tail[cap + 3 * c + k : cap + 3 * c + k + 1, :].astype(F32) for k in range(3)
                            )
                            col = (high + low * F32(2.0**-WORD)) * jnp.exp2(f - WORD)
                            cols = cols + jnp.where(hit, jnp.broadcast_to(col, (blocks, size)), F32(0))
                    return cols

                cols = lax.fori_loop(0, rows, weigh, cols)

            begin = spans[h][0]

            def strip(k, _):
                at = pl.multiple_of(k * 16, 16)

                def add(q, sums):
                    sums = list(sums)
                    for c in range(cap):
                        spot = pl.multiple_of(begin + c * part + at, 16)
                        value = to_float(landed[i, q, pl.ds(spot, 16), :])
                        for b in range(blocks):
                            sums[b] = sums[b] + value * table[q * cap + c, b : b + 1, :]
                    return tuple(sums)

                sums = lax.fori_loop(0, rows, add, (jnp.zeros((16, size), F32),) * blocks)
                for b in range(blocks):
                    partial[b, pl.ds(at, 16), :] = sums[b]
                return 0

            lax.fori_loop(0, part // 16, strip, 0)

            def join(way):
                chain(i, h, way).wait_recv()
                exps[...] = jnp.exp2(to_float(inbox[way, targets[i], h, data : data + blocks, :]) - WORD)

                def one(b, _):
                    got = to_float(inbox[way, targets[i], h, pl.ds(pl.multiple_of(b * part, part), part), :])
                    partial[b] += got * exps[pl.ds(b, 1), :]
                    return 0

                lax.fori_loop(0, blocks, one, 0)

            def join_cols(way):
                f, high, low = (
                    to_float(inbox[way, targets[i], h, data + (k + 1) * blocks : data + (k + 2) * blocks, :])
                    for k in range(3)
                )
                colsum[...] += (high + low * F32(2.0**-WORD)) * jnp.exp2(f - WORD)

            if first and h == 0:
                colsum = weight_ref
                colsum[...] = cols
            if i < columns - 1:
                @pl.when(joined)
                def _():
                    join(side)
                    if first and h == 0:
                        join_cols(side)

                def squeeze(b, _):
                    value = partial[b]
                    e = exponent_of(jnp.max(jnp.abs(value), axis=0, keepdims=True))
                    exps[pl.ds(b, 1), :] = e
                    packed[i, h, pl.ds(pl.multiple_of(b * part, part), part), :] = to_int16(
                        to_words(value * jnp.exp2(WORD - e))
                    )
                    return 0

                lax.fori_loop(0, blocks, squeeze, 0)
                packed[i, h, data : data + blocks, :] = to_int16(exps[...])
                if first and h == 0:
                    col = colsum[...]
                    f = exponent_of(jnp.abs(col))
                    scaled = col * jnp.exp2(WORD - f)
                    high = to_words(scaled)
                    for k, row in enumerate((f, high, to_words((scaled - high) * F32(2.0**WORD)))):
                        packed[i, h, data + (k + 1) * blocks : data + (k + 2) * blocks, :] = to_int16(row)
                chain(i, h, side).start()
            else:
                for way, there in ((0, z > 0), (1, z < columns - 1)):
                    @pl.when(there)
                    def _():
                        join(way)
                        if first and h == 0:
                            join_cols(way)

                def finish(b, _):
                    inflow_ref[b, h * part : (h + 1) * part, :] = partial[b]
                    return 0

                lax.fori_loop(0, blocks, finish, 0)
                if first and h == 0:
                    colsum[...] += F32(1)
            step = i * halves + h
            if first and step < pieces:
                count_seeds(columns, cores_ref, spam_ref, step, pieces)

    if first:
        for t in others:
            know(t, r).wait_send()
            know(t, t).wait_recv()
    for i in range(columns):
        for h in range(halves):
            for t in others:
                across(i, h, t, r).wait_send()
            if i < columns - 1:
                chain(i, h, jnp.where(targets[i] > z, 0, 1)).wait_send()


def trust_kernel(inflow, good_ref, spam_ref, weight_ref, trust_ref, shield_ref, share_ref):
    size = inflow.shape[2]

    def one(b, _):
        trust = F32(0.85) * inflow[b] + F32(0.15) * good_ref[b]
        trust_ref[pl.ds(pl.multiple_of(b * size, size), size), :] = jnp.transpose(trust)
        shield_ref[b] = F32(1) / (F32(1) + trust)
        return 0

    lax.fori_loop(0, inflow.shape[0], one, 0)
    shares(shield_ref, weight_ref, lambda b: spam_ref[b], share_ref)


def pull_kernel(last, *refs):
    if last:
        src_ref, slot_ref, fetched_ref, spam_ref, tiles_ref, out_ref, acc = refs
    else:
        (src_ref, slot_ref, fetched_ref, spam_ref, shield_ref, weight_ref, tiles_ref,
         out_ref, acc) = refs
    step = pl.program_id(0)
    per_step = tiles_ref.shape[0]
    size = acc.shape[2]

    @pl.when(step == 0)
    def _():
        acc[...] = jnp.zeros_like(acc)

    def some(g, _):
        products = []
        for k in range(GROUP):
            n = step * per_step + g * GROUP + k
            products.append(
                lax.dot_general(
                    fetched_ref[slot_ref[n]], tiles_ref[g * GROUP + k], (((1,), (1,)), ((), ())),
                    preferred_element_type=F32,
                )
            )
        for k in range(GROUP):
            acc[src_ref[step * per_step + g * GROUP + k]] += products[k]
        return 0

    lax.fori_loop(0, per_step // GROUP, some, 0)

    @pl.when(step == pl.num_programs(0) - 1)
    def _():
        def distrust(b):
            return F32(0.85) * acc[b] + F32(0.15) * spam_ref[b]

        if last:
            def one(b, _):
                out_ref[pl.ds(pl.multiple_of(b * size, size), size), :] = jnp.transpose(distrust(b))
                return 0

            lax.fori_loop(0, acc.shape[0], one, 0)
        else:
            shares(shield_ref, weight_ref, distrust, out_ref)


def start_kernel(columns, good_ref, spam_ref, count_ref, list_ref):
    list_ref[...] = jnp.transpose(spam_ref[...].astype(F32)).astype(jnp.int32)
    count_seeds(columns, good_ref, count_ref)


def body(columns, tiles, tile_src, tile_slot, slot_block, out_degree, good_seeds, spam_cores):
    tile_count, size, _ = tiles.shape
    hosts = out_degree.shape[0]
    blocks = hosts // size
    seeds = good_seeds.shape[0]
    slots = slot_block.shape[0]
    peers = lax.axis_size(AXES)
    cap = slots // peers
    tail = -(-4 * cap // 16) * 16
    steps = 8
    shape = jax.ShapeDtypeStruct
    vector = (blocks, seeds, size)
    degree = out_degree.reshape(blocks, 1, size)

    rows = peers // columns
    part = seeds // HALVES
    good, spam_list = pl.pallas_call(
        functools.partial(start_kernel, columns),
        out_shape=(shape(vector, F32), shape(spam_cores.shape, jnp.int32)),
        in_specs=[VM, VM],
        out_specs=(VM, VM),
    )(good_seeds, spam_cores.T)

    tile_spec = pl.BlockSpec((tile_count // steps, size, size), lambda i: (i, 0, 0))
    words = shape((peers, cap * size + tail, size), jnp.int16)
    outgoing = pl.pallas_call(
        functools.partial(push_kernel, True, cap, part),
        grid=(steps,),
        out_shape=words,
        in_specs=[SM, SM, SM, VM, VM, tile_spec],
        out_specs=VM,
        scratch_shapes=[
            pltpu.VMEM((slots, seeds + 16, size), F32),
            pltpu.VMEM((blocks, seeds + 16, size), BF16),
        ],
    )(tile_src, tile_slot, slot_block, good, degree, tiles)

    def reduce(first, words_in, *rest):
        long = blocks * part + blocks * (4 if first else 1)
        dma = pltpu.SemaphoreType.DMA
        outs = (
            shape(vector, F32), shape((blocks, size), F32), shape(vector, F32),
            shape((rows, 1, slots), jnp.int32),
        )
        return pl.pallas_call(
            functools.partial(reduce_kernel, first, rows, columns, cap),
            out_shape=outs if first else outs[:1],
            in_specs=[ANY, VM, VM] if first else [ANY],
            out_specs=(VM,) * 4 if first else (VM,),
            scratch_shapes=[
                pltpu.VMEM((columns, rows, cap * size + tail, size), jnp.int16),
                pltpu.VMEM((rows * cap, blocks, size), F32),
                pltpu.VMEM((blocks, part, size), F32),
                pltpu.VMEM((blocks, size), F32),
                pltpu.VMEM((columns - 1, HALVES, long, size), jnp.int16),
                pltpu.VMEM((2, columns, HALVES, long, size), jnp.int16),
                dma((columns,)),
                dma((columns, HALVES, rows)),
                dma((columns, HALVES, rows)),
                dma((columns - 1, HALVES)),
                dma((2, columns, HALVES)),
                *([dma((rows,)), dma((rows,))] if first else []),
            ],
            compiler_params=pltpu.CompilerParams(
                collective_id=1 if first else 2, has_side_effects=True
            ),
        )(words_in, *rest)

    inflow, weight, spam, want = reduce(True, outgoing, spam_list, slot_block.reshape(1, slots))
    outgoing = pl.pallas_call(
        functools.partial(push_kernel, False, cap, part),
        grid=(steps,),
        out_shape=words,
        in_specs=[SM, SM, SM, VM, VM, VM, tile_spec],
        out_specs=VM,
        scratch_shapes=[
            pltpu.VMEM((slots, seeds, size), F32),
            pltpu.VMEM(vector, BF16),
        ],
    )(tile_src, tile_slot, slot_block, inflow, good, degree, tiles)
    (inflow,) = reduce(False, outgoing)
    fetch = pl.pallas_call(
        functools.partial(fetch_kernel, rows, columns, cap),
        out_shape=shape((slots, seeds, size), BF16),
        in_specs=[SM, VM],
        out_specs=VM,
        scratch_shapes=[
            *[pltpu.VMEM(vector, BF16)] * (2 * columns - 2),
            pltpu.VMEM((rows, columns * cap, seeds, size), BF16),
            pltpu.SemaphoreType.DMA((2 * columns - 2,)),
            pltpu.SemaphoreType.DMA((2 * columns - 2,)),
            pltpu.SemaphoreType.DMA((rows, columns)),
            pltpu.SemaphoreType.DMA((rows, columns)),
        ],
        compiler_params=pltpu.CompilerParams(collective_id=0, has_side_effects=True),
    )
    trust, shield, share = pl.pallas_call(
        trust_kernel,
        out_shape=(shape((hosts, seeds), F32), shape(vector, F32), shape(vector, BF16)),
        in_specs=[VM, VM, VM, VM],
        out_specs=(VM, VM, VM),
    )(inflow, good, spam, weight)
    fetched = fetch(want, share)
    share = pl.pallas_call(
        functools.partial(pull_kernel, False),
        grid=(steps,),
        out_shape=shape(vector, BF16),
        in_specs=[SM, SM, VM, VM, VM, VM, tile_spec],
        out_specs=VM,
        scratch_shapes=[pltpu.VMEM(vector, F32)],
    )(tile_src, tile_slot, fetched, spam, shield, weight, tiles)
    fetched = fetch(want, share)
    distrust = pl.pallas_call(
        functools.partial(pull_kernel, True),
        grid=(steps,),
        out_shape=shape((hosts, seeds), F32),
        in_specs=[SM, SM, VM, VM, tile_spec],
        out_specs=VM,
        scratch_shapes=[pltpu.VMEM(vector, F32)],
    )(tile_src, tile_slot, fetched, spam, tiles)
    return trust, distrust


def solution(mesh):
    in_specs = (
        P(AXES, None, None),
        P(AXES),
        P(AXES),
        P(AXES),
        P(AXES),
        P(None, AXES),
        P(None, AXES),
    )
    out_specs = (P(AXES, None), P(AXES, None))
    return jax.shard_map(
        functools.partial(body, mesh.shape["col"]),
        mesh=mesh, in_specs=in_specs, out_specs=out_specs, check_vma=False,
    )
```

```python
import functools

import jax
import jax.numpy as jnp
from jax import lax
from jax.experimental import pallas as pl
from jax.experimental.pallas import tpu as pltpu
from jax.sharding import PartitionSpec as P

AXES = ("row", "col")
VM = pl.BlockSpec(memory_space=pltpu.VMEM)
SM = pl.BlockSpec(memory_space=pltpu.SMEM)
LIMIT = 28 << 20
ANY = pl.BlockSpec(memory_space=pl.ANY)
F32 = jnp.float32
BF16 = jnp.bfloat16
PLAIN = pltpu.CompilerParams(vmem_limit_bytes=LIMIT)
WORD = 15
GROUP = 16
HALVES = 2
MESH = pl.DeviceIdType.MESH


def count_seeds(columns, source, target, step=0, pieces=1):
    blocks, seeds, size = target.shape
    hosts = blocks * size
    base = (lax.axis_index("row") * columns + lax.axis_index("col")) * hosts
    count = source.shape[1]
    factor = F32(hosts / count)
    block_iota = lax.broadcasted_iota(jnp.int32, (blocks, count), 0) * size
    lane_iota = lax.broadcasted_iota(jnp.int32, (size, count), 0)

    def one(s, _):
        local = source[pl.ds(s, 1), :] - base
        shifted = local - block_iota
        inside = jnp.where((shifted >= 0) & (shifted < size), F32(1), F32(0)).astype(BF16)
        start = jnp.max(jnp.where(local >= block_iota, block_iota, 0), axis=0, keepdims=True)
        lane = jnp.where(lane_iota == local - start, F32(1), F32(0)).astype(BF16)
        counts = lax.dot_general(
            inside, lane, (((1,), (1,)), ((), ())), preferred_element_type=F32
        )
        for b in range(blocks):
            target[b, pl.ds(s, 1), :] = counts[b : b + 1, :] * factor
        return 0

    share = seeds // pieces
    lax.fori_loop(step * share, (step + 1) * share, one, 0, unroll=4)


def exponent_of(peak):
    return jnp.floor(jnp.log2(jnp.maximum(peak, F32(2.0**-100)))) + F32(1)


def to_words(value):
    return jnp.clip(jnp.floor(value + F32(0.5)), F32(-32767), F32(32767))


def pack(first, cap, part, bits, acc, block_ref, out_ref):
    peers = out_ref.shape[0]
    size = acc.shape[2]
    halves = size // part
    tail = out_ref.shape[1] - cap * size

    def one(p, _):
        exps, cols = [], []
        for c in range(cap):
            n = p * cap + c
            value = acc[n, :size, :]
            e = exponent_of(jnp.max(jnp.abs(value), axis=0, keepdims=True))
            words = to_words(value * jnp.exp2(WORD - e)).astype(jnp.int32).astype(jnp.int16)
            for h in range(halves):
                at = (h * cap + c) * part + (tail if h else 0)
                out_ref[p, at : at + part, :] = words[h * part : (h + 1) * part, :]
            exps.append(e * F32(2**bits) + block_ref[n].astype(F32))
            if first:
                col = acc[n, size : size + 8, :][:1, :]
                f = exponent_of(jnp.abs(col))
                scaled = col * jnp.exp2(WORD - f)
                high = to_words(scaled)
                cols += [f, high, to_words((scaled - high) * F32(2.0**WORD))]
        rows = exps + cols
        if tail > len(rows):
            rows.append(jnp.zeros((tail - len(rows), size), F32))
        at = cap * part
        out_ref[p, at : at + tail, :] = jnp.concatenate(rows, axis=0).astype(jnp.int32).astype(jnp.int16)
        return 0

    lax.fori_loop(0, peers, one, 0)


def push_kernel(first, cap, part, *refs):
    if first:
        src_ref, slot_ref, block_ref, good_ref, degree_ref, tiles_ref, out_ref, acc, scaled = refs
    else:
        src_ref, slot_ref, block_ref, inflow, good_ref, degree_ref, tiles_ref, out_ref, acc, scaled = refs
    step = pl.program_id(0)
    blocks, seeds, size = good_ref.shape
    per_step = tiles_ref.shape[0]

    @pl.when(step == 0)
    def _():
        acc[...] = jnp.zeros_like(acc)
        def one(b, _):
            degree = degree_ref[b].astype(F32)
            trust = good_ref[b]
            if not first:
                trust = F32(0.85) * inflow[b] + F32(0.15) * trust
            scaled[b, :seeds, :] = (trust / degree).astype(BF16)
            if first:
                scaled[b, seeds:, :] = jnp.ones((scaled.shape[1] - seeds, size), BF16)
            return 0

        lax.fori_loop(0, blocks, one, 0)

    def some(g, _):
        products = []
        for k in range(GROUP):
            n = step * per_step + g * GROUP + k
            products.append(
                jnp.dot(scaled[src_ref[n]], tiles_ref[g * GROUP + k], preferred_element_type=F32)
            )
        for k in range(GROUP):
            acc[slot_ref[step * per_step + g * GROUP + k]] += products[k]
        return 0

    lax.fori_loop(0, per_step // GROUP, some, 0)

    @pl.when(step == pl.num_programs(0) - 1)
    def _():
        pack(first, cap, part, blocks.bit_length() - 1, acc, block_ref, out_ref)


def shares(shield_ref, weight_ref, start_of, share_ref):
    def one(b, _):
        weight = weight_ref[pl.ds(b, 1), :]
        share_ref[b] = (shield_ref[b] * start_of(b) / weight).astype(BF16)
        return 0

    lax.fori_loop(0, share_ref.shape[0], one, 0)


def greet(devices):
    barrier = pltpu.get_barrier_semaphore()
    for device, there in devices:
        @pl.when(there)
        def _():
            pl.semaphore_signal(barrier, inc=1, device_id=device, device_id_type=MESH)
    pl.semaphore_wait(barrier, sum(jnp.where(there, 1, 0) for _, there in devices))


def fetch_kernel(rows, columns, cap, want_ref, share_ref, fetched_ref, *scratch):
    line = 2 * (columns - 1)
    held, (picked, line_send, line_recv, send, recv) = scratch[:line], scratch[line:]
    r, z = lax.axis_index("row"), lax.axis_index("col")
    others = [lax.rem(r + d, rows) for d in range(1, rows)]
    sides = (-1, 1)
    inside = {side: (z + side >= 0) & (z + side < columns) for side in sides}
    greet([((t, z), t >= 0) for t in others] + [((r, z + side), inside[side]) for side in sides])

    def place(side, d):
        return 2 * (d - 1) + (0 if side < 0 else 1)

    def pass_on(source, d, side):
        slot = place(-side, d)
        return pltpu.make_async_remote_copy(
            src_ref=source, dst_ref=held[slot],
            send_sem=line_send.at[slot], recv_sem=line_recv.at[slot],
            device_id=(r, z + side), device_id_type=MESH,
        )

    def serve(t, origin):
        return pltpu.make_async_remote_copy(
            src_ref=picked.at[t, pl.ds(origin * cap, cap)],
            dst_ref=fetched_ref.at[pl.ds((r * columns + origin) * cap, cap)],
            send_sem=send.at[t, origin], recv_sem=recv.at[r, origin],
            device_id=(t, z), device_id_type=MESH,
        )

    def spread(source, origin):
        before = None
        for t in others:
            for j in range(cap):
                picked[t, origin * cap + j] = source[want_ref[t, 0, (r * columns + origin) * cap + j]]
            if before is not None:
                serve(before, origin).start()
            before = t
        for j in range(cap):
            fetched_ref[(r * columns + origin) * cap + j] = source[want_ref[r, 0, (r * columns + origin) * cap + j]]
        serve(before, origin).start()

    for side in sides:
        @pl.when(inside[side])
        def _():
            pass_on(share_ref, 1, side).start()
    spread(share_ref, z)
    for d in range(1, columns):
        for side in sides:
            origin = z + side * d

            @pl.when((origin >= 0) & (origin < columns))
            def _():
                here = held[place(side, d)]
                pass_on(share_ref, d, -side).wait_recv()

                if d < columns - 1:
                    @pl.when(inside[-side])
                    def _():
                        pass_on(here, d + 1, -side).start()

                spread(here, origin)
    for origin in range(columns):
        for t in others:
            serve(t, origin).wait_send()
            pltpu.make_async_remote_copy(
                src_ref=picked.at[t, pl.ds(origin * cap, cap)],
                dst_ref=fetched_ref.at[pl.ds((t * columns + origin) * cap, cap)],
                send_sem=send.at[t, origin], recv_sem=recv.at[t, origin],
                device_id=(t, z), device_id_type=MESH,
            ).wait_recv()
    for d in range(columns - 1):
        for side in sides:
            origin = z - side * d

            @pl.when((origin >= 0) & (origin < columns) & inside[side])
            def _():
                pass_on(share_ref, d + 1, side).wait_send()


def order_of(z, columns):
    table = []
    for plane in range(columns):
        line = []
        for k in range(columns):
            if columns - 1 - k > plane:
                line.append(columns - 1 - k)
            if k < plane:
                line.append(k)
        table.append(line + [plane])
    picks = []
    for i in range(columns):
        pick = z * 0
        for plane in range(columns):
            pick = pick + jnp.where(z == plane, table[plane][i], 0)
        picks.append(pick)
    return picks


def reduce_kernel(first, rows, columns, cap, words_ref, *refs):
    if first:
        cores_ref, mine_ref, inflow_ref, weight_ref, spam_ref, want_ref, *refs = refs
    else:
        inflow_ref, *refs = refs
    landed, table, partial, exps, packed, inbox, own, send, recv, chain_send, chain_recv, *refs = refs
    r, z = lax.axis_index("row"), lax.axis_index("col")
    blocks, part, size = partial.shape
    seeds = inflow_ref.shape[1]
    halves = seeds // part
    bits = blocks.bit_length() - 1
    tail_at = cap * part
    spans = []
    for h in range(halves):
        start = spans[-1][0] + spans[-1][1] if spans else 0
        spans.append((start, cap * part + (landed.shape[2] - cap * seeds if h == 0 else 0)))
    data = blocks * part
    longs = [data + blocks * (4 if first and h == 0 else 1) for h in range(halves)]
    others = [lax.rem(r + d, rows) for d in range(1, rows)]
    targets = order_of(z, columns)
    block_iota = lax.broadcasted_iota(jnp.int32, (blocks, size), 0)
    greet(
        [((t, z), t >= 0) for t in others]
        + [((r, z - 1), z > 0), ((r, z + 1), z < columns - 1)]
    )

    def across(i, h, t, origin):
        at = pl.ds(*spans[h])
        return pltpu.make_async_remote_copy(
            src_ref=words_ref.at[t * columns + targets[i], at], dst_ref=landed.at[i, origin, at],
            send_sem=send.at[i, h, t], recv_sem=recv.at[i, h, origin],
            device_id=(t, z), device_id_type=MESH,
        )

    def mine(i):
        return pltpu.make_async_copy(
            words_ref.at[r * columns + targets[i]], landed.at[i, r], own.at[i]
        )

    def chain(i, h, side):
        at = pl.ds(0, longs[h])
        return pltpu.make_async_remote_copy(
            src_ref=packed.at[min(i, columns - 2), h, at], dst_ref=inbox.at[side, targets[i], h, at],
            send_sem=chain_send.at[min(i, columns - 2), h], recv_sem=chain_recv.at[side, targets[i], h],
            device_id=(r, z + 1 - 2 * side), device_id_type=MESH,
        )

    def to_int16(value):
        return value.astype(jnp.int32).astype(jnp.int16)

    def to_float(value):
        return value.astype(jnp.int32).astype(F32)

    if first:
        known_send, known_recv = refs

        def know(t, origin):
            return pltpu.make_async_remote_copy(
                src_ref=mine_ref, dst_ref=want_ref.at[origin],
                send_sem=known_send.at[t], recv_sem=known_recv.at[origin],
                device_id=(t, z), device_id_type=MESH,
            )

        for t in others:
            know(t, r).start()
        want_ref[r] = mine_ref[...]
    for i in range(columns):
        for h in range(halves):
            for t in others:
                across(i, h, t, r).start()
        mine(i).start()

    pieces = min(4, (columns - 1) * halves)
    for i in range(columns):
        mine(i).wait()
        side = jnp.where(targets[i] > z, 0, 1)
        joined = jnp.where(targets[i] > z, z > 0, z < columns - 1)
        cols = jnp.zeros((blocks, size), F32)
        for h in range(halves):
            for t in others:
                across(i, h, t, t).wait_recv()
            if h == 0:
                def weigh(q, cols):
                    tail = landed[i, q, tail_at : spans[0][1], :].astype(jnp.int32)
                    for c in range(cap):
                        word = tail[c : c + 1, :]
                        hit = block_iota == (word & (blocks - 1))
                        scale = jnp.exp2((word >> bits).astype(F32) - WORD)
                        table[q * cap + c] = jnp.where(
                            hit, jnp.broadcast_to(scale, (blocks, size)), F32(0)
                        )
                        if first:
                            f, high, low = (
                                tail[cap + 3 * c + k : cap + 3 * c + k + 1, :].astype(F32) for k in range(3)
                            )
                            col = (high + low * F32(2.0**-WORD)) * jnp.exp2(f - WORD)
                            cols = cols + jnp.where(hit, jnp.broadcast_to(col, (blocks, size)), F32(0))
                    return cols

                cols = lax.fori_loop(0, rows, weigh, cols)

            begin = spans[h][0]

            def strip(k, _):
                at = pl.multiple_of(k * 16, 16)

                def add(q, sums):
                    sums = list(sums)
                    for c in range(cap):
                        spot = pl.multiple_of(begin + c * part + at, 16)
                        value = to_float(landed[i, q, pl.ds(spot, 16), :])
                        for b in range(blocks):
                            sums[b] = sums[b] + value * table[q * cap + c, b : b + 1, :]
                    return tuple(sums)

                sums = lax.fori_loop(0, rows, add, (jnp.zeros((16, size), F32),) * blocks)
                for b in range(blocks):
                    partial[b, pl.ds(at, 16), :] = sums[b]
                return 0

            lax.fori_loop(0, part // 16, strip, 0)

            def join(way):
                chain(i, h, way).wait_recv()
                exps[...] = jnp.exp2(to_float(inbox[way, targets[i], h, data : data + blocks, :]) - WORD)

                def one(b, _):
                    got = to_float(inbox[way, targets[i], h, pl.ds(pl.multiple_of(b * part, part), part), :])
                    partial[b] += got * exps[pl.ds(b, 1), :]
                    return 0

                lax.fori_loop(0, blocks, one, 0)

            def join_cols(way):
                f, high, low = (
                    to_float(inbox[way, targets[i], h, data + (k + 1) * blocks : data + (k + 2) * blocks, :])
                    for k in range(3)
                )
                colsum[...] += (high + low * F32(2.0**-WORD)) * jnp.exp2(f - WORD)

            if first and h == 0:
                colsum = weight_ref
                colsum[...] = cols
            if i < columns - 1:
                @pl.when(joined)
                def _():
                    join(side)
                    if first and h == 0:
                        join_cols(side)

                def squeeze(b, _):
                    value = partial[b]
                    e = exponent_of(jnp.max(jnp.abs(value), axis=0, keepdims=True))
                    exps[pl.ds(b, 1), :] = e
                    packed[i, h, pl.ds(pl.multiple_of(b * part, part), part), :] = to_int16(
                        to_words(value * jnp.exp2(WORD - e))
                    )
                    return 0

                lax.fori_loop(0, blocks, squeeze, 0)
                packed[i, h, data : data + blocks, :] = to_int16(exps[...])
                if first and h == 0:
                    col = colsum[...]
                    f = exponent_of(jnp.abs(col))
                    scaled = col * jnp.exp2(WORD - f)
                    high = to_words(scaled)
                    for k, row in enumerate((f, high, to_words((scaled - high) * F32(2.0**WORD)))):
                        packed[i, h, data + (k + 1) * blocks : data + (k + 2) * blocks, :] = to_int16(row)
                chain(i, h, side).start()
            else:
                for way, there in ((0, z > 0), (1, z < columns - 1)):
                    @pl.when(there)
                    def _():
                        join(way)
                        if first and h == 0:
                            join_cols(way)

                def finish(b, _):
                    inflow_ref[b, h * part : (h + 1) * part, :] = partial[b]
                    return 0

                lax.fori_loop(0, blocks, finish, 0)
                if first and h == 0:
                    colsum[...] += F32(1)
            step = i * halves + h
            if first and step < pieces:
                count_seeds(columns, cores_ref, spam_ref, step, pieces)

    if first:
        for t in others:
            know(t, r).wait_send()
            know(t, t).wait_recv()
    for i in range(columns):
        for h in range(halves):
            for t in others:
                across(i, h, t, r).wait_send()
            if i < columns - 1:
                chain(i, h, jnp.where(targets[i] > z, 0, 1)).wait_send()


def trust_kernel(inflow, good_ref, spam_ref, weight_ref, trust_ref, shield_ref, share_ref):
    size = inflow.shape[2]

    def one(b, _):
        trust = F32(0.85) * inflow[b] + F32(0.15) * good_ref[b]
        trust_ref[pl.ds(pl.multiple_of(b * size, size), size), :] = jnp.transpose(trust)
        shield_ref[b] = F32(1) / (F32(1) + trust)
        return 0

    lax.fori_loop(0, inflow.shape[0], one, 0)
    shares(shield_ref, weight_ref, lambda b: spam_ref[b], share_ref)


def pull_kernel(last, *refs):
    if last:
        src_ref, slot_ref, fetched_ref, spam_ref, tiles_ref, out_ref, acc = refs
    else:
        (src_ref, slot_ref, fetched_ref, spam_ref, shield_ref, weight_ref, tiles_ref,
         out_ref, acc) = refs
    step = pl.program_id(0)
    per_step = tiles_ref.shape[0]
    size = acc.shape[2]

    @pl.when(step == 0)
    def _():
        acc[...] = jnp.zeros_like(acc)

    def some(g, _):
        products = []
        for k in range(GROUP):
            n = step * per_step + g * GROUP + k
            products.append(
                lax.dot_general(
                    fetched_ref[slot_ref[n]], tiles_ref[g * GROUP + k], (((1,), (1,)), ((), ())),
                    preferred_element_type=F32,
                )
            )
        for k in range(GROUP):
            acc[src_ref[step * per_step + g * GROUP + k]] += products[k]
        return 0

    lax.fori_loop(0, per_step // GROUP, some, 0)

    @pl.when(step == pl.num_programs(0) - 1)
    def _():
        def distrust(b):
            return F32(0.85) * acc[b] + F32(0.15) * spam_ref[b]

        if last:
            def one(b, _):
                out_ref[pl.ds(pl.multiple_of(b * size, size), size), :] = jnp.transpose(distrust(b))
                return 0

            lax.fori_loop(0, acc.shape[0], one, 0)
        else:
            shares(shield_ref, weight_ref, distrust, out_ref)


def start_kernel(columns, good_ref, spam_ref, count_ref, list_ref):
    list_ref[...] = jnp.transpose(spam_ref[...].astype(F32)).astype(jnp.int32)
    count_seeds(columns, good_ref, count_ref)


def body(columns, tiles, tile_src, tile_slot, slot_block, out_degree, good_seeds, spam_cores):
    tile_count, size, _ = tiles.shape
    hosts = out_degree.shape[0]
    blocks = hosts // size
    seeds = good_seeds.shape[0]
    slots = slot_block.shape[0]
    peers = lax.axis_size(AXES)
    cap = slots // peers
    tail = -(-4 * cap // 16) * 16
    steps = 8
    shape = jax.ShapeDtypeStruct
    vector = (blocks, seeds, size)
    degree = out_degree.reshape(blocks, 1, size)

    rows = peers // columns
    part = seeds // HALVES
    good, spam_list = pl.pallas_call(
        functools.partial(start_kernel, columns),
        out_shape=(shape(vector, F32), shape(spam_cores.shape, jnp.int32)),
        in_specs=[VM, VM],
        out_specs=(VM, VM),
        compiler_params=PLAIN,
    )(good_seeds, spam_cores.T)

    tile_spec = pl.BlockSpec((tile_count // steps, size, size), lambda i: (i, 0, 0))
    words = shape((peers, cap * size + tail, size), jnp.int16)
    outgoing = pl.pallas_call(
        functools.partial(push_kernel, True, cap, part),
        grid=(steps,),
        out_shape=words,
        in_specs=[SM, SM, SM, VM, VM, tile_spec],
        out_specs=VM,
        scratch_shapes=[
            pltpu.VMEM((slots, seeds + 16, size), F32),
            pltpu.VMEM((blocks, seeds + 16, size), BF16),
        ],
        compiler_params=PLAIN,
    )(tile_src, tile_slot, slot_block, good, degree, tiles)

    def reduce(first, words_in, *rest):
        long = blocks * part + blocks * (4 if first else 1)
        dma = pltpu.SemaphoreType.DMA
        outs = (
            shape(vector, F32), shape((blocks, size), F32), shape(vector, F32),
            shape((rows, 1, slots), jnp.int32),
        )
        return pl.pallas_call(
            functools.partial(reduce_kernel, first, rows, columns, cap),
            out_shape=outs if first else outs[:1],
            in_specs=[ANY, VM, VM] if first else [ANY],
            out_specs=(VM,) * 4 if first else (VM,),
            scratch_shapes=[
                pltpu.VMEM((columns, rows, cap * size + tail, size), jnp.int16),
                pltpu.VMEM((rows * cap, blocks, size), F32),
                pltpu.VMEM((blocks, part, size), F32),
                pltpu.VMEM((blocks, size), F32),
                pltpu.VMEM((columns - 1, HALVES, long, size), jnp.int16),
                pltpu.VMEM((2, columns, HALVES, long, size), jnp.int16),
                dma((columns,)),
                dma((columns, HALVES, rows)),
                dma((columns, HALVES, rows)),
                dma((columns - 1, HALVES)),
                dma((2, columns, HALVES)),
                *([dma((rows,)), dma((rows,))] if first else []),
            ],
            compiler_params=pltpu.CompilerParams(
                collective_id=1 if first else 2, has_side_effects=True,
                vmem_limit_bytes=LIMIT,
            ),
        )(words_in, *rest)

    inflow, weight, spam, want = reduce(True, outgoing, spam_list, slot_block.reshape(1, slots))
    outgoing = pl.pallas_call(
        functools.partial(push_kernel, False, cap, part),
        grid=(steps,),
        out_shape=words,
        in_specs=[SM, SM, SM, VM, VM, VM, tile_spec],
        out_specs=VM,
        scratch_shapes=[
            pltpu.VMEM((slots, seeds, size), F32),
            pltpu.VMEM(vector, BF16),
        ],
        compiler_params=PLAIN,
    )(tile_src, tile_slot, slot_block, inflow, good, degree, tiles)
    (inflow,) = reduce(False, outgoing)
    fetch = pl.pallas_call(
        functools.partial(fetch_kernel, rows, columns, cap),
        out_shape=shape((slots, seeds, size), BF16),
        in_specs=[SM, VM],
        out_specs=VM,
        scratch_shapes=[
            *[pltpu.VMEM(vector, BF16)] * (2 * columns - 2),
            pltpu.VMEM((rows, columns * cap, seeds, size), BF16),
            pltpu.SemaphoreType.DMA((2 * columns - 2,)),
            pltpu.SemaphoreType.DMA((2 * columns - 2,)),
            pltpu.SemaphoreType.DMA((rows, columns)),
            pltpu.SemaphoreType.DMA((rows, columns)),
        ],
        compiler_params=pltpu.CompilerParams(collective_id=0, has_side_effects=True, vmem_limit_bytes=LIMIT),
    )
    trust, shield, share = pl.pallas_call(
        trust_kernel,
        out_shape=(shape((hosts, seeds), F32), shape(vector, F32), shape(vector, BF16)),
        in_specs=[VM, VM, VM, VM],
        out_specs=(VM, VM, VM),
        compiler_params=PLAIN,
    )(inflow, good, spam, weight)
    fetched = fetch(want, share)
    share = pl.pallas_call(
        functools.partial(pull_kernel, False),
        grid=(steps,),
        out_shape=shape(vector, BF16),
        in_specs=[SM, SM, VM, VM, VM, VM, tile_spec],
        out_specs=VM,
        scratch_shapes=[pltpu.VMEM(vector, F32)],
        compiler_params=PLAIN,
    )(tile_src, tile_slot, fetched, spam, shield, weight, tiles)
    fetched = fetch(want, share)
    distrust = pl.pallas_call(
        functools.partial(pull_kernel, True),
        grid=(steps,),
        out_shape=shape((hosts, seeds), F32),
        in_specs=[SM, SM, VM, VM, tile_spec],
        out_specs=VM,
        scratch_shapes=[pltpu.VMEM(vector, F32)],
        compiler_params=PLAIN,
    )(tile_src, tile_slot, fetched, spam, tiles)
    return trust, distrust


def solution(mesh):
    in_specs = (
        P(AXES, None, None),
        P(AXES),
        P(AXES),
        P(AXES),
        P(AXES),
        P(None, AXES),
        P(None, AXES),
    )
    out_specs = (P(AXES, None), P(AXES, None))
    return jax.shard_map(
        functools.partial(body, mesh.shape["col"]),
        mesh=mesh, in_specs=in_specs, out_specs=out_specs, check_vma=False,
    )
```

```python
import functools

import jax
import jax.numpy as jnp
from jax import lax
from jax.experimental import pallas as pl
from jax.experimental.pallas import tpu as pltpu
from jax.sharding import PartitionSpec as P

AXES = ("row", "col")
VM = pl.BlockSpec(memory_space=pltpu.VMEM)
SM = pl.BlockSpec(memory_space=pltpu.SMEM)
LIMIT = 28 << 20
ANY = pl.BlockSpec(memory_space=pl.ANY)
F32 = jnp.float32
BF16 = jnp.bfloat16
PLAIN = pltpu.CompilerParams(vmem_limit_bytes=LIMIT)
WORD = 15
GROUP = 16
HALVES = 4
MESH = pl.DeviceIdType.MESH


def count_seeds(columns, source, tally, step=0, pieces=1):
    seeds, blocks, size = tally.shape
    hosts = blocks * size
    base = (lax.axis_index("row") * columns + lax.axis_index("col")) * hosts
    count = source.shape[1]
    block_iota = lax.broadcasted_iota(jnp.int32, (blocks, count), 0) * size
    lane_iota = lax.broadcasted_iota(jnp.int32, (size, count), 0)

    def one(s, _):
        local = source[pl.ds(s, 1), :] - base
        shifted = local - block_iota
        inside = jnp.where((shifted >= 0) & (shifted < size), F32(1), F32(0)).astype(BF16)
        start = jnp.max(jnp.where(local >= block_iota, block_iota, 0), axis=0, keepdims=True)
        lane = jnp.where(lane_iota == local - start, F32(1), F32(0)).astype(BF16)
        tally[s] = lax.dot_general(
            inside, lane, (((1,), (1,)), ((), ())), preferred_element_type=F32
        )
        return 0

    share = seeds // pieces
    lax.fori_loop(step * share, (step + 1) * share, one, 0, unroll=16)


def spread_seeds(count, tally, target):
    blocks, _, size = target.shape
    factor = F32(blocks * size / count)
    for b in range(blocks):
        target[b] = tally[:, b, :] * factor


def exponent_of(peak):
    return jnp.floor(jnp.log2(jnp.maximum(peak, F32(2.0**-100)))) + F32(1)


def to_words(value):
    return jnp.clip(jnp.floor(value + F32(0.5)), F32(-32767), F32(32767))


def pack(first, cap, part, bits, acc, block_ref, out_ref):
    peers = out_ref.shape[0]
    size = acc.shape[2]
    halves = size // part
    tail = out_ref.shape[1] - cap * size

    def one(p, _):
        exps, cols = [], []
        for c in range(cap):
            n = p * cap + c
            value = acc[n, :size, :]
            e = exponent_of(jnp.max(jnp.abs(value), axis=0, keepdims=True))
            words = to_words(value * jnp.exp2(WORD - e)).astype(jnp.int32).astype(jnp.int16)
            for h in range(halves):
                at = (h * cap + c) * part + (tail if h else 0)
                out_ref[p, at : at + part, :] = words[h * part : (h + 1) * part, :]
            exps.append(e * F32(2**bits) + block_ref[n].astype(F32))
            if first:
                col = acc[n, size : size + 8, :][:1, :]
                f = exponent_of(jnp.abs(col))
                scaled = col * jnp.exp2(WORD - f)
                high = to_words(scaled)
                cols += [f, high, to_words((scaled - high) * F32(2.0**WORD))]
        rows = exps + cols
        if tail > len(rows):
            rows.append(jnp.zeros((tail - len(rows), size), F32))
        at = cap * part
        out_ref[p, at : at + tail, :] = jnp.concatenate(rows, axis=0).astype(jnp.int32).astype(jnp.int16)
        return 0

    lax.fori_loop(0, peers, one, 0)


def push_kernel(first, cap, part, *refs):
    if first:
        src_ref, slot_ref, block_ref, good_ref, degree_ref, tiles_ref, out_ref, acc, scaled = refs
    else:
        src_ref, slot_ref, block_ref, inflow, good_ref, degree_ref, tiles_ref, out_ref, acc, scaled = refs
    step = pl.program_id(0)
    blocks, seeds, size = good_ref.shape
    per_step = tiles_ref.shape[0]

    @pl.when(step == 0)
    def _():
        acc[...] = jnp.zeros_like(acc)
        def one(b, _):
            degree = degree_ref[b].astype(F32)
            trust = good_ref[b]
            if not first:
                trust = F32(0.85) * inflow[b] + F32(0.15) * trust
            scaled[b, :seeds, :] = (trust / degree).astype(BF16)
            if first:
                scaled[b, seeds:, :] = jnp.ones((scaled.shape[1] - seeds, size), BF16)
            return 0

        lax.fori_loop(0, blocks, one, 0)

    def some(g, _):
        products = []
        for k in range(GROUP):
            n = step * per_step + g * GROUP + k
            products.append(
                jnp.dot(scaled[src_ref[n]], tiles_ref[g * GROUP + k], preferred_element_type=F32)
            )
        for k in range(GROUP):
            acc[slot_ref[step * per_step + g * GROUP + k]] += products[k]
        return 0

    lax.fori_loop(0, per_step // GROUP, some, 0)

    @pl.when(step == pl.num_programs(0) - 1)
    def _():
        pack(first, cap, part, blocks.bit_length() - 1, acc, block_ref, out_ref)


def shares(shield_ref, weight_ref, start_of, share_ref):
    def one(b, _):
        weight = weight_ref[pl.ds(b, 1), :]
        share_ref[b] = (shield_ref[b] * start_of(b) / weight).astype(BF16)
        return 0

    lax.fori_loop(0, share_ref.shape[0], one, 0)


def greet(devices):
    barrier = pltpu.get_barrier_semaphore()
    for device, there in devices:
        @pl.when(there)
        def _():
            pl.semaphore_signal(barrier, inc=1, device_id=device, device_id_type=MESH)
    pl.semaphore_wait(barrier, sum(jnp.where(there, 1, 0) for _, there in devices))


def fetch_kernel(rows, columns, cap, want_ref, share_ref, fetched_ref, *scratch):
    line = 2 * (columns - 1)
    held, (picked, line_send, line_recv, send, recv) = scratch[:line], scratch[line:]
    r, z = lax.axis_index("row"), lax.axis_index("col")
    others = [lax.rem(r + d, rows) for d in range(1, rows)]
    sides = (-1, 1)
    inside = {side: (z + side >= 0) & (z + side < columns) for side in sides}
    greet([((t, z), t >= 0) for t in others] + [((r, z + side), inside[side]) for side in sides])

    def place(side, d):
        return 2 * (d - 1) + (0 if side < 0 else 1)

    def pass_on(source, d, side):
        slot = place(-side, d)
        return pltpu.make_async_remote_copy(
            src_ref=source, dst_ref=held[slot],
            send_sem=line_send.at[slot], recv_sem=line_recv.at[slot],
            device_id=(r, z + side), device_id_type=MESH,
        )

    def serve(t, origin):
        return pltpu.make_async_remote_copy(
            src_ref=picked.at[t, pl.ds(origin * cap, cap)],
            dst_ref=fetched_ref.at[pl.ds((r * columns + origin) * cap, cap)],
            send_sem=send.at[t, origin], recv_sem=recv.at[r, origin],
            device_id=(t, z), device_id_type=MESH,
        )

    def spread(source, origin):
        before = None
        for t in others:
            for j in range(cap):
                picked[t, origin * cap + j] = source[want_ref[t, 0, (r * columns + origin) * cap + j]]
            if before is not None:
                serve(before, origin).start()
            before = t
        for j in range(cap):
            fetched_ref[(r * columns + origin) * cap + j] = source[want_ref[r, 0, (r * columns + origin) * cap + j]]
        serve(before, origin).start()

    for side in sides:
        @pl.when(inside[side])
        def _():
            pass_on(share_ref, 1, side).start()
    spread(share_ref, z)
    for d in range(1, columns):
        for side in sides:
            origin = z + side * d

            @pl.when((origin >= 0) & (origin < columns))
            def _():
                here = held[place(side, d)]
                pass_on(share_ref, d, -side).wait_recv()

                if d < columns - 1:
                    @pl.when(inside[-side])
                    def _():
                        pass_on(here, d + 1, -side).start()

                spread(here, origin)
    for origin in range(columns):
        for t in others:
            serve(t, origin).wait_send()
            pltpu.make_async_remote_copy(
                src_ref=picked.at[t, pl.ds(origin * cap, cap)],
                dst_ref=fetched_ref.at[pl.ds((t * columns + origin) * cap, cap)],
                send_sem=send.at[t, origin], recv_sem=recv.at[t, origin],
                device_id=(t, z), device_id_type=MESH,
            ).wait_recv()
    for d in range(columns - 1):
        for side in sides:
            origin = z - side * d

            @pl.when((origin >= 0) & (origin < columns) & inside[side])
            def _():
                pass_on(share_ref, d + 1, side).wait_send()


def order_of(z, columns):
    table = []
    for plane in range(columns):
        line = []
        for k in range(columns):
            if columns - 1 - k > plane:
                line.append(columns - 1 - k)
            if k < plane:
                line.append(k)
        table.append(line + [plane])
    picks = []
    for i in range(columns):
        pick = z * 0
        for plane in range(columns):
            pick = pick + jnp.where(z == plane, table[plane][i], 0)
        picks.append(pick)
    return picks


def reduce_kernel(first, rows, columns, cap, words_ref, *refs):
    if first:
        cores_ref, mine_ref, inflow_ref, weight_ref, spam_ref, want_ref, *refs = refs
    else:
        inflow_ref, *refs = refs
    landed, table, partial, exps, packed, inbox, own, send, recv, chain_send, chain_recv, *refs = refs
    r, z = lax.axis_index("row"), lax.axis_index("col")
    blocks, part, size = partial.shape
    seeds = inflow_ref.shape[1]
    halves = seeds // part
    bits = blocks.bit_length() - 1
    tail_at = cap * part
    spans = []
    for h in range(halves):
        start = spans[-1][0] + spans[-1][1] if spans else 0
        spans.append((start, cap * part + (landed.shape[2] - cap * seeds if h == 0 else 0)))
    data = blocks * part
    longs = [data + blocks * (4 if first and h == 0 else 1) for h in range(halves)]
    others = [lax.rem(r + d, rows) for d in range(1, rows)]
    targets = order_of(z, columns)
    block_iota = lax.broadcasted_iota(jnp.int32, (blocks, size), 0)
    greet(
        [((t, z), t >= 0) for t in others]
        + [((r, z - 1), z > 0), ((r, z + 1), z < columns - 1)]
    )

    def across(i, h, t, origin):
        at = pl.ds(*spans[h])
        return pltpu.make_async_remote_copy(
            src_ref=words_ref.at[t * columns + targets[i], at], dst_ref=landed.at[i, origin, at],
            send_sem=send.at[i, h, t], recv_sem=recv.at[i, h, origin],
            device_id=(t, z), device_id_type=MESH,
        )

    def mine(i):
        return pltpu.make_async_copy(
            words_ref.at[r * columns + targets[i]], landed.at[i, r], own.at[i]
        )

    def chain(i, h, side):
        at = pl.ds(0, longs[h])
        return pltpu.make_async_remote_copy(
            src_ref=packed.at[min(i, columns - 2), h, at], dst_ref=inbox.at[side, targets[i], h, at],
            send_sem=chain_send.at[min(i, columns - 2), h], recv_sem=chain_recv.at[side, targets[i], h],
            device_id=(r, z + 1 - 2 * side), device_id_type=MESH,
        )

    def to_int16(value):
        return value.astype(jnp.int32).astype(jnp.int16)

    def to_float(value):
        return value.astype(jnp.int32).astype(F32)

    if first:
        known_send, known_recv, tally = refs

        def know(t, origin):
            return pltpu.make_async_remote_copy(
                src_ref=mine_ref, dst_ref=want_ref.at[origin],
                send_sem=known_send.at[t], recv_sem=known_recv.at[origin],
                device_id=(t, z), device_id_type=MESH,
            )

        for t in others:
            know(t, r).start()
        want_ref[r] = mine_ref[...]
    for i in range(columns):
        for h in range(halves):
            for t in others:
                across(i, h, t, r).start()
        mine(i).start()

    pieces = min(4, (columns - 1) * halves)
    for i in range(columns):
        mine(i).wait()
        side = jnp.where(targets[i] > z, 0, 1)
        joined = jnp.where(targets[i] > z, z > 0, z < columns - 1)
        cols = jnp.zeros((blocks, size), F32)
        for h in range(halves):
            for t in others:
                across(i, h, t, t).wait_recv()
            if h == 0:
                def weigh(q, cols):
                    tail = landed[i, q, tail_at : spans[0][1], :].astype(jnp.int32)
                    for c in range(cap):
                        word = tail[c : c + 1, :]
                        hit = block_iota == (word & (blocks - 1))
                        scale = jnp.exp2((word >> bits).astype(F32) - WORD)
                        table[q * cap + c] = jnp.where(
                            hit, jnp.broadcast_to(scale, (blocks, size)), F32(0)
                        )
                        if first:
                            f, high, low = (
                                tail[cap + 3 * c + k : cap + 3 * c + k + 1, :].astype(F32) for k in range(3)
                            )
                            col = (high + low * F32(2.0**-WORD)) * jnp.exp2(f - WORD)
                            cols = cols + jnp.where(hit, jnp.broadcast_to(col, (blocks, size)), F32(0))
                    return cols

                cols = lax.fori_loop(0, rows, weigh, cols)

            begin = spans[h][0]

            def strip(k, _):
                at = pl.multiple_of(k * 16, 16)

                def add(q, sums):
                    sums = list(sums)
                    for c in range(cap):
                        spot = pl.multiple_of(begin + c * part + at, 16)
                        value = to_float(landed[i, q, pl.ds(spot, 16), :])
                        for b in range(blocks):
                            sums[b] = sums[b] + value * table[q * cap + c, b : b + 1, :]
                    return tuple(sums)

                sums = lax.fori_loop(0, rows, add, (jnp.zeros((16, size), F32),) * blocks)
                for b in range(blocks):
                    partial[b, pl.ds(at, 16), :] = sums[b]
                return 0

            lax.fori_loop(0, part // 16, strip, 0)

            def join(way):
                chain(i, h, way).wait_recv()
                exps[...] = jnp.exp2(to_float(inbox[way, targets[i], h, data : data + blocks, :]) - WORD)

                def one(b, _):
                    got = to_float(inbox[way, targets[i], h, pl.ds(pl.multiple_of(b * part, part), part), :])
                    partial[b] += got * exps[pl.ds(b, 1), :]
                    return 0

                lax.fori_loop(0, blocks, one, 0)

            def join_cols(way):
                f, high, low = (
                    to_float(inbox[way, targets[i], h, data + (k + 1) * blocks : data + (k + 2) * blocks, :])
                    for k in range(3)
                )
                colsum[...] += (high + low * F32(2.0**-WORD)) * jnp.exp2(f - WORD)

            if first and h == 0:
                colsum = weight_ref
                colsum[...] = cols
            if i < columns - 1:
                @pl.when(joined)
                def _():
                    join(side)
                    if first and h == 0:
                        join_cols(side)

                def squeeze(b, _):
                    value = partial[b]
                    e = exponent_of(jnp.max(jnp.abs(value), axis=0, keepdims=True))
                    exps[pl.ds(b, 1), :] = e
                    packed[i, h, pl.ds(pl.multiple_of(b * part, part), part), :] = to_int16(
                        to_words(value * jnp.exp2(WORD - e))
                    )
                    return 0

                lax.fori_loop(0, blocks, squeeze, 0)
                packed[i, h, data : data + blocks, :] = to_int16(exps[...])
                if first and h == 0:
                    col = colsum[...]
                    f = exponent_of(jnp.abs(col))
                    scaled = col * jnp.exp2(WORD - f)
                    high = to_words(scaled)
                    for k, row in enumerate((f, high, to_words((scaled - high) * F32(2.0**WORD)))):
                        packed[i, h, data + (k + 1) * blocks : data + (k + 2) * blocks, :] = to_int16(row)
                chain(i, h, side).start()
            else:
                for way, there in ((0, z > 0), (1, z < columns - 1)):
                    @pl.when(there)
                    def _():
                        join(way)
                        if first and h == 0:
                            join_cols(way)

                def finish(b, _):
                    inflow_ref[b, h * part : (h + 1) * part, :] = partial[b]
                    return 0

                lax.fori_loop(0, blocks, finish, 0)
                if first and h == 0:
                    colsum[...] += F32(1)
            step = i * halves + h
            if first and step < pieces:
                count_seeds(columns, cores_ref, tally, step, pieces)
            if first and step == pieces:
                spread_seeds(cores_ref.shape[1], tally, spam_ref)

    if first:
        for t in others:
            know(t, r).wait_send()
            know(t, t).wait_recv()
    for i in range(columns):
        for h in range(halves):
            for t in others:
                across(i, h, t, r).wait_send()
            if i < columns - 1:
                chain(i, h, jnp.where(targets[i] > z, 0, 1)).wait_send()


def trust_kernel(inflow, good_ref, spam_ref, weight_ref, trust_ref, shield_ref, share_ref):
    size = inflow.shape[2]

    def one(b, _):
        trust = F32(0.85) * inflow[b] + F32(0.15) * good_ref[b]
        trust_ref[pl.ds(pl.multiple_of(b * size, size), size), :] = jnp.transpose(trust)
        shield_ref[b] = F32(1) / (F32(1) + trust)
        return 0

    lax.fori_loop(0, inflow.shape[0], one, 0)
    shares(shield_ref, weight_ref, lambda b: spam_ref[b], share_ref)


def pull_kernel(last, *refs):
    if last:
        src_ref, slot_ref, fetched_ref, spam_ref, tiles_ref, out_ref, acc = refs
    else:
        (src_ref, slot_ref, fetched_ref, spam_ref, shield_ref, weight_ref, tiles_ref,
         out_ref, acc) = refs
    step = pl.program_id(0)
    per_step = tiles_ref.shape[0]
    size = acc.shape[2]

    @pl.when(step == 0)
    def _():
        acc[...] = jnp.zeros_like(acc)

    def some(g, _):
        products = []
        for k in range(GROUP):
            n = step * per_step + g * GROUP + k
            products.append(
                lax.dot_general(
                    fetched_ref[slot_ref[n]], tiles_ref[g * GROUP + k], (((1,), (1,)), ((), ())),
                    preferred_element_type=F32,
                )
            )
        for k in range(GROUP):
            acc[src_ref[step * per_step + g * GROUP + k]] += products[k]
        return 0

    lax.fori_loop(0, per_step // GROUP, some, 0)

    @pl.when(step == pl.num_programs(0) - 1)
    def _():
        def distrust(b):
            return F32(0.85) * acc[b] + F32(0.15) * spam_ref[b]

        if last:
            def one(b, _):
                out_ref[pl.ds(pl.multiple_of(b * size, size), size), :] = jnp.transpose(distrust(b))
                return 0

            lax.fori_loop(0, acc.shape[0], one, 0)
        else:
            shares(shield_ref, weight_ref, distrust, out_ref)


def start_kernel(columns, good_ref, spam_ref, count_ref, list_ref, tally):
    list_ref[...] = jnp.transpose(spam_ref[...].astype(F32)).astype(jnp.int32)
    count_seeds(columns, good_ref, tally)
    spread_seeds(good_ref.shape[1], tally, count_ref)


def body(columns, tiles, tile_src, tile_slot, slot_block, out_degree, good_seeds, spam_cores):
    tile_count, size, _ = tiles.shape
    here = lambda x: pltpu.with_memory_space_constraint(x, pltpu.HBM)
    hosts = out_degree.shape[0]
    blocks = hosts // size
    seeds = good_seeds.shape[0]
    slots = slot_block.shape[0]
    peers = lax.axis_size(AXES)
    cap = slots // peers
    tail = -(-4 * cap // 16) * 16
    steps = 8
    shape = jax.ShapeDtypeStruct
    vector = (blocks, seeds, size)
    degree = out_degree.reshape(blocks, 1, size)

    rows = peers // columns
    part = seeds // HALVES
    good, spam_list = pl.pallas_call(
        functools.partial(start_kernel, columns),
        out_shape=(shape(vector, F32), shape(spam_cores.shape, jnp.int32)),
        in_specs=[VM, VM],
        out_specs=(VM, VM),
        scratch_shapes=[pltpu.VMEM((seeds, blocks, size), F32)],
        compiler_params=PLAIN,
        cost_estimate=pl.CostEstimate(
            flops=2 * seeds * good_seeds.size * (blocks + size), transcendentals=0,
            bytes_accessed=24 << 20,
        ),
    )(here(good_seeds), here(spam_cores.T))

    tile_spec = pl.BlockSpec((tile_count // steps, size, size), lambda i: (i, 0, 0))
    words = shape((peers, cap * size + tail, size), jnp.int16)
    outgoing = pl.pallas_call(
        functools.partial(push_kernel, True, cap, part),
        grid=(steps,),
        out_shape=words,
        in_specs=[SM, SM, SM, VM, VM, tile_spec],
        out_specs=VM,
        scratch_shapes=[
            pltpu.VMEM((slots, seeds + 16, size), F32),
            pltpu.VMEM((blocks, seeds + 16, size), BF16),
        ],
        compiler_params=PLAIN,
    )(here(tile_src), here(tile_slot), here(slot_block), good, here(degree), here(tiles))

    def reduce(first, words_in, *rest):
        long = blocks * part + blocks * (4 if first else 1)
        dma = pltpu.SemaphoreType.DMA
        outs = (
            shape(vector, F32), shape((blocks, size), F32), shape(vector, F32),
            shape((rows, 1, slots), jnp.int32),
        )
        return pl.pallas_call(
            functools.partial(reduce_kernel, first, rows, columns, cap),
            out_shape=outs if first else outs[:1],
            in_specs=[ANY, VM, VM] if first else [ANY],
            out_specs=(VM,) * 4 if first else (VM,),
            scratch_shapes=[
                pltpu.VMEM((columns, rows, cap * size + tail, size), jnp.int16),
                pltpu.VMEM((rows * cap, blocks, size), F32),
                pltpu.VMEM((blocks, part, size), F32),
                pltpu.VMEM((blocks, size), F32),
                pltpu.VMEM((columns - 1, HALVES, long, size), jnp.int16),
                pltpu.VMEM((2, columns, HALVES, long, size), jnp.int16),
                dma((columns,)),
                dma((columns, HALVES, rows)),
                dma((columns, HALVES, rows)),
                dma((columns - 1, HALVES)),
                dma((2, columns, HALVES)),
                *([dma((rows,)), dma((rows,)), pltpu.VMEM((seeds, blocks, size), F32)] if first else []),
            ],
            compiler_params=pltpu.CompilerParams(
                collective_id=1 if first else 2, has_side_effects=True,
                vmem_limit_bytes=LIMIT,
            ),
        )(words_in, *rest)

    inflow, weight, spam, want = reduce(True, outgoing, spam_list, slot_block.reshape(1, slots))
    outgoing = pl.pallas_call(
        functools.partial(push_kernel, False, cap, part),
        grid=(steps,),
        out_shape=words,
        in_specs=[SM, SM, SM, VM, VM, VM, tile_spec],
        out_specs=VM,
        scratch_shapes=[
            pltpu.VMEM((slots, seeds, size), F32),
            pltpu.VMEM(vector, BF16),
        ],
        compiler_params=PLAIN,
    )(tile_src, tile_slot, slot_block, inflow, good, degree, tiles)
    (inflow,) = reduce(False, outgoing)
    fetch = pl.pallas_call(
        functools.partial(fetch_kernel, rows, columns, cap),
        out_shape=shape((slots, seeds, size), BF16),
        in_specs=[SM, VM],
        out_specs=VM,
        scratch_shapes=[
            *[pltpu.VMEM(vector, BF16)] * (2 * columns - 2),
            pltpu.VMEM((rows, columns * cap, seeds, size), BF16),
            pltpu.SemaphoreType.DMA((2 * columns - 2,)),
            pltpu.SemaphoreType.DMA((2 * columns - 2,)),
            pltpu.SemaphoreType.DMA((rows, columns)),
            pltpu.SemaphoreType.DMA((rows, columns)),
        ],
        compiler_params=pltpu.CompilerParams(collective_id=0, has_side_effects=True, vmem_limit_bytes=LIMIT),
    )
    trust, shield, share = pl.pallas_call(
        trust_kernel,
        out_shape=(shape((hosts, seeds), F32), shape(vector, F32), shape(vector, BF16)),
        in_specs=[VM, VM, VM, VM],
        out_specs=(VM, VM, VM),
        compiler_params=PLAIN,
    )(inflow, good, spam, weight)
    fetched = fetch(want, share)
    share = pl.pallas_call(
        functools.partial(pull_kernel, False),
        grid=(steps,),
        out_shape=shape(vector, BF16),
        in_specs=[SM, SM, VM, VM, VM, VM, tile_spec],
        out_specs=VM,
        scratch_shapes=[pltpu.VMEM(vector, F32)],
        compiler_params=PLAIN,
    )(tile_src, tile_slot, fetched, spam, shield, weight, tiles)
    fetched = fetch(want, share)
    distrust = pl.pallas_call(
        functools.partial(pull_kernel, True),
        grid=(steps,),
        out_shape=shape((hosts, seeds), F32),
        in_specs=[SM, SM, VM, VM, tile_spec],
        out_specs=VM,
        scratch_shapes=[pltpu.VMEM(vector, F32)],
        compiler_params=PLAIN,
    )(tile_src, tile_slot, fetched, spam, tiles)
    return trust, distrust


def solution(mesh):
    in_specs = (
        P(AXES, None, None),
        P(AXES),
        P(AXES),
        P(AXES),
        P(AXES),
        P(None, AXES),
        P(None, AXES),
    )
    out_specs = (P(AXES, None), P(AXES, None))
    return jax.shard_map(
        functools.partial(body, mesh.shape["col"]),
        mesh=mesh, in_specs=in_specs, out_specs=out_specs, check_vma=False,
    )
```

```python
import functools

import jax
import jax.numpy as jnp
from jax import lax
from jax.experimental import pallas as pl
from jax.experimental.pallas import tpu as pltpu
from jax.sharding import PartitionSpec as P

AXES = ("row", "col")
VM = pl.BlockSpec(memory_space=pltpu.VMEM)
SM = pl.BlockSpec(memory_space=pltpu.SMEM)
LIMIT = 28 << 20
ANY = pl.BlockSpec(memory_space=pl.ANY)
F32 = jnp.float32
BF16 = jnp.bfloat16
PLAIN = pltpu.CompilerParams(vmem_limit_bytes=LIMIT)
WORD = 15
GROUP = 16
HALVES = 4
LAYERS = 5
MESH = pl.DeviceIdType.MESH


def count_seeds(columns, source, tally, step=0, pieces=1):
    seeds, blocks, size = tally.shape
    hosts = blocks * size
    base = (lax.axis_index("row") * columns + lax.axis_index("col")) * hosts
    count = source.shape[1]
    block_iota = lax.broadcasted_iota(jnp.int32, (blocks, count), 0) * size
    lane_iota = lax.broadcasted_iota(jnp.int32, (size, count), 0)

    def one(s, _):
        local = source[pl.ds(s, 1), :] - base
        shifted = local - block_iota
        inside = jnp.where((shifted >= 0) & (shifted < size), F32(1), F32(0)).astype(BF16)
        start = jnp.max(jnp.where(local >= block_iota, block_iota, 0), axis=0, keepdims=True)
        lane = jnp.where(lane_iota == local - start, F32(1), F32(0)).astype(BF16)
        tally[s] = lax.dot_general(
            inside, lane, (((1,), (1,)), ((), ())), preferred_element_type=F32
        )
        return 0

    share = seeds // pieces
    lax.fori_loop(step * share, (step + 1) * share, one, 0, unroll=16)


def spread_seeds(count, tally, target):
    blocks, _, size = target.shape
    factor = F32(blocks * size / count)
    for b in range(blocks):
        target[b] = tally[:, b, :] * factor


def exponent_of(peak):
    return jnp.floor(jnp.log2(jnp.maximum(peak, F32(2.0**-100)))) + F32(1)


def to_words(value):
    return jnp.clip(jnp.floor(value + F32(0.5)), F32(-32767), F32(32767))


def pack(first, cap, part, bits, acc, block_ref, out_ref):
    peers = out_ref.shape[0]
    size = acc.shape[2]
    halves = size // part
    tail = out_ref.shape[1] - cap * size

    def one(p, _):
        exps, cols = [], []
        for c in range(cap):
            n = p * cap + c
            value = acc[n, :size, :]
            e = exponent_of(jnp.max(jnp.abs(value), axis=0, keepdims=True))
            words = to_words(value * jnp.exp2(WORD - e)).astype(jnp.int32).astype(jnp.int16)
            for h in range(halves):
                at = (h * cap + c) * part + (tail if h else 0)
                out_ref[p, at : at + part, :] = words[h * part : (h + 1) * part, :]
            exps.append(e * F32(2**bits) + block_ref[n].astype(F32))
            if first:
                col = acc[n, size : size + 8, :][:1, :]
                f = exponent_of(jnp.abs(col))
                scaled = col * jnp.exp2(WORD - f)
                high = to_words(scaled)
                cols += [f, high, to_words((scaled - high) * F32(2.0**WORD))]
        rows = exps + cols
        if tail > len(rows):
            rows.append(jnp.zeros((tail - len(rows), size), F32))
        at = cap * part
        out_ref[p, at : at + tail, :] = jnp.concatenate(rows, axis=0).astype(jnp.int32).astype(jnp.int16)
        return 0

    lax.fori_loop(0, peers, one, 0)


def push_kernel(first, cap, part, *refs):
    if first:
        src_ref, slot_ref, block_ref, good_ref, degree_ref, tiles_ref, out_ref, acc, scaled = refs
    else:
        src_ref, slot_ref, block_ref, inflow, good_ref, degree_ref, tiles_ref, out_ref, acc, scaled = refs
    step = pl.program_id(0)
    blocks, seeds, size = good_ref.shape
    per_step = tiles_ref.shape[0]

    @pl.when(step == 0)
    def _():
        acc[...] = jnp.zeros_like(acc)
        def one(b, _):
            degree = degree_ref[b].astype(F32)
            trust = good_ref[b]
            if not first:
                trust = F32(0.85) * inflow[b] + F32(0.15) * trust
            scaled[b, :seeds, :] = (trust / degree).astype(BF16)
            if first:
                scaled[b, seeds:, :] = jnp.ones((scaled.shape[1] - seeds, size), BF16)
            return 0

        lax.fori_loop(0, blocks, one, 0)

    def some(g, _):
        products = []
        for k in range(GROUP):
            n = step * per_step + g * GROUP + k
            products.append(
                jnp.dot(scaled[src_ref[n]], tiles_ref[g * GROUP + k], preferred_element_type=F32)
            )
        for k in range(GROUP):
            acc[slot_ref[step * per_step + g * GROUP + k]] += products[k]
        return 0

    lax.fori_loop(0, per_step // GROUP, some, 0)

    @pl.when(step == pl.num_programs(0) - 1)
    def _():
        pack(first, cap, part, blocks.bit_length() - 1, acc, block_ref, out_ref)


def shares(shield_ref, weight_ref, start_of, share_ref):
    def one(b, _):
        weight = weight_ref[pl.ds(b, 1), :]
        share_ref[b] = (shield_ref[b] * start_of(b) / weight).astype(BF16)
        return 0

    lax.fori_loop(0, share_ref.shape[0], one, 0)


def greet(devices):
    barrier = pltpu.get_barrier_semaphore()
    for device, there in devices:
        @pl.when(there)
        def _():
            pl.semaphore_signal(barrier, inc=1, device_id=device, device_id_type=MESH)
    pl.semaphore_wait(barrier, sum(jnp.where(there, 1, 0) for _, there in devices))


def fetch_kernel(rows, columns, cap, want_ref, share_ref, fetched_ref, *scratch):
    line = 2 * (columns - 1)
    held, (picked, line_send, line_recv, send, recv) = scratch[:line], scratch[line:]
    r, z = lax.axis_index("row"), lax.axis_index("col")
    others = [lax.rem(r + d, rows) for d in range(1, rows)]
    sides = (-1, 1)
    inside = {side: (z + side >= 0) & (z + side < columns) for side in sides}
    greet([((t, z), t >= 0) for t in others] + [((r, z + side), inside[side]) for side in sides])

    def place(side, d):
        return 2 * (d - 1) + (0 if side < 0 else 1)

    def pass_on(source, d, side):
        slot = place(-side, d)
        return pltpu.make_async_remote_copy(
            src_ref=source, dst_ref=held[slot],
            send_sem=line_send.at[slot], recv_sem=line_recv.at[slot],
            device_id=(r, z + side), device_id_type=MESH,
        )

    def serve(t, origin):
        return pltpu.make_async_remote_copy(
            src_ref=picked.at[t, pl.ds(origin * cap, cap)],
            dst_ref=fetched_ref.at[pl.ds((r * columns + origin) * cap, cap)],
            send_sem=send.at[t, origin], recv_sem=recv.at[r, origin],
            device_id=(t, z), device_id_type=MESH,
        )

    def spread(source, origin):
        before = None
        for t in others:
            for j in range(cap):
                picked[t, origin * cap + j] = source[want_ref[t, 0, (r * columns + origin) * cap + j]]
            if before is not None:
                serve(before, origin).start()
            before = t
        for j in range(cap):
            fetched_ref[(r * columns + origin) * cap + j] = source[want_ref[r, 0, (r * columns + origin) * cap + j]]
        serve(before, origin).start()

    for side in sides:
        @pl.when(inside[side])
        def _():
            pass_on(share_ref, 1, side).start()
    spread(share_ref, z)
    for d in range(1, columns):
        for side in sides:
            origin = z + side * d

            @pl.when((origin >= 0) & (origin < columns))
            def _():
                here = held[place(side, d)]
                pass_on(share_ref, d, -side).wait_recv()

                if d < columns - 1:
                    @pl.when(inside[-side])
                    def _():
                        pass_on(here, d + 1, -side).start()

                spread(here, origin)
    for origin in range(columns):
        for t in others:
            serve(t, origin).wait_send()
            pltpu.make_async_remote_copy(
                src_ref=picked.at[t, pl.ds(origin * cap, cap)],
                dst_ref=fetched_ref.at[pl.ds((t * columns + origin) * cap, cap)],
                send_sem=send.at[t, origin], recv_sem=recv.at[t, origin],
                device_id=(t, z), device_id_type=MESH,
            ).wait_recv()
    for d in range(columns - 1):
        for side in sides:
            origin = z - side * d

            @pl.when((origin >= 0) & (origin < columns) & inside[side])
            def _():
                pass_on(share_ref, d + 1, side).wait_send()


def take(table, index):
    return jnp.take_along_axis(table, index, axis=1, mode="promise_in_bounds")


def bound_of(code):
    return LAYERS + 4 * code


def find_ranks(groups, blocks, keys):
    lines, size = keys.shape
    count = size // groups
    least = lax.broadcasted_iota(jnp.int32, (lines, size), 1) * blocks
    spots = [jnp.full((lines, size), count * g, jnp.int32) for g in range(groups)]
    step = count // 2
    while True:
        probes = [take(keys, spot + (max(step, 1) - 1)) for spot in spots]
        spots = [spot + jnp.where(probe < least, max(step, 1), 0) for spot, probe in zip(spots, probes)]
        if step == 0:
            return spots
        step //= 2


def ends_of(g, groups, spots):
    lines, size = spots.shape
    lane = lax.broadcasted_iota(jnp.int32, (lines, size), 1)
    after = pltpu.roll(spots, size - 1, 1)
    return jnp.where(lane == size - 1, (size // groups) * (g + 1), after)


def sort_hosts(columns, blocks, raw):
    count, seeds = raw.shape
    groups = seeds // count
    lines = seeds // groups
    base = (lax.axis_index("row") * columns + lax.axis_index("col")) * (blocks * seeds)
    local = (raw - base).astype(F32)
    stacked = jnp.concatenate(
        [local] + [pltpu.roll(local, seeds - g * lines, 1) for g in range(1, groups)], axis=0
    )
    hosts = jnp.transpose(stacked)[:lines, :].astype(jnp.int32)
    keys = ((hosts & (seeds - 1)) * blocks + hosts // seeds).astype(F32)
    lane = lax.broadcasted_iota(jnp.int32, keys.shape, 1)
    k = 2
    while k <= count:
        j = k // 2
        while j:
            other = take(keys, lane ^ j)
            rising = ((lane & k) == 0) | (k == count)
            lower = ((lane & j) == 0) == rising
            keys = jnp.where(lower, jnp.minimum(keys, other), jnp.maximum(keys, other))
            j //= 2
        k *= 2
    keys = keys.astype(jnp.int32)
    spots = find_ranks(groups, blocks, keys)
    most = functools.reduce(
        jnp.maximum, [ends_of(g, groups, spot) - spot for g, spot in enumerate(spots)]
    ).astype(F32)
    most = jnp.max(jnp.max(most, axis=1, keepdims=True), axis=0, keepdims=True).astype(jnp.int32)
    code = jnp.maximum(most - LAYERS + 3, 0) >> 2
    return (keys + code * (blocks * seeds)).astype(jnp.int16)


class Spread:
    def __init__(self, rows, columns, own, out, sems):
        self.rows, self.columns, self.own, self.out = rows, columns, own, out
        self.line_send, self.line_recv, self.plane_send, self.plane_recv, self.pair_send, self.pair_recv = sems
        r, z = lax.axis_index("row"), lax.axis_index("col")
        self.r, self.z = r, z
        self.twin = r + 1 - 2 * lax.rem(r, 2)
        self.mates = [lax.rem(r + d, rows) for d in range(2, rows, 2)]
        self.others = [self.twin] + [lax.rem(self.twin + d, rows) for d in range(2, rows, 2)]
        self.inside = {side: (z + side >= 0) & (z + side < columns) for side in (-1, 1)}

    def send(self, source, row, origin, sends, recvs, to):
        return pltpu.make_async_remote_copy(
            src_ref=source, dst_ref=self.out.at[row * self.columns + origin],
            send_sem=sends, recv_sem=recvs, device_id=to, device_id_type=MESH,
        )

    def place(self, row, origin):
        return self.out.at[row * self.columns + origin]

    def line(self, source, origin, side):
        way = 0 if side < 0 else 1
        return self.send(
            source, self.r, origin, self.line_send.at[way, origin], self.line_recv.at[origin],
            (self.r, self.z + side),
        )

    def plane(self, source, t, row, origin):
        return self.send(
            source, row, origin, self.plane_send.at[t, origin], self.plane_recv.at[row, origin],
            (t, self.z),
        )

    def pair(self, source, row, origin):
        return self.send(
            source, row, origin, self.pair_send.at[row, origin], self.pair_recv.at[row, origin],
            (self.twin, self.z),
        )

    def across(self, source, origin):
        for t in self.mates:
            self.plane(source, t, self.r, origin).start()
        self.pair(source, self.r, origin).start()

    def begin(self):
        for side in (-1, 1):
            @pl.when(self.inside[side])
            def _():
                self.line(self.own, self.z, side).start()
        self.across(self.own, self.z)
        self.out[self.r * self.columns + self.z] = self.own[...]

    def each(self, d):
        for side in (-1, 1):
            origin = self.z + side * d
            yield side, origin, (origin >= 0) & (origin < self.columns)

    def hop(self, d):
        for side, origin, there in self.each(d):
            @pl.when(there)
            def _():
                here = self.place(self.r, origin)
                self.line(here, origin, side).wait_recv()

                @pl.when(self.inside[-side])
                def _():
                    self.line(here, origin, -side).start()

                self.across(here, origin)

    def collect(self):
        for t in self.mates:
            for origin in range(self.columns):
                here = self.place(t, origin)
                self.plane(here, t, t, origin).wait_recv()
                self.pair(here, t, origin).start()

    def finish(self):
        for t in self.others:
            for origin in range(self.columns):
                self.pair(self.place(t, origin), t, origin).wait_recv()
        for side in (-1, 1):
            @pl.when(self.inside[side])
            def _():
                self.line(self.own, self.z, side).wait_send()
        for d in range(1, self.columns):
            for side, origin, there in self.each(d):
                @pl.when(there & self.inside[-side])
                def _():
                    self.line(self.own, origin, -side).wait_send()
        for origin in range(self.columns):
            for t in self.mates:
                self.plane(self.own, t, self.r, origin).wait_send()
                self.pair(self.own, t, origin).wait_send()
            self.pair(self.own, self.r, origin).wait_send()


def value_kernel(rows, columns, groups, blocks, own_ref, lists_ref, vals_ref, rank_ref, *sems):
    spread = Spread(rows, columns, own_ref, vals_ref, sems)
    peers, lines, size = lists_ref.shape
    greet(
        [((t, spread.z), t >= 0) for t in spread.mates + [spread.twin]]
        + [((spread.r, spread.z + side), spread.inside[side]) for side in (-1, 1)]
    )

    def find(q, _):
        keys = lists_ref[q].astype(jnp.int32) & (blocks * size - 1)
        for g, spots in enumerate(find_ranks(groups, blocks, keys)):
            rank_ref[q, g * lines : (g + 1) * lines, :] = spots
        return 0

    share = peers // (columns + 1)
    spread.begin()
    for d in range(1, columns):
        lax.fori_loop((d - 1) * share, d * share, find, 0, unroll=2)
        spread.hop(d)
    lax.fori_loop((columns - 1) * share, columns * share, find, 0, unroll=2)
    spread.collect()
    lax.fori_loop(columns * share, peers, find, 0, unroll=2)
    spread.finish()


def expand(cap, block_ref, lists_ref, vals_ref, rank_ref, blocks, bounds, fetched):
    peers, lines, size = lists_ref.shape
    groups = fetched.shape[1] // lines
    tall = 16

    def paint(q, low, high):
        tags = [
            F32(1) + (block_ref[q * cap + c] + 1).astype(F32) * F32(2.0**-14) for c in range(cap)
        ]

        def some(i, _):
            at = pl.multiple_of(i * tall, tall)
            block = lists_ref[q, pl.ds(at, tall), :].astype(jnp.int32) & (blocks - 1)
            value = vals_ref[q, pl.ds(at, tall), :].astype(F32)
            marked = value * (F32(1) + (block + 1).astype(F32) * F32(2.0**-14))
            for g in range(groups):
                row = pl.multiple_of(g * lines + at, tall)
                spots = rank_ref[q, pl.ds(row, tall), :]
                ends = ends_of(g, groups, spots)

                def layer(j, outs):
                    spot = spots + j
                    live = spot < ends
                    got = jnp.where(live, take(marked, jnp.minimum(spot, size - 1)), F32(0))
                    plain = got.astype(BF16).astype(F32)
                    return tuple(
                        jnp.where(live & (plain * tag == got), plain, out) for tag, out in zip(tags, outs)
                    )

                if high is None:
                    outs = (jnp.zeros((tall, size), F32),) * cap
                    for j in range(low):
                        outs = layer(j, outs)
                else:
                    outs = tuple(
                        fetched[q * cap + c, pl.ds(row, tall), :].astype(F32) for c in range(cap)
                    )
                    outs = lax.fori_loop(low, high, layer, outs)
                for c in range(cap):
                    fetched[q * cap + c, pl.ds(row, tall), :] = outs[c].astype(BF16)
            return 0

        lax.fori_loop(0, lines // tall, some, 0, unroll=2 if high is None else 1)

    def one(q, _):
        paint(q, LAYERS, None)
        code = bounds[q, 0]

        @pl.when(code > 0)
        def _():
            paint(q, LAYERS, bound_of(code))

        return 0

    lax.fori_loop(0, peers, one, 0)


def order_of(z, columns):
    table = []
    for plane in range(columns):
        line = []
        for k in range(columns):
            if columns - 1 - k > plane:
                line.append(columns - 1 - k)
            if k < plane:
                line.append(k)
        table.append(line + [plane])
    picks = []
    for i in range(columns):
        pick = z * 0
        for plane in range(columns):
            pick = pick + jnp.where(z == plane, table[plane][i], 0)
        picks.append(pick)
    return picks


def reduce_kernel(first, rows, columns, cap, words_ref, *refs):
    if first:
        cores_ref, mine_ref, keys_ref, inflow_ref, weight_ref, spam_ref, want_ref, lists_ref, *refs = refs
    else:
        inflow_ref, *refs = refs
    landed, table, partial, exps, packed, inbox, own, send, recv, chain_send, chain_recv, *refs = refs
    r, z = lax.axis_index("row"), lax.axis_index("col")
    blocks, part, size = partial.shape
    seeds = inflow_ref.shape[1]
    halves = seeds // part
    bits = blocks.bit_length() - 1
    tail_at = cap * part
    spans = []
    for h in range(halves):
        start = spans[-1][0] + spans[-1][1] if spans else 0
        spans.append((start, cap * part + (landed.shape[2] - cap * seeds if h == 0 else 0)))
    data = blocks * part
    longs = [data + blocks * (4 if first and h == 0 else 1) for h in range(halves)]
    others = [lax.rem(r + d, rows) for d in range(1, rows)]
    targets = order_of(z, columns)
    block_iota = lax.broadcasted_iota(jnp.int32, (blocks, size), 0)
    greet(
        [((t, z), t >= 0) for t in others]
        + [((r, z - 1), z > 0), ((r, z + 1), z < columns - 1)]
    )

    def across(i, h, t, origin):
        at = pl.ds(*spans[h])
        return pltpu.make_async_remote_copy(
            src_ref=words_ref.at[t * columns + targets[i], at], dst_ref=landed.at[i, origin, at],
            send_sem=send.at[i, h, t], recv_sem=recv.at[i, h, origin],
            device_id=(t, z), device_id_type=MESH,
        )

    def mine(i):
        return pltpu.make_async_copy(
            words_ref.at[r * columns + targets[i]], landed.at[i, r], own.at[i]
        )

    def chain(i, h, side):
        at = pl.ds(0, longs[h])
        return pltpu.make_async_remote_copy(
            src_ref=packed.at[min(i, columns - 2), h, at], dst_ref=inbox.at[side, targets[i], h, at],
            send_sem=chain_send.at[min(i, columns - 2), h], recv_sem=chain_recv.at[side, targets[i], h],
            device_id=(r, z + 1 - 2 * side), device_id_type=MESH,
        )

    def to_int16(value):
        return value.astype(jnp.int32).astype(jnp.int16)

    def to_float(value):
        return value.astype(jnp.int32).astype(F32)

    if first:
        known_send, known_recv, tally, *sems = refs
        spread = Spread(rows, columns, keys_ref, lists_ref, sems)

        def know(t, origin):
            return pltpu.make_async_remote_copy(
                src_ref=mine_ref, dst_ref=want_ref.at[origin],
                send_sem=known_send.at[t], recv_sem=known_recv.at[origin],
                device_id=(t, z), device_id_type=MESH,
            )

        for t in others:
            know(t, r).start()
        want_ref[r] = mine_ref[...]
        spread.begin()
    for i in range(columns):
        for h in range(halves):
            for t in others:
                across(i, h, t, r).start()
        mine(i).start()

    pieces = min(4, (columns - 1) * halves)
    for i in range(columns):
        mine(i).wait()
        side = jnp.where(targets[i] > z, 0, 1)
        joined = jnp.where(targets[i] > z, z > 0, z < columns - 1)
        cols = jnp.zeros((blocks, size), F32)
        for h in range(halves):
            for t in others:
                across(i, h, t, t).wait_recv()
            if h == 0:
                def weigh(q, cols):
                    tail = landed[i, q, tail_at : spans[0][1], :].astype(jnp.int32)
                    for c in range(cap):
                        word = tail[c : c + 1, :]
                        hit = block_iota == (word & (blocks - 1))
                        scale = jnp.exp2((word >> bits).astype(F32) - WORD)
                        table[q * cap + c] = jnp.where(
                            hit, jnp.broadcast_to(scale, (blocks, size)), F32(0)
                        )
                        if first:
                            f, high, low = (
                                tail[cap + 3 * c + k : cap + 3 * c + k + 1, :].astype(F32) for k in range(3)
                            )
                            col = (high + low * F32(2.0**-WORD)) * jnp.exp2(f - WORD)
                            cols = cols + jnp.where(hit, jnp.broadcast_to(col, (blocks, size)), F32(0))
                    return cols

                cols = lax.fori_loop(0, rows, weigh, cols)

            begin = spans[h][0]

            def strip(k, _):
                at = pl.multiple_of(k * 16, 16)

                def add(q, sums):
                    sums = list(sums)
                    for c in range(cap):
                        spot = pl.multiple_of(begin + c * part + at, 16)
                        value = to_float(landed[i, q, pl.ds(spot, 16), :])
                        for b in range(blocks):
                            sums[b] = sums[b] + value * table[q * cap + c, b : b + 1, :]
                    return tuple(sums)

                sums = lax.fori_loop(0, rows, add, (jnp.zeros((16, size), F32),) * blocks)
                for b in range(blocks):
                    partial[b, pl.ds(at, 16), :] = sums[b]
                return 0

            lax.fori_loop(0, part // 16, strip, 0)

            def join(way):
                chain(i, h, way).wait_recv()
                exps[...] = jnp.exp2(to_float(inbox[way, targets[i], h, data : data + blocks, :]) - WORD)

                def one(b, _):
                    got = to_float(inbox[way, targets[i], h, pl.ds(pl.multiple_of(b * part, part), part), :])
                    partial[b] += got * exps[pl.ds(b, 1), :]
                    return 0

                lax.fori_loop(0, blocks, one, 0)

            def join_cols(way):
                f, high, low = (
                    to_float(inbox[way, targets[i], h, data + (k + 1) * blocks : data + (k + 2) * blocks, :])
                    for k in range(3)
                )
                colsum[...] += (high + low * F32(2.0**-WORD)) * jnp.exp2(f - WORD)

            if first and h == 0:
                colsum = weight_ref
                colsum[...] = cols
            if i < columns - 1:
                @pl.when(joined)
                def _():
                    join(side)
                    if first and h == 0:
                        join_cols(side)

                def squeeze(b, _):
                    value = partial[b]
                    e = exponent_of(jnp.max(jnp.abs(value), axis=0, keepdims=True))
                    exps[pl.ds(b, 1), :] = e
                    packed[i, h, pl.ds(pl.multiple_of(b * part, part), part), :] = to_int16(
                        to_words(value * jnp.exp2(WORD - e))
                    )
                    return 0

                lax.fori_loop(0, blocks, squeeze, 0)
                packed[i, h, data : data + blocks, :] = to_int16(exps[...])
                if first and h == 0:
                    col = colsum[...]
                    f = exponent_of(jnp.abs(col))
                    scaled = col * jnp.exp2(WORD - f)
                    high = to_words(scaled)
                    for k, row in enumerate((f, high, to_words((scaled - high) * F32(2.0**WORD)))):
                        packed[i, h, data + (k + 1) * blocks : data + (k + 2) * blocks, :] = to_int16(row)
                chain(i, h, side).start()
            else:
                for way, there in ((0, z > 0), (1, z < columns - 1)):
                    @pl.when(there)
                    def _():
                        join(way)
                        if first and h == 0:
                            join_cols(way)

                def finish(b, _):
                    inflow_ref[b, h * part : (h + 1) * part, :] = partial[b]
                    return 0

                lax.fori_loop(0, blocks, finish, 0)
                if first and h == 0:
                    colsum[...] += F32(1)
            step = i * halves + h
            if first and 0 < step < columns:
                spread.hop(step)
            if first and step < pieces:
                count_seeds(columns, cores_ref, tally, step, pieces)
            if first and step == pieces:
                spread_seeds(cores_ref.shape[1], tally, spam_ref)

    if first:
        for t in others:
            know(t, r).wait_send()
            know(t, t).wait_recv()
        spread.collect()
        spread.finish()
    for i in range(columns):
        for h in range(halves):
            for t in others:
                across(i, h, t, r).wait_send()
            if i < columns - 1:
                chain(i, h, jnp.where(targets[i] > z, 0, 1)).wait_send()


def trust_kernel(inflow, good_ref, spam_ref, weight_ref, keys_ref, trust_ref, shield_ref, vals_ref):
    blocks, seeds, size = inflow.shape
    lines = keys_ref.shape[0]
    groups = seeds // lines
    keys = keys_ref[...].astype(jnp.int32) & (blocks * size - 1)
    lanes = keys // blocks
    block = keys & (blocks - 1)
    part = lax.broadcasted_iota(jnp.int32, (lines, size), 1) // (size // groups)

    def one(b, vals):
        trust = F32(0.85) * inflow[b] + F32(0.15) * good_ref[b]
        trust_ref[pl.ds(pl.multiple_of(b * size, size), size), :] = jnp.transpose(trust)
        shield = F32(1) / (F32(1) + trust)
        shield_ref[b] = shield
        share = (shield * spam_ref[b] / weight_ref[pl.ds(b, 1), :]).astype(BF16).astype(F32)
        for g in range(groups):
            got = take(share[g * lines : (g + 1) * lines, :], lanes)
            vals = jnp.where((block == b) & (part == g), got, vals)
        return vals

    vals = lax.fori_loop(0, blocks, one, jnp.zeros((lines, size), F32), unroll=2)
    vals_ref[...] = vals.astype(BF16)


def pull_kernel(last, *refs):
    if last:
        src_ref, slot_ref, fetched_ref, spam_ref, tiles_ref, out_ref, acc = refs
    else:
        (src_ref, slot_ref, block_ref, lists_ref, vals_ref, rank_ref, spam_ref, shield_ref, weight_ref,
         tiles_ref, out_ref, acc, fetched_ref, codes, bounds, sem) = refs
    step = pl.program_id(0)
    per_step = tiles_ref.shape[0]
    size = acc.shape[2]

    @pl.when(step == 0)
    def _():
        acc[...] = jnp.zeros_like(acc)
        if not last:
            blocks = acc.shape[0]
            codes[...] = lists_ref[:, 0, :].astype(jnp.int32) // (blocks * size)
            copy = pltpu.make_async_copy(codes, bounds, sem)
            copy.start()
            copy.wait()
            expand(
                block_ref.shape[0] // lists_ref.shape[0], block_ref, lists_ref, vals_ref, rank_ref,
                blocks, bounds, fetched_ref,
            )

    def some(g, _):
        products = []
        for k in range(GROUP):
            n = step * per_step + g * GROUP + k
            products.append(
                lax.dot_general(
                    fetched_ref[slot_ref[n]], tiles_ref[g * GROUP + k], (((1,), (1,)), ((), ())),
                    preferred_element_type=F32,
                )
            )
        for k in range(GROUP):
            acc[src_ref[step * per_step + g * GROUP + k]] += products[k]
        return 0

    lax.fori_loop(0, per_step // GROUP, some, 0)

    @pl.when(step == pl.num_programs(0) - 1)
    def _():
        def distrust(b):
            return F32(0.85) * acc[b] + F32(0.15) * spam_ref[b]

        if last:
            def one(b, _):
                out_ref[pl.ds(pl.multiple_of(b * size, size), size), :] = jnp.transpose(distrust(b))
                return 0

            lax.fori_loop(0, acc.shape[0], one, 0)
        else:
            shares(shield_ref, weight_ref, distrust, out_ref)


def start_kernel(columns, good_ref, spam_ref, count_ref, list_ref, keys_ref, tally):
    raw = spam_ref[...]
    list_ref[...] = jnp.transpose(raw.astype(F32)).astype(jnp.int32)
    keys_ref[...] = sort_hosts(columns, count_ref.shape[0], raw)
    count_seeds(columns, good_ref, tally)
    spread_seeds(good_ref.shape[1], tally, count_ref)


def body(columns, tiles, tile_src, tile_slot, slot_block, out_degree, good_seeds, spam_cores):
    tile_count, size, _ = tiles.shape
    here = lambda x: pltpu.with_memory_space_constraint(x, pltpu.HBM)
    hosts = out_degree.shape[0]
    blocks = hosts // size
    seeds = good_seeds.shape[0]
    slots = slot_block.shape[0]
    peers = lax.axis_size(AXES)
    cap = slots // peers
    tail = -(-4 * cap // 16) * 16
    steps = 8
    shape = jax.ShapeDtypeStruct
    vector = (blocks, seeds, size)
    degree = out_degree.reshape(blocks, 1, size)

    rows = peers // columns
    part = seeds // HALVES
    count = spam_cores.shape[1]
    groups = seeds // count
    lines = seeds // groups
    good, spam_list, keys = pl.pallas_call(
        functools.partial(start_kernel, columns),
        out_shape=(
            shape(vector, F32), shape(spam_cores.shape, jnp.int32), shape((lines, size), jnp.int16),
        ),
        in_specs=[VM, VM],
        out_specs=(VM, VM, VM),
        scratch_shapes=[pltpu.VMEM((seeds, blocks, size), F32)],
        compiler_params=PLAIN,
        cost_estimate=pl.CostEstimate(
            flops=2 * seeds * good_seeds.size * (blocks + size), transcendentals=0,
            bytes_accessed=24 << 20,
        ),
    )(here(good_seeds), here(spam_cores.T))

    tile_spec = pl.BlockSpec((tile_count // steps, size, size), lambda i: (i, 0, 0))
    words = shape((peers, cap * size + tail, size), jnp.int16)
    outgoing = pl.pallas_call(
        functools.partial(push_kernel, True, cap, part),
        grid=(steps,),
        out_shape=words,
        in_specs=[SM, SM, SM, VM, VM, tile_spec],
        out_specs=VM,
        scratch_shapes=[
            pltpu.VMEM((slots, seeds + 16, size), F32),
            pltpu.VMEM((blocks, seeds + 16, size), BF16),
        ],
        compiler_params=PLAIN,
    )(here(tile_src), here(tile_slot), here(slot_block), good, here(degree), here(tiles))

    dma = pltpu.SemaphoreType.DMA
    spread_sems = [
        dma((2, columns)), dma((columns,)), dma((rows, columns)), dma((rows, columns)),
        dma((rows, columns)), dma((rows, columns)),
    ]

    def reduce(first, words_in, *rest):
        long = blocks * part + blocks * (4 if first else 1)
        outs = (
            shape(vector, F32), shape((blocks, size), F32), shape(vector, F32),
            shape((rows, 1, slots), jnp.int32), shape((peers, lines, size), jnp.int16),
        )
        return pl.pallas_call(
            functools.partial(reduce_kernel, first, rows, columns, cap),
            out_shape=outs if first else outs[:1],
            in_specs=[ANY, VM, VM, VM] if first else [ANY],
            out_specs=(VM,) * 5 if first else (VM,),
            scratch_shapes=[
                pltpu.VMEM((columns, rows, cap * size + tail, size), jnp.int16),
                pltpu.VMEM((rows * cap, blocks, size), F32),
                pltpu.VMEM((blocks, part, size), F32),
                pltpu.VMEM((blocks, size), F32),
                pltpu.VMEM((columns - 1, HALVES, long, size), jnp.int16),
                pltpu.VMEM((2, columns, HALVES, long, size), jnp.int16),
                dma((columns,)),
                dma((columns, HALVES, rows)),
                dma((columns, HALVES, rows)),
                dma((columns - 1, HALVES)),
                dma((2, columns, HALVES)),
                *([dma((rows,)), dma((rows,)), pltpu.VMEM((seeds, blocks, size), F32), *spread_sems] if first else []),
            ],
            compiler_params=pltpu.CompilerParams(
                collective_id=1 if first else 2, has_side_effects=True,
                vmem_limit_bytes=LIMIT,
            ),
        )(words_in, *rest)

    inflow, weight, spam, want, lists = reduce(
        True, outgoing, spam_list, slot_block.reshape(1, slots), keys
    )
    outgoing = pl.pallas_call(
        functools.partial(push_kernel, False, cap, part),
        grid=(steps,),
        out_shape=words,
        in_specs=[SM, SM, SM, VM, VM, VM, tile_spec],
        out_specs=VM,
        scratch_shapes=[
            pltpu.VMEM((slots, seeds, size), F32),
            pltpu.VMEM(vector, BF16),
        ],
        compiler_params=PLAIN,
    )(tile_src, tile_slot, slot_block, inflow, good, degree, tiles)
    (inflow,) = reduce(False, outgoing)
    fetch = pl.pallas_call(
        functools.partial(fetch_kernel, rows, columns, cap),
        out_shape=shape((slots, seeds, size), BF16),
        in_specs=[SM, VM],
        out_specs=VM,
        scratch_shapes=[
            *[pltpu.VMEM(vector, BF16)] * (2 * columns - 2),
            pltpu.VMEM((rows, columns * cap, seeds, size), BF16),
            pltpu.SemaphoreType.DMA((2 * columns - 2,)),
            pltpu.SemaphoreType.DMA((2 * columns - 2,)),
            pltpu.SemaphoreType.DMA((rows, columns)),
            pltpu.SemaphoreType.DMA((rows, columns)),
        ],
        compiler_params=pltpu.CompilerParams(collective_id=0, has_side_effects=True, vmem_limit_bytes=LIMIT),
    )
    trust, shield, vals = pl.pallas_call(
        trust_kernel,
        out_shape=(shape((hosts, seeds), F32), shape(vector, F32), shape((lines, size), BF16)),
        in_specs=[VM, VM, VM, VM, VM],
        out_specs=(VM, VM, VM),
        compiler_params=PLAIN,
    )(inflow, good, spam, weight, keys)
    vals, ranks = pl.pallas_call(
        functools.partial(value_kernel, rows, columns, groups, blocks),
        out_shape=(shape((peers, lines, size), BF16), shape((peers, seeds, size), jnp.int32)),
        in_specs=[VM, VM],
        out_specs=(VM, VM),
        scratch_shapes=spread_sems,
        compiler_params=pltpu.CompilerParams(
            collective_id=3, has_side_effects=True, vmem_limit_bytes=LIMIT
        ),
    )(vals, lists)
    share = pl.pallas_call(
        functools.partial(pull_kernel, False),
        grid=(steps,),
        out_shape=shape(vector, BF16),
        in_specs=[SM, SM, SM, VM, VM, VM, VM, VM, VM, tile_spec],
        out_specs=VM,
        scratch_shapes=[
            pltpu.VMEM(vector, F32),
            pltpu.VMEM((slots, seeds, size), BF16),
            pltpu.VMEM((peers, size), jnp.int32),
            pltpu.SMEM((peers, size), jnp.int32),
            pltpu.SemaphoreType.DMA,
        ],
        compiler_params=PLAIN,
    )(tile_src, tile_slot, slot_block, lists, vals, ranks, spam, shield, weight, tiles)
    fetched = fetch(want, share)
    distrust = pl.pallas_call(
        functools.partial(pull_kernel, True),
        grid=(steps,),
        out_shape=shape((hosts, seeds), F32),
        in_specs=[SM, SM, VM, VM, tile_spec],
        out_specs=VM,
        scratch_shapes=[pltpu.VMEM(vector, F32)],
        compiler_params=PLAIN,
    )(tile_src, tile_slot, fetched, spam, tiles)
    return trust, distrust


def solution(mesh):
    in_specs = (
        P(AXES, None, None),
        P(AXES),
        P(AXES),
        P(AXES),
        P(AXES),
        P(None, AXES),
        P(None, AXES),
    )
    out_specs = (P(AXES, None), P(AXES, None))
    return jax.shard_map(
        functools.partial(body, mesh.shape["col"]),
        mesh=mesh, in_specs=in_specs, out_specs=out_specs, check_vma=False,
    )
```

```python
import functools

import jax
import jax.numpy as jnp
from jax import lax
from jax.experimental import pallas as pl
from jax.experimental.pallas import tpu as pltpu
from jax.sharding import PartitionSpec as P

AXES = ("row", "col")
VM = pl.BlockSpec(memory_space=pltpu.VMEM)
SM = pl.BlockSpec(memory_space=pltpu.SMEM)
LIMIT = 28 << 20
ANY = pl.BlockSpec(memory_space=pl.ANY)
F32 = jnp.float32
BF16 = jnp.bfloat16
PLAIN = pltpu.CompilerParams(vmem_limit_bytes=LIMIT)
WORD = 15
GROUP = 16
HALVES = 4
LAYERS = 6
MORE = 2
MESH = pl.DeviceIdType.MESH


def count_seeds(columns, source, tally, step=0, pieces=1):
    seeds, blocks, size = tally.shape
    hosts = blocks * size
    base = (lax.axis_index("row") * columns + lax.axis_index("col")) * hosts
    count = source.shape[1]
    block_iota = lax.broadcasted_iota(jnp.int32, (blocks, count), 0) * size
    lane_iota = lax.broadcasted_iota(jnp.int32, (size, count), 0)

    def one(s, _):
        local = source[pl.ds(s, 1), :] - base
        shifted = local - block_iota
        inside = jnp.where((shifted >= 0) & (shifted < size), F32(1), F32(0)).astype(BF16)
        start = jnp.max(jnp.where(local >= block_iota, block_iota, 0), axis=0, keepdims=True)
        lane = jnp.where(lane_iota == local - start, F32(1), F32(0)).astype(BF16)
        tally[s] = lax.dot_general(
            inside, lane, (((1,), (1,)), ((), ())), preferred_element_type=F32
        )
        return 0

    share = seeds // pieces
    lax.fori_loop(step * share, (step + 1) * share, one, 0, unroll=16)


def spread_seeds(count, tally, target):
    blocks, _, size = target.shape
    factor = F32(blocks * size / count)
    for b in range(blocks):
        target[b] = tally[:, b, :] * factor


def exponent_of(peak):
    return jnp.floor(jnp.log2(jnp.maximum(peak, F32(2.0**-100)))) + F32(1)


def to_words(value):
    return jnp.clip(jnp.floor(value + F32(0.5)), F32(-32767), F32(32767))


def pack(first, cap, part, bits, acc, block_ref, out_ref):
    peers = out_ref.shape[0]
    size = acc.shape[2]
    halves = size // part
    tail = out_ref.shape[1] - cap * size

    def one(p, _):
        exps, cols = [], []
        for c in range(cap):
            n = p * cap + c
            value = acc[n, :size, :]
            e = exponent_of(jnp.max(jnp.abs(value), axis=0, keepdims=True))
            words = to_words(value * jnp.exp2(WORD - e)).astype(jnp.int32).astype(jnp.int16)
            for h in range(halves):
                at = (h * cap + c) * part + (tail if h else 0)
                out_ref[p, at : at + part, :] = words[h * part : (h + 1) * part, :]
            exps.append(e * F32(2**bits) + block_ref[n].astype(F32))
            if first:
                col = acc[n, size : size + 8, :][:1, :]
                f = exponent_of(jnp.abs(col))
                scaled = col * jnp.exp2(WORD - f)
                high = to_words(scaled)
                cols += [f, high, to_words((scaled - high) * F32(2.0**WORD))]
        rows = exps + cols
        if tail > len(rows):
            rows.append(jnp.zeros((tail - len(rows), size), F32))
        at = cap * part
        out_ref[p, at : at + tail, :] = jnp.concatenate(rows, axis=0).astype(jnp.int32).astype(jnp.int16)
        return 0

    lax.fori_loop(0, peers, one, 0)


def push_kernel(first, cap, part, *refs):
    if first:
        src_ref, slot_ref, block_ref, good_ref, degree_ref, tiles_ref, out_ref, acc, scaled = refs
    else:
        src_ref, slot_ref, block_ref, inflow, good_ref, degree_ref, tiles_ref, out_ref, acc, scaled = refs
    step = pl.program_id(0)
    blocks, seeds, size = good_ref.shape
    per_step = tiles_ref.shape[0]

    @pl.when(step == 0)
    def _():
        acc[...] = jnp.zeros_like(acc)
        def one(b, _):
            degree = degree_ref[b].astype(F32)
            trust = good_ref[b]
            if not first:
                trust = F32(0.85) * inflow[b] + F32(0.15) * trust
            scaled[b, :seeds, :] = (trust / degree).astype(BF16)
            if first:
                scaled[b, seeds:, :] = jnp.ones((scaled.shape[1] - seeds, size), BF16)
            return 0

        lax.fori_loop(0, blocks, one, 0)

    def some(g, _):
        products = []
        for k in range(GROUP):
            n = step * per_step + g * GROUP + k
            products.append(
                jnp.dot(scaled[src_ref[n]], tiles_ref[g * GROUP + k], preferred_element_type=F32)
            )
        for k in range(GROUP):
            acc[slot_ref[step * per_step + g * GROUP + k]] += products[k]
        return 0

    lax.fori_loop(0, per_step // GROUP, some, 0)

    @pl.when(step == pl.num_programs(0) - 1)
    def _():
        pack(first, cap, part, blocks.bit_length() - 1, acc, block_ref, out_ref)


def shares(shield_ref, weight_ref, start_of, share_ref):
    def one(b, _):
        weight = weight_ref[pl.ds(b, 1), :]
        share_ref[b] = (shield_ref[b] * start_of(b) / weight).astype(BF16)
        return 0

    lax.fori_loop(0, share_ref.shape[0], one, 0)


def greet(devices):
    barrier = pltpu.get_barrier_semaphore()
    for device, there in devices:
        @pl.when(there)
        def _():
            pl.semaphore_signal(barrier, inc=1, device_id=device, device_id_type=MESH)
    pl.semaphore_wait(barrier, sum(jnp.where(there, 1, 0) for _, there in devices))


def fetch_kernel(rows, columns, cap, want_ref, share_ref, fetched_ref, *scratch):
    line = 2 * (columns - 1)
    held, (picked, line_send, line_recv, send, recv) = scratch[:line], scratch[line:]
    r, z = lax.axis_index("row"), lax.axis_index("col")
    others = [lax.rem(r + d, rows) for d in range(1, rows)]
    sides = (-1, 1)
    inside = {side: (z + side >= 0) & (z + side < columns) for side in sides}
    greet([((t, z), t >= 0) for t in others] + [((r, z + side), inside[side]) for side in sides])

    def place(side, d):
        return 2 * (d - 1) + (0 if side < 0 else 1)

    def pass_on(source, d, side):
        slot = place(-side, d)
        return pltpu.make_async_remote_copy(
            src_ref=source, dst_ref=held[slot],
            send_sem=line_send.at[slot], recv_sem=line_recv.at[slot],
            device_id=(r, z + side), device_id_type=MESH,
        )

    def serve(t, origin):
        return pltpu.make_async_remote_copy(
            src_ref=picked.at[t, pl.ds(origin * cap, cap)],
            dst_ref=fetched_ref.at[pl.ds((r * columns + origin) * cap, cap)],
            send_sem=send.at[t, origin], recv_sem=recv.at[r, origin],
            device_id=(t, z), device_id_type=MESH,
        )

    def spread(source, origin):
        before = None
        for t in others:
            for j in range(cap):
                picked[t, origin * cap + j] = source[want_ref[t, 0, (r * columns + origin) * cap + j]]
            if before is not None:
                serve(before, origin).start()
            before = t
        for j in range(cap):
            fetched_ref[(r * columns + origin) * cap + j] = source[want_ref[r, 0, (r * columns + origin) * cap + j]]
        serve(before, origin).start()

    for side in sides:
        @pl.when(inside[side])
        def _():
            pass_on(share_ref, 1, side).start()
    spread(share_ref, z)
    for d in range(1, columns):
        for side in sides:
            origin = z + side * d

            @pl.when((origin >= 0) & (origin < columns))
            def _():
                here = held[place(side, d)]
                pass_on(share_ref, d, -side).wait_recv()

                if d < columns - 1:
                    @pl.when(inside[-side])
                    def _():
                        pass_on(here, d + 1, -side).start()

                spread(here, origin)
    for origin in range(columns):
        for t in others:
            serve(t, origin).wait_send()
            pltpu.make_async_remote_copy(
                src_ref=picked.at[t, pl.ds(origin * cap, cap)],
                dst_ref=fetched_ref.at[pl.ds((t * columns + origin) * cap, cap)],
                send_sem=send.at[t, origin], recv_sem=recv.at[t, origin],
                device_id=(t, z), device_id_type=MESH,
            ).wait_recv()
    for d in range(columns - 1):
        for side in sides:
            origin = z - side * d

            @pl.when((origin >= 0) & (origin < columns) & inside[side])
            def _():
                pass_on(share_ref, d + 1, side).wait_send()


def take(table, index):
    return jnp.take_along_axis(table, index, axis=1, mode="promise_in_bounds")


def find_ranks(groups, blocks, keys):
    lines, size = keys.shape
    count = size // groups
    least = lax.broadcasted_iota(jnp.int32, (lines, size), 1) * blocks
    spots = [jnp.full((lines, size), count * g, jnp.int32) for g in range(groups)]
    step = count // 2
    while True:
        probes = [take(keys, spot + (max(step, 1) - 1)) for spot in spots]
        spots = [spot + jnp.where(probe < least, max(step, 1), 0) for spot, probe in zip(spots, probes)]
        if step == 0:
            return spots
        step //= 2


def ends_of(g, groups, spots):
    lines, size = spots.shape
    lane = lax.broadcasted_iota(jnp.int32, (lines, size), 1)
    after = pltpu.roll(spots, size - 1, 1)
    return jnp.where(lane == size - 1, (size // groups) * (g + 1), after)


def sort_hosts(columns, blocks, raw):
    count, seeds = raw.shape
    groups = seeds // count
    lines = seeds // groups
    base = (lax.axis_index("row") * columns + lax.axis_index("col")) * (blocks * seeds)
    local = (raw - base).astype(F32)
    stacked = jnp.concatenate(
        [local] + [pltpu.roll(local, seeds - g * lines, 1) for g in range(1, groups)], axis=0
    )
    hosts = jnp.transpose(stacked)[:lines, :].astype(jnp.int32)
    keys = ((hosts & (seeds - 1)) * blocks + hosts // seeds).astype(F32)
    lane = lax.broadcasted_iota(jnp.int32, keys.shape, 1)
    k = 2
    while k <= count:
        j = k // 2
        while j:
            other = take(keys, lane ^ j)
            rising = ((lane & k) == 0) | (k == count)
            lower = ((lane & j) == 0) == rising
            keys = jnp.where(lower, jnp.minimum(keys, other), jnp.maximum(keys, other))
            j //= 2
        k *= 2
    keys = keys.astype(jnp.int32)
    spots = find_ranks(groups, blocks, keys)
    most = functools.reduce(
        jnp.maximum, [ends_of(g, groups, spot) - spot for g, spot in enumerate(spots)]
    ).astype(F32)
    most = jnp.max(jnp.max(most, axis=1, keepdims=True), axis=0, keepdims=True).astype(jnp.int32)
    code = jnp.where(most > LAYERS, 1, 0) + jnp.where(most > LAYERS + MORE, 1, 0)
    return (keys + code * (blocks * seeds)).astype(jnp.int16)


class Spread:
    def __init__(self, rows, columns, own, out, sems):
        self.rows, self.columns, self.own, self.out = rows, columns, own, out
        self.line_send, self.line_recv, self.plane_send, self.plane_recv, self.pair_send, self.pair_recv = sems
        r, z = lax.axis_index("row"), lax.axis_index("col")
        self.r, self.z = r, z
        self.twin = r + 1 - 2 * lax.rem(r, 2)
        self.mates = [lax.rem(r + d, rows) for d in range(2, rows, 2)]
        self.others = [self.twin] + [lax.rem(self.twin + d, rows) for d in range(2, rows, 2)]
        self.inside = {side: (z + side >= 0) & (z + side < columns) for side in (-1, 1)}

    def send(self, source, row, origin, sends, recvs, to):
        return pltpu.make_async_remote_copy(
            src_ref=source, dst_ref=self.out.at[row * self.columns + origin],
            send_sem=sends, recv_sem=recvs, device_id=to, device_id_type=MESH,
        )

    def place(self, row, origin):
        return self.out.at[row * self.columns + origin]

    def line(self, source, origin, side):
        way = 0 if side < 0 else 1
        return self.send(
            source, self.r, origin, self.line_send.at[way, origin], self.line_recv.at[origin],
            (self.r, self.z + side),
        )

    def plane(self, source, t, row, origin):
        return self.send(
            source, row, origin, self.plane_send.at[t, origin], self.plane_recv.at[row, origin],
            (t, self.z),
        )

    def pair(self, source, row, origin):
        return self.send(
            source, row, origin, self.pair_send.at[row, origin], self.pair_recv.at[row, origin],
            (self.twin, self.z),
        )

    def across(self, source, origin):
        for t in self.mates:
            self.plane(source, t, self.r, origin).start()
        self.pair(source, self.r, origin).start()

    def begin(self):
        for side in (-1, 1):
            @pl.when(self.inside[side])
            def _():
                self.line(self.own, self.z, side).start()
        self.across(self.own, self.z)
        self.out[self.r * self.columns + self.z] = self.own[...]

    def each(self, d):
        for side in (-1, 1):
            origin = self.z + side * d
            yield side, origin, (origin >= 0) & (origin < self.columns)

    def hop(self, d):
        for side, origin, there in self.each(d):
            @pl.when(there)
            def _():
                here = self.place(self.r, origin)
                self.line(here, origin, side).wait_recv()

                @pl.when(self.inside[-side])
                def _():
                    self.line(here, origin, -side).start()

                self.across(here, origin)

    def collect(self):
        for t in self.mates:
            for origin in range(self.columns):
                here = self.place(t, origin)
                self.plane(here, t, t, origin).wait_recv()
                self.pair(here, t, origin).start()

    def finish(self):
        for t in self.others:
            for origin in range(self.columns):
                self.pair(self.place(t, origin), t, origin).wait_recv()
        for side in (-1, 1):
            @pl.when(self.inside[side])
            def _():
                self.line(self.own, self.z, side).wait_send()
        for d in range(1, self.columns):
            for side, origin, there in self.each(d):
                @pl.when(there & self.inside[-side])
                def _():
                    self.line(self.own, origin, -side).wait_send()
        for origin in range(self.columns):
            for t in self.mates:
                self.plane(self.own, t, self.r, origin).wait_send()
                self.pair(self.own, t, origin).wait_send()
            self.pair(self.own, self.r, origin).wait_send()


def value_kernel(rows, columns, own_ref, vals_ref, *sems):
    spread = Spread(rows, columns, own_ref, vals_ref, sems)
    greet(
        [((t, spread.z), t >= 0) for t in spread.mates + [spread.twin]]
        + [((spread.r, spread.z + side), spread.inside[side]) for side in (-1, 1)]
    )
    spread.begin()
    for d in range(1, columns):
        spread.hop(d)
    spread.collect()
    spread.finish()


def expand(cap, block_ref, lists_ref, vals_ref, rank_ref, blocks, bounds, fetched):
    peers, lines, size = lists_ref.shape
    groups = fetched.shape[1] // lines
    tall = 16

    def paint(q, low, high, fresh):
        tags = [
            F32(1) + (block_ref[q * cap + c] + 1).astype(F32) * F32(2.0**-14) for c in range(cap)
        ]

        def some(i, _):
            at = pl.multiple_of(i * tall, tall)
            block = lists_ref[q, pl.ds(at, tall), :].astype(jnp.int32) & (blocks - 1)
            value = vals_ref[q, pl.ds(at, tall), :].astype(F32)
            marked = value * (F32(1) + (block + 1).astype(F32) * F32(2.0**-14))
            for g in range(groups):
                row = pl.multiple_of(g * lines + at, tall)
                spots = rank_ref[q, pl.ds(row, tall), :]
                ends = ends_of(g, groups, spots)

                def layer(j, outs):
                    spot = spots + j
                    live = spot < ends
                    got = jnp.where(live, take(marked, jnp.minimum(spot, size - 1)), F32(0))
                    plain = got.astype(BF16).astype(F32)
                    return tuple(
                        jnp.where(live & (plain * tag == got), plain, out) for tag, out in zip(tags, outs)
                    )

                if fresh:
                    outs = (jnp.zeros((tall, size), F32),) * cap
                else:
                    outs = tuple(
                        fetched[q * cap + c, pl.ds(row, tall), :].astype(F32) for c in range(cap)
                    )
                if high - low > LAYERS:
                    outs = lax.fori_loop(low, high, layer, outs)
                else:
                    for j in range(low, high):
                        outs = layer(j, outs)
                for c in range(cap):
                    fetched[q * cap + c, pl.ds(row, tall), :] = outs[c].astype(BF16)
            return 0

        lax.fori_loop(0, lines // tall, some, 0, unroll=2 if fresh else 1)

    def one(q, _):
        paint(q, 0, LAYERS, True)
        code = bounds[q, 0]

        @pl.when(code > 0)
        def _():
            paint(q, LAYERS, LAYERS + MORE, False)

        @pl.when(code > 1)
        def _():
            paint(q, LAYERS + MORE, size // groups, False)

        return 0

    lax.fori_loop(0, peers, one, 0)


def order_of(z, columns):
    table = []
    for plane in range(columns):
        line = []
        for k in range(columns):
            if columns - 1 - k > plane:
                line.append(columns - 1 - k)
            if k < plane:
                line.append(k)
        table.append(line + [plane])
    picks = []
    for i in range(columns):
        pick = z * 0
        for plane in range(columns):
            pick = pick + jnp.where(z == plane, table[plane][i], 0)
        picks.append(pick)
    return picks


def reduce_kernel(first, rows, columns, cap, words_ref, *refs):
    if first:
        cores_ref, mine_ref, raw_ref, inflow_ref, weight_ref, spam_ref, want_ref, keys_ref, lists_ref, *refs = refs
    else:
        lists_ref, inflow_ref, rank_ref, *refs = refs
    landed, table, partial, exps, packed, inbox, own, send, recv, chain_send, chain_recv, *refs = refs
    r, z = lax.axis_index("row"), lax.axis_index("col")
    blocks, part, size = partial.shape
    seeds = inflow_ref.shape[1]
    halves = seeds // part
    bits = blocks.bit_length() - 1
    tail_at = cap * part
    spans = []
    for h in range(halves):
        start = spans[-1][0] + spans[-1][1] if spans else 0
        spans.append((start, cap * part + (landed.shape[2] - cap * seeds if h == 0 else 0)))
    data = blocks * part
    longs = [data + blocks * (4 if first and h == 0 else 1) for h in range(halves)]
    others = [lax.rem(r + d, rows) for d in range(1, rows)]
    targets = order_of(z, columns)
    block_iota = lax.broadcasted_iota(jnp.int32, (blocks, size), 0)
    greet(
        [((t, z), t >= 0) for t in others]
        + [((r, z - 1), z > 0), ((r, z + 1), z < columns - 1)]
    )

    def across(i, h, t, origin):
        at = pl.ds(*spans[h])
        return pltpu.make_async_remote_copy(
            src_ref=words_ref.at[t * columns + targets[i], at], dst_ref=landed.at[i, origin, at],
            send_sem=send.at[i, h, t], recv_sem=recv.at[i, h, origin],
            device_id=(t, z), device_id_type=MESH,
        )

    def mine(i):
        return pltpu.make_async_copy(
            words_ref.at[r * columns + targets[i]], landed.at[i, r], own.at[i]
        )

    def chain(i, h, side):
        at = pl.ds(0, longs[h])
        return pltpu.make_async_remote_copy(
            src_ref=packed.at[min(i, columns - 2), h, at], dst_ref=inbox.at[side, targets[i], h, at],
            send_sem=chain_send.at[min(i, columns - 2), h], recv_sem=chain_recv.at[side, targets[i], h],
            device_id=(r, z + 1 - 2 * side), device_id_type=MESH,
        )

    def to_int16(value):
        return value.astype(jnp.int32).astype(jnp.int16)

    def to_float(value):
        return value.astype(jnp.int32).astype(F32)

    if first:
        known_send, known_recv, tally, *sems = refs
        spread = Spread(rows, columns, keys_ref, lists_ref, sems)

        def know(t, origin):
            return pltpu.make_async_remote_copy(
                src_ref=mine_ref, dst_ref=want_ref.at[origin],
                send_sem=known_send.at[t], recv_sem=known_recv.at[origin],
                device_id=(t, z), device_id_type=MESH,
            )

        for t in others:
            know(t, r).start()
        want_ref[r] = mine_ref[...]

    def launch(i):
        for h in range(halves):
            for t in others:
                across(i, h, t, r).start()
        mine(i).start()

    launch(0)
    launch(1)
    if first:
        keys_ref[...] = sort_hosts(columns, blocks, raw_ref[...])
        spread.begin()
    else:
        peers, lines, _ = lists_ref.shape
        groups = seeds // lines
        turns = min(8, (columns - 1) * halves)
        load = -(-peers // turns)

        def find(q, _):
            keys = lists_ref[q].astype(jnp.int32) & (blocks * size - 1)
            for g, spots in enumerate(find_ranks(groups, blocks, keys)):
                rank_ref[q, g * lines : (g + 1) * lines, :] = spots
            return 0

    pieces = min(4, (columns - 1) * halves)
    for i in range(columns):
        mine(i).wait()
        side = jnp.where(targets[i] > z, 0, 1)
        joined = jnp.where(targets[i] > z, z > 0, z < columns - 1)
        cols = jnp.zeros((blocks, size), F32)
        for h in range(halves):
            for t in others:
                across(i, h, t, t).wait_recv()
            if h == 0:
                def weigh(q, cols):
                    tail = landed[i, q, tail_at : spans[0][1], :].astype(jnp.int32)
                    for c in range(cap):
                        word = tail[c : c + 1, :]
                        hit = block_iota == (word & (blocks - 1))
                        scale = jnp.exp2((word >> bits).astype(F32) - WORD)
                        table[q * cap + c] = jnp.where(
                            hit, jnp.broadcast_to(scale, (blocks, size)), F32(0)
                        )
                        if first:
                            f, high, low = (
                                tail[cap + 3 * c + k : cap + 3 * c + k + 1, :].astype(F32) for k in range(3)
                            )
                            col = (high + low * F32(2.0**-WORD)) * jnp.exp2(f - WORD)
                            cols = cols + jnp.where(hit, jnp.broadcast_to(col, (blocks, size)), F32(0))
                    return cols

                cols = lax.fori_loop(0, rows, weigh, cols)

            begin = spans[h][0]

            def strip(k, _):
                at = pl.multiple_of(k * 16, 16)

                def add(q, sums):
                    sums = list(sums)
                    for c in range(cap):
                        spot = pl.multiple_of(begin + c * part + at, 16)
                        value = to_float(landed[i, q, pl.ds(spot, 16), :])
                        for b in range(blocks):
                            sums[b] = sums[b] + value * table[q * cap + c, b : b + 1, :]
                    return tuple(sums)

                sums = lax.fori_loop(0, rows, add, (jnp.zeros((16, size), F32),) * blocks)
                for b in range(blocks):
                    partial[b, pl.ds(at, 16), :] = sums[b]
                return 0

            lax.fori_loop(0, part // 16, strip, 0)

            def join(way):
                chain(i, h, way).wait_recv()
                exps[...] = jnp.exp2(to_float(inbox[way, targets[i], h, data : data + blocks, :]) - WORD)

                def one(b, _):
                    got = to_float(inbox[way, targets[i], h, pl.ds(pl.multiple_of(b * part, part), part), :])
                    partial[b] += got * exps[pl.ds(b, 1), :]
                    return 0

                lax.fori_loop(0, blocks, one, 0)

            def join_cols(way):
                f, high, low = (
                    to_float(inbox[way, targets[i], h, data + (k + 1) * blocks : data + (k + 2) * blocks, :])
                    for k in range(3)
                )
                colsum[...] += (high + low * F32(2.0**-WORD)) * jnp.exp2(f - WORD)

            if first and h == 0:
                colsum = weight_ref
                colsum[...] = cols
            if i < columns - 1:
                @pl.when(joined)
                def _():
                    join(side)
                    if first and h == 0:
                        join_cols(side)

                def squeeze(b, _):
                    value = partial[b]
                    e = exponent_of(jnp.max(jnp.abs(value), axis=0, keepdims=True))
                    exps[pl.ds(b, 1), :] = e
                    packed[i, h, pl.ds(pl.multiple_of(b * part, part), part), :] = to_int16(
                        to_words(value * jnp.exp2(WORD - e))
                    )
                    return 0

                lax.fori_loop(0, blocks, squeeze, 0)
                packed[i, h, data : data + blocks, :] = to_int16(exps[...])
                if first and h == 0:
                    col = colsum[...]
                    f = exponent_of(jnp.abs(col))
                    scaled = col * jnp.exp2(WORD - f)
                    high = to_words(scaled)
                    for k, row in enumerate((f, high, to_words((scaled - high) * F32(2.0**WORD)))):
                        packed[i, h, data + (k + 1) * blocks : data + (k + 2) * blocks, :] = to_int16(row)
                chain(i, h, side).start()
            else:
                for way, there in ((0, z > 0), (1, z < columns - 1)):
                    @pl.when(there)
                    def _():
                        join(way)
                        if first and h == 0:
                            join_cols(way)

                def finish(b, _):
                    inflow_ref[b, h * part : (h + 1) * part, :] = partial[b]
                    return 0

                lax.fori_loop(0, blocks, finish, 0)
                if first and h == 0:
                    colsum[...] += F32(1)
            step = i * halves + h
            if first and step < columns - 1:
                spread.hop(step + 1)
            if h == min(columns, halves) - 1 and i + 2 < columns:
                launch(i + 2)
            if first and step == (columns - 2) * halves:
                spread.collect()
            if not first and step < turns:
                lax.fori_loop(step * load, min(peers, (step + 1) * load), find, 0, unroll=2)
            if first and step < pieces:
                count_seeds(columns, cores_ref, tally, step, pieces)
            if first and step == pieces:
                spread_seeds(cores_ref.shape[1], tally, spam_ref)

    if first:
        for t in others:
            know(t, r).wait_send()
            know(t, t).wait_recv()
        spread.finish()
    for i in range(columns):
        for h in range(halves):
            for t in others:
                across(i, h, t, r).wait_send()
            if i < columns - 1:
                chain(i, h, jnp.where(targets[i] > z, 0, 1)).wait_send()


def trust_kernel(inflow, good_ref, spam_ref, weight_ref, keys_ref, trust_ref, shield_ref, vals_ref):
    blocks, seeds, size = inflow.shape
    lines = keys_ref.shape[0]
    groups = seeds // lines
    keys = keys_ref[...].astype(jnp.int32) & (blocks * size - 1)
    lanes = keys // blocks
    block = keys & (blocks - 1)
    part = lax.broadcasted_iota(jnp.int32, (lines, size), 1) // (size // groups)

    def one(b, vals):
        trust = F32(0.85) * inflow[b] + F32(0.15) * good_ref[b]
        trust_ref[pl.ds(pl.multiple_of(b * size, size), size), :] = jnp.transpose(trust)
        shield = F32(1) / (F32(1) + trust)
        shield_ref[b] = shield
        share = (shield * spam_ref[b] / weight_ref[pl.ds(b, 1), :]).astype(BF16).astype(F32)
        for g in range(groups):
            got = take(share[g * lines : (g + 1) * lines, :], lanes)
            vals = jnp.where((block == b) & (part == g), got, vals)
        return vals

    vals = lax.fori_loop(0, blocks, one, jnp.zeros((lines, size), F32), unroll=2)
    vals_ref[...] = vals.astype(BF16)


def pull_kernel(last, *refs):
    if last:
        src_ref, slot_ref, fetched_ref, spam_ref, tiles_ref, out_ref, acc = refs
    else:
        (src_ref, slot_ref, block_ref, lists_ref, vals_ref, rank_ref, spam_ref, shield_ref, weight_ref,
         tiles_ref, out_ref, acc, fetched_ref, codes, bounds, sem) = refs
    step = pl.program_id(0)
    per_step = tiles_ref.shape[0]
    size = acc.shape[2]

    @pl.when(step == 0)
    def _():
        acc[...] = jnp.zeros_like(acc)
        if not last:
            blocks = acc.shape[0]
            codes[...] = lists_ref[:, 0, :].astype(jnp.int32) // (blocks * size)
            copy = pltpu.make_async_copy(codes, bounds, sem)
            copy.start()
            copy.wait()
            expand(
                block_ref.shape[0] // lists_ref.shape[0], block_ref, lists_ref, vals_ref, rank_ref,
                blocks, bounds, fetched_ref,
            )

    def some(g, _):
        products = []
        for k in range(GROUP):
            n = step * per_step + g * GROUP + k
            products.append(
                lax.dot_general(
                    fetched_ref[slot_ref[n]], tiles_ref[g * GROUP + k], (((1,), (1,)), ((), ())),
                    preferred_element_type=F32,
                )
            )
        for k in range(GROUP):
            acc[src_ref[step * per_step + g * GROUP + k]] += products[k]
        return 0

    lax.fori_loop(0, per_step // GROUP, some, 0)

    @pl.when(step == pl.num_programs(0) - 1)
    def _():
        def distrust(b):
            return F32(0.85) * acc[b] + F32(0.15) * spam_ref[b]

        if last:
            def one(b, _):
                out_ref[pl.ds(pl.multiple_of(b * size, size), size), :] = jnp.transpose(distrust(b))
                return 0

            lax.fori_loop(0, acc.shape[0], one, 0)
        else:
            shares(shield_ref, weight_ref, distrust, out_ref)


def start_kernel(columns, good_ref, spam_ref, count_ref, list_ref, tally):
    list_ref[...] = jnp.transpose(spam_ref[...].astype(F32)).astype(jnp.int32)
    count_seeds(columns, good_ref, tally)
    spread_seeds(good_ref.shape[1], tally, count_ref)


def body(columns, tiles, tile_src, tile_slot, slot_block, out_degree, good_seeds, spam_cores):
    tile_count, size, _ = tiles.shape
    here = lambda x: pltpu.with_memory_space_constraint(x, pltpu.HBM)
    hosts = out_degree.shape[0]
    blocks = hosts // size
    seeds = good_seeds.shape[0]
    slots = slot_block.shape[0]
    peers = lax.axis_size(AXES)
    cap = slots // peers
    tail = -(-4 * cap // 16) * 16
    steps = 8
    shape = jax.ShapeDtypeStruct
    vector = (blocks, seeds, size)
    degree = out_degree.reshape(blocks, 1, size)

    rows = peers // columns
    part = seeds // HALVES
    count = spam_cores.shape[1]
    groups = seeds // count
    lines = seeds // groups
    good, spam_list = pl.pallas_call(
        functools.partial(start_kernel, columns),
        out_shape=(shape(vector, F32), shape(spam_cores.shape, jnp.int32)),
        in_specs=[VM, VM],
        out_specs=(VM, VM),
        scratch_shapes=[pltpu.VMEM((seeds, blocks, size), F32)],
        compiler_params=PLAIN,
        cost_estimate=pl.CostEstimate(
            flops=2 * seeds * good_seeds.size * (blocks + size), transcendentals=0,
            bytes_accessed=24 << 20,
        ),
    )(here(good_seeds), here(spam_cores.T))

    tile_spec = pl.BlockSpec((tile_count // steps, size, size), lambda i: (i, 0, 0))
    words = shape((peers, cap * size + tail, size), jnp.int16)
    outgoing = pl.pallas_call(
        functools.partial(push_kernel, True, cap, part),
        grid=(steps,),
        out_shape=words,
        in_specs=[SM, SM, SM, VM, VM, tile_spec],
        out_specs=VM,
        scratch_shapes=[
            pltpu.VMEM((slots, seeds + 16, size), F32),
            pltpu.VMEM((blocks, seeds + 16, size), BF16),
        ],
        compiler_params=PLAIN,
    )(here(tile_src), here(tile_slot), here(slot_block), good, here(degree), here(tiles))

    dma = pltpu.SemaphoreType.DMA
    spread_sems = [
        dma((2, columns)), dma((columns,)), dma((rows, columns)), dma((rows, columns)),
        dma((rows, columns)), dma((rows, columns)),
    ]

    def reduce(first, words_in, *rest):
        long = blocks * part + blocks * (4 if first else 1)
        outs = (
            shape(vector, F32), shape((blocks, size), F32), shape(vector, F32),
            shape((rows, 1, slots), jnp.int32), shape((lines, size), jnp.int16),
            shape((peers, lines, size), jnp.int16),
        )
        if not first:
            outs = (shape(vector, F32), shape((peers, seeds, size), jnp.int32))
        return pl.pallas_call(
            functools.partial(reduce_kernel, first, rows, columns, cap),
            out_shape=outs,
            in_specs=[ANY, VM, VM, VM] if first else [ANY, VM],
            out_specs=(VM,) * len(outs),
            scratch_shapes=[
                pltpu.VMEM((columns, rows, cap * size + tail, size), jnp.int16),
                pltpu.VMEM((rows * cap, blocks, size), F32),
                pltpu.VMEM((blocks, part, size), F32),
                pltpu.VMEM((blocks, size), F32),
                pltpu.VMEM((columns - 1, HALVES, long, size), jnp.int16),
                pltpu.VMEM((2, columns, HALVES, long, size), jnp.int16),
                dma((columns,)),
                dma((columns, HALVES, rows)),
                dma((columns, HALVES, rows)),
                dma((columns - 1, HALVES)),
                dma((2, columns, HALVES)),
                *([dma((rows,)), dma((rows,)), pltpu.VMEM((seeds, blocks, size), F32), *spread_sems] if first else []),
            ],
            compiler_params=pltpu.CompilerParams(
                collective_id=1 if first else 2, has_side_effects=True,
                vmem_limit_bytes=LIMIT,
            ),
        )(words_in, *rest)

    inflow, weight, spam, want, keys, lists = reduce(
        True, outgoing, spam_list, slot_block.reshape(1, slots), spam_cores.T
    )
    outgoing = pl.pallas_call(
        functools.partial(push_kernel, False, cap, part),
        grid=(steps,),
        out_shape=words,
        in_specs=[SM, SM, SM, VM, VM, VM, tile_spec],
        out_specs=VM,
        scratch_shapes=[
            pltpu.VMEM((slots, seeds, size), F32),
            pltpu.VMEM(vector, BF16),
        ],
        compiler_params=PLAIN,
    )(tile_src, tile_slot, slot_block, inflow, good, degree, tiles)
    inflow, ranks = reduce(False, outgoing, lists)
    fetch = pl.pallas_call(
        functools.partial(fetch_kernel, rows, columns, cap),
        out_shape=shape((slots, seeds, size), BF16),
        in_specs=[SM, VM],
        out_specs=VM,
        scratch_shapes=[
            *[pltpu.VMEM(vector, BF16)] * (2 * columns - 2),
            pltpu.VMEM((rows, columns * cap, seeds, size), BF16),
            pltpu.SemaphoreType.DMA((2 * columns - 2,)),
            pltpu.SemaphoreType.DMA((2 * columns - 2,)),
            pltpu.SemaphoreType.DMA((rows, columns)),
            pltpu.SemaphoreType.DMA((rows, columns)),
        ],
        compiler_params=pltpu.CompilerParams(collective_id=0, has_side_effects=True, vmem_limit_bytes=LIMIT),
    )
    trust, shield, vals = pl.pallas_call(
        trust_kernel,
        out_shape=(shape((hosts, seeds), F32), shape(vector, F32), shape((lines, size), BF16)),
        in_specs=[VM, VM, VM, VM, VM],
        out_specs=(VM, VM, VM),
        compiler_params=PLAIN,
    )(inflow, good, spam, weight, keys)
    vals = pl.pallas_call(
        functools.partial(value_kernel, rows, columns),
        out_shape=shape((peers, lines, size), BF16),
        in_specs=[VM],
        out_specs=VM,
        scratch_shapes=spread_sems,
        compiler_params=pltpu.CompilerParams(
            collective_id=3, has_side_effects=True, vmem_limit_bytes=LIMIT
        ),
    )(vals)
    share = pl.pallas_call(
        functools.partial(pull_kernel, False),
        grid=(steps,),
        out_shape=shape(vector, BF16),
        in_specs=[SM, SM, SM, VM, VM, VM, VM, VM, VM, tile_spec],
        out_specs=VM,
        scratch_shapes=[
            pltpu.VMEM(vector, F32),
            pltpu.VMEM((slots, seeds, size), BF16),
            pltpu.VMEM((peers, size), jnp.int32),
            pltpu.SMEM((peers, size), jnp.int32),
            pltpu.SemaphoreType.DMA,
        ],
        compiler_params=PLAIN,
    )(tile_src, tile_slot, slot_block, lists, vals, ranks, spam, shield, weight, tiles)
    fetched = fetch(want, share)
    distrust = pl.pallas_call(
        functools.partial(pull_kernel, True),
        grid=(steps,),
        out_shape=shape((hosts, seeds), F32),
        in_specs=[SM, SM, VM, VM, tile_spec],
        out_specs=VM,
        scratch_shapes=[pltpu.VMEM(vector, F32)],
        compiler_params=PLAIN,
    )(tile_src, tile_slot, fetched, spam, tiles)
    return trust, distrust


def solution(mesh):
    in_specs = (
        P(AXES, None, None),
        P(AXES),
        P(AXES),
        P(AXES),
        P(AXES),
        P(None, AXES),
        P(None, AXES),
    )
    out_specs = (P(AXES, None), P(AXES, None))
    return jax.shard_map(
        functools.partial(body, mesh.shape["col"]),
        mesh=mesh, in_specs=in_specs, out_specs=out_specs, check_vma=False,
    )
```

```python
import functools

import jax
import jax.numpy as jnp
from jax import lax
from jax.experimental import pallas as pl
from jax.experimental.pallas import tpu as pltpu
from jax.sharding import PartitionSpec as P

AXES = ("row", "col")
VM = pl.BlockSpec(memory_space=pltpu.VMEM)
SM = pl.BlockSpec(memory_space=pltpu.SMEM)
LIMIT = 28 << 20
ANY = pl.BlockSpec(memory_space=pl.ANY)
F32 = jnp.float32
BF16 = jnp.bfloat16
PLAIN = pltpu.CompilerParams(vmem_limit_bytes=LIMIT)
WORD = 15
GROUP = 16
HALVES = 4
LAYERS = 6
MORE = 2
MESH = pl.DeviceIdType.MESH


def count_seeds(columns, source, tally, step=0, pieces=1):
    seeds, blocks, size = tally.shape
    hosts = blocks * size
    base = (lax.axis_index("row") * columns + lax.axis_index("col")) * hosts
    count = source.shape[1]
    block_iota = lax.broadcasted_iota(jnp.int32, (blocks, count), 0) * size
    lane_iota = lax.broadcasted_iota(jnp.int32, (size, count), 0)

    def one(s, _):
        local = source[pl.ds(s, 1), :] - base
        shifted = local - block_iota
        inside = jnp.where((shifted >= 0) & (shifted < size), F32(1), F32(0)).astype(BF16)
        start = jnp.max(jnp.where(local >= block_iota, block_iota, 0), axis=0, keepdims=True)
        lane = jnp.where(lane_iota == local - start, F32(1), F32(0)).astype(BF16)
        tally[s] = lax.dot_general(
            inside, lane, (((1,), (1,)), ((), ())), preferred_element_type=F32
        )
        return 0

    share = seeds // pieces
    lax.fori_loop(step * share, (step + 1) * share, one, 0, unroll=16)


def spread_seeds(count, tally, target):
    blocks, _, size = target.shape
    factor = F32(blocks * size / count)
    for b in range(blocks):
        target[b] = tally[:, b, :] * factor


def exponent_of(peak):
    return jnp.floor(jnp.log2(jnp.maximum(peak, F32(2.0**-100)))) + F32(1)


def to_words(value):
    return jnp.clip(jnp.floor(value + F32(0.5)), F32(-32767), F32(32767))


def pack(first, cap, part, bits, acc, block_ref, out_ref):
    peers = out_ref.shape[0]
    size = acc.shape[2]
    halves = size // part
    tail = out_ref.shape[1] - cap * size

    def one(p, _):
        exps, cols = [], []
        for c in range(cap):
            n = p * cap + c
            value = acc[n, :size, :]
            e = exponent_of(jnp.max(jnp.abs(value), axis=0, keepdims=True))
            words = to_words(value * jnp.exp2(WORD - e)).astype(jnp.int32).astype(jnp.int16)
            for h in range(halves):
                at = (h * cap + c) * part + (tail if h else 0)
                out_ref[p, at : at + part, :] = words[h * part : (h + 1) * part, :]
            exps.append(e * F32(2**bits) + block_ref[n].astype(F32))
            if first:
                col = acc[n, size : size + 8, :][:1, :]
                f = exponent_of(jnp.abs(col))
                scaled = col * jnp.exp2(WORD - f)
                high = to_words(scaled)
                cols += [f, high, to_words((scaled - high) * F32(2.0**WORD))]
        rows = exps + cols
        if tail > len(rows):
            rows.append(jnp.zeros((tail - len(rows), size), F32))
        at = cap * part
        out_ref[p, at : at + tail, :] = jnp.concatenate(rows, axis=0).astype(jnp.int32).astype(jnp.int16)
        return 0

    lax.fori_loop(0, peers, one, 0)


def push_kernel(first, cap, part, *refs):
    if first:
        src_ref, slot_ref, block_ref, good_ref, degree_ref, tiles_ref, out_ref, acc, scaled = refs
    else:
        src_ref, slot_ref, block_ref, inflow, good_ref, degree_ref, tiles_ref, out_ref, acc, scaled = refs
    step = pl.program_id(0)
    blocks, seeds, size = good_ref.shape
    per_step = tiles_ref.shape[0]

    @pl.when(step == 0)
    def _():
        acc[...] = jnp.zeros_like(acc)
        def one(b, _):
            degree = degree_ref[b].astype(F32)
            trust = good_ref[b]
            if not first:
                trust = F32(0.85) * inflow[b] + F32(0.15) * trust
            scaled[b, :seeds, :] = (trust / degree).astype(BF16)
            if first:
                scaled[b, seeds:, :] = jnp.ones((scaled.shape[1] - seeds, size), BF16)
            return 0

        lax.fori_loop(0, blocks, one, 0)

    def some(g, _):
        products = []
        for k in range(GROUP):
            n = step * per_step + g * GROUP + k
            products.append(
                jnp.dot(scaled[src_ref[n]], tiles_ref[g * GROUP + k], preferred_element_type=F32)
            )
        for k in range(GROUP):
            acc[slot_ref[step * per_step + g * GROUP + k]] += products[k]
        return 0

    lax.fori_loop(0, per_step // GROUP, some, 0)

    @pl.when(step == pl.num_programs(0) - 1)
    def _():
        pack(first, cap, part, blocks.bit_length() - 1, acc, block_ref, out_ref)


def shares(shield_ref, weight_ref, start_of, share_ref):
    def one(b, _):
        weight = weight_ref[pl.ds(b, 1), :]
        share_ref[b] = (shield_ref[b] * start_of(b) / weight).astype(BF16)
        return 0

    lax.fori_loop(0, share_ref.shape[0], one, 0)


def greet(devices):
    barrier = pltpu.get_barrier_semaphore()
    for device, there in devices:
        @pl.when(there)
        def _():
            pl.semaphore_signal(barrier, inc=1, device_id=device, device_id_type=MESH)
    pl.semaphore_wait(barrier, sum(jnp.where(there, 1, 0) for _, there in devices))


def fetch_kernel(rows, columns, cap, want_ref, share_ref, fetched_ref, *scratch):
    line = 2 * (columns - 1)
    held, (picked, line_send, line_recv, send, recv) = scratch[:line], scratch[line:]
    r, z = lax.axis_index("row"), lax.axis_index("col")
    others = [lax.rem(r + d, rows) for d in range(1, rows)]
    sides = (-1, 1)
    inside = {side: (z + side >= 0) & (z + side < columns) for side in sides}
    greet([((t, z), t >= 0) for t in others] + [((r, z + side), inside[side]) for side in sides])

    def place(side, d):
        return 2 * (d - 1) + (0 if side < 0 else 1)

    def pass_on(source, d, side):
        slot = place(-side, d)
        return pltpu.make_async_remote_copy(
            src_ref=source, dst_ref=held[slot],
            send_sem=line_send.at[slot], recv_sem=line_recv.at[slot],
            device_id=(r, z + side), device_id_type=MESH,
        )

    def serve(t, origin):
        return pltpu.make_async_remote_copy(
            src_ref=picked.at[t, pl.ds(origin * cap, cap)],
            dst_ref=fetched_ref.at[pl.ds((r * columns + origin) * cap, cap)],
            send_sem=send.at[t, origin], recv_sem=recv.at[r, origin],
            device_id=(t, z), device_id_type=MESH,
        )

    def spread(source, origin):
        before = None
        for t in others:
            for j in range(cap):
                picked[t, origin * cap + j] = source[want_ref[t, 0, (r * columns + origin) * cap + j]]
            if before is not None:
                serve(before, origin).start()
            before = t
        for j in range(cap):
            fetched_ref[(r * columns + origin) * cap + j] = source[want_ref[r, 0, (r * columns + origin) * cap + j]]
        serve(before, origin).start()

    for side in sides:
        @pl.when(inside[side])
        def _():
            pass_on(share_ref, 1, side).start()
    spread(share_ref, z)
    for d in range(1, columns):
        for side in sides:
            origin = z + side * d

            @pl.when((origin >= 0) & (origin < columns))
            def _():
                here = held[place(side, d)]
                pass_on(share_ref, d, -side).wait_recv()

                if d < columns - 1:
                    @pl.when(inside[-side])
                    def _():
                        pass_on(here, d + 1, -side).start()

                spread(here, origin)
    for origin in range(columns):
        for t in others:
            serve(t, origin).wait_send()
            pltpu.make_async_remote_copy(
                src_ref=picked.at[t, pl.ds(origin * cap, cap)],
                dst_ref=fetched_ref.at[pl.ds((t * columns + origin) * cap, cap)],
                send_sem=send.at[t, origin], recv_sem=recv.at[t, origin],
                device_id=(t, z), device_id_type=MESH,
            ).wait_recv()
    for d in range(columns - 1):
        for side in sides:
            origin = z - side * d

            @pl.when((origin >= 0) & (origin < columns) & inside[side])
            def _():
                pass_on(share_ref, d + 1, side).wait_send()


def take(table, index):
    return jnp.take_along_axis(table, index, axis=1, mode="promise_in_bounds")


def find_ranks(groups, blocks, keys):
    lines, size = keys.shape
    count = size // groups
    least = lax.broadcasted_iota(jnp.int32, (lines, size), 1) * blocks
    spots = [jnp.full((lines, size), count * g, jnp.int32) for g in range(groups)]
    step = count // 2
    while True:
        probes = [take(keys, spot + (max(step, 1) - 1)) for spot in spots]
        spots = [spot + jnp.where(probe < least, max(step, 1), 0) for spot, probe in zip(spots, probes)]
        if step == 0:
            return spots
        step //= 2


def ends_of(g, groups, spots):
    lines, size = spots.shape
    lane = lax.broadcasted_iota(jnp.int32, (lines, size), 1)
    after = pltpu.roll(spots, size - 1, 1)
    return jnp.where(lane == size - 1, (size // groups) * (g + 1), after)


def sort_hosts(columns, blocks, raw):
    count, seeds = raw.shape
    groups = seeds // count
    lines = seeds // groups
    base = (lax.axis_index("row") * columns + lax.axis_index("col")) * (blocks * seeds)
    local = (raw - base).astype(F32)
    stacked = jnp.concatenate(
        [local] + [pltpu.roll(local, seeds - g * lines, 1) for g in range(1, groups)], axis=0
    )
    hosts = jnp.transpose(stacked)[:lines, :].astype(jnp.int32)
    keys = ((hosts & (seeds - 1)) * blocks + hosts // seeds).astype(F32)
    lane = lax.broadcasted_iota(jnp.int32, keys.shape, 1)
    k = 2
    while k <= count:
        j = k // 2
        while j:
            other = take(keys, lane ^ j)
            rising = ((lane & k) == 0) | (k == count)
            lower = ((lane & j) == 0) == rising
            keys = jnp.where(lower, jnp.minimum(keys, other), jnp.maximum(keys, other))
            j //= 2
        k *= 2
    keys = keys.astype(jnp.int32)
    spots = find_ranks(groups, blocks, keys)
    most = functools.reduce(
        jnp.maximum, [ends_of(g, groups, spot) - spot for g, spot in enumerate(spots)]
    ).astype(F32)
    most = jnp.max(jnp.max(most, axis=1, keepdims=True), axis=0, keepdims=True).astype(jnp.int32)
    code = jnp.where(most > LAYERS, 1, 0) + jnp.where(most > LAYERS + MORE, 1, 0)
    return (keys + code * (blocks * seeds)).astype(jnp.int16)


class Spread:
    def __init__(self, rows, columns, own, out, sems):
        self.rows, self.columns, self.own, self.out = rows, columns, own, out
        self.line_send, self.line_recv, self.plane_send, self.plane_recv, self.pair_send, self.pair_recv = sems
        r, z = lax.axis_index("row"), lax.axis_index("col")
        self.r, self.z = r, z
        self.twin = r + 1 - 2 * lax.rem(r, 2)
        self.mates = [lax.rem(r + d, rows) for d in range(2, rows, 2)]
        self.others = [self.twin] + [lax.rem(self.twin + d, rows) for d in range(2, rows, 2)]
        self.peers = [lax.rem(z + d, columns) for d in range(1, columns)]

    def send(self, source, row, origin, sends, recvs, to):
        return pltpu.make_async_remote_copy(
            src_ref=source, dst_ref=self.out.at[row * self.columns + origin],
            send_sem=sends, recv_sem=recvs, device_id=to, device_id_type=MESH,
        )

    def place(self, row, origin):
        return self.out.at[row * self.columns + origin]

    def line(self, d, origin):
        return self.send(
            self.own, self.r, origin, self.line_send.at[d], self.line_recv.at[origin],
            (self.r, lax.rem(self.z + d, self.columns)),
        )

    def plane(self, source, t, row, origin):
        return self.send(
            source, row, origin, self.plane_send.at[t, origin], self.plane_recv.at[row, origin],
            (t, self.z),
        )

    def pair(self, source, row, origin):
        return self.send(
            source, row, origin, self.pair_send.at[row, origin], self.pair_recv.at[row, origin],
            (self.twin, self.z),
        )

    def across(self, source, origin):
        for t in self.mates:
            self.plane(source, t, self.r, origin).start()
        self.pair(source, self.r, origin).start()

    def begin(self):
        for d in range(1, self.columns):
            self.line(d, self.z).start()
        self.across(self.own, self.z)
        self.out[self.r * self.columns + self.z] = self.own[...]

    def hop(self, d):
        origin = lax.rem(self.z + d, self.columns)
        self.line(d, origin).wait_recv()
        self.across(self.place(self.r, origin), origin)

    def collect(self):
        for t in self.mates:
            for origin in range(self.columns):
                here = self.place(t, origin)
                self.plane(here, t, t, origin).wait_recv()
                self.pair(here, t, origin).start()

    def finish(self):
        for t in self.others:
            for origin in range(self.columns):
                self.pair(self.place(t, origin), t, origin).wait_recv()
        for d in range(1, self.columns):
            self.line(d, self.z).wait_send()
        for origin in range(self.columns):
            for t in self.mates:
                self.plane(self.own, t, self.r, origin).wait_send()
                self.pair(self.own, t, origin).wait_send()
            self.pair(self.own, self.r, origin).wait_send()


def value_kernel(rows, columns, own_ref, vals_ref, *sems):
    spread = Spread(rows, columns, own_ref, vals_ref, sems)
    greet(
        [((t, spread.z), t >= 0) for t in spread.mates + [spread.twin]]
        + [((spread.r, y), y >= 0) for y in spread.peers]
    )
    spread.begin()
    for d in range(1, columns):
        spread.hop(d)
    spread.collect()
    spread.finish()


def expand(cap, block_ref, lists_ref, vals_ref, rank_ref, blocks, bounds, fetched):
    peers, lines, size = lists_ref.shape
    groups = fetched.shape[1] // lines
    tall = 16

    def paint(q, low, high, fresh):
        tags = [
            F32(1) + (block_ref[q * cap + c] + 1).astype(F32) * F32(2.0**-14) for c in range(cap)
        ]

        def some(i, _):
            at = pl.multiple_of(i * tall, tall)
            block = lists_ref[q, pl.ds(at, tall), :].astype(jnp.int32) & (blocks - 1)
            value = vals_ref[q, pl.ds(at, tall), :].astype(F32)
            marked = value * (F32(1) + (block + 1).astype(F32) * F32(2.0**-14))
            for g in range(groups):
                row = pl.multiple_of(g * lines + at, tall)
                spots = rank_ref[q, pl.ds(row, tall), :]
                ends = ends_of(g, groups, spots)

                def layer(j, outs):
                    spot = spots + j
                    live = spot < ends
                    got = jnp.where(live, take(marked, jnp.minimum(spot, size - 1)), F32(0))
                    plain = got.astype(BF16).astype(F32)
                    return tuple(
                        jnp.where(live & (plain * tag == got), plain, out) for tag, out in zip(tags, outs)
                    )

                if fresh:
                    outs = (jnp.zeros((tall, size), F32),) * cap
                else:
                    outs = tuple(
                        fetched[q * cap + c, pl.ds(row, tall), :].astype(F32) for c in range(cap)
                    )
                if high - low > LAYERS:
                    outs = lax.fori_loop(low, high, layer, outs)
                else:
                    for j in range(low, high):
                        outs = layer(j, outs)
                for c in range(cap):
                    fetched[q * cap + c, pl.ds(row, tall), :] = outs[c].astype(BF16)
            return 0

        lax.fori_loop(0, lines // tall, some, 0, unroll=2 if fresh else 1)

    def one(q, _):
        paint(q, 0, LAYERS, True)
        code = bounds[q, 0]

        @pl.when(code > 0)
        def _():
            paint(q, LAYERS, LAYERS + MORE, False)

        @pl.when(code > 1)
        def _():
            paint(q, LAYERS + MORE, size // groups, False)

        return 0

    lax.fori_loop(0, peers, one, 0)


def order_of(z, columns):
    table = []
    for plane in range(columns):
        line = []
        for k in range(columns):
            ahead = [t for t in (columns - 1 - k,) if t > plane]
            back = [t for t in (k,) if t < plane]
            line += ahead + back if 2 * plane < columns else back + ahead
        table.append(line + [plane])
    picks = []
    for i in range(columns):
        pick = z * 0
        for plane in range(columns):
            pick = pick + jnp.where(z == plane, table[plane][i], 0)
        picks.append(pick)
    return picks


def reduce_kernel(first, rows, columns, cap, words_ref, *refs):
    if first:
        cores_ref, mine_ref, raw_ref, inflow_ref, weight_ref, spam_ref, want_ref, keys_ref, lists_ref, *refs = refs
    else:
        lists_ref, inflow_ref, rank_ref, *refs = refs
    landed, table, partial, exps, gains, packed, inbox, own, send, recv, chain_send, chain_recv, *refs = refs
    r, z = lax.axis_index("row"), lax.axis_index("col")
    blocks, part, size = partial.shape
    seeds = inflow_ref.shape[1]
    halves = seeds // part
    bits = blocks.bit_length() - 1
    tail_at = cap * part
    spans = []
    for h in range(halves):
        start = spans[-1][0] + spans[-1][1] if spans else 0
        spans.append((start, cap * part + (landed.shape[2] - cap * seeds if h == 0 else 0)))
    data = blocks * part
    longs = [data + blocks * (4 if first and h == 0 else 1) for h in range(halves)]
    others = [lax.rem(r + d, rows) for d in range(1, rows)]
    targets = order_of(z, columns)
    block_iota = lax.broadcasted_iota(jnp.int32, (blocks, size), 0)
    greet(
        [((t, z), t >= 0) for t in others]
        + (
            [((r, lax.rem(z + d, columns)), z >= 0) for d in range(1, columns)] if first
            else [((r, z - 1), z > 0), ((r, z + 1), z < columns - 1)]
        )
    )

    def across(i, h, t, origin):
        at = pl.ds(*spans[h])
        return pltpu.make_async_remote_copy(
            src_ref=words_ref.at[t * columns + targets[i], at], dst_ref=landed.at[i, origin, at],
            send_sem=send.at[i, h, t], recv_sem=recv.at[i, h, origin],
            device_id=(t, z), device_id_type=MESH,
        )

    def mine(i):
        return pltpu.make_async_copy(
            words_ref.at[r * columns + targets[i]], landed.at[i, r], own.at[i]
        )

    def chain(i, h, side):
        at = pl.ds(0, longs[h])
        return pltpu.make_async_remote_copy(
            src_ref=packed.at[min(i, columns - 2), h, at], dst_ref=inbox.at[side, targets[i], h, at],
            send_sem=chain_send.at[min(i, columns - 2), h], recv_sem=chain_recv.at[side, targets[i], h],
            device_id=(r, z + 1 - 2 * side), device_id_type=MESH,
        )

    def to_int16(value):
        return value.astype(jnp.int32).astype(jnp.int16)

    def to_float(value):
        return value.astype(jnp.int32).astype(F32)

    if first:
        known_send, known_recv, tally, *sems = refs
        spread = Spread(rows, columns, keys_ref, lists_ref, sems)

        def know(t, origin):
            return pltpu.make_async_remote_copy(
                src_ref=mine_ref, dst_ref=want_ref.at[origin],
                send_sem=known_send.at[t], recv_sem=known_recv.at[origin],
                device_id=(t, z), device_id_type=MESH,
            )

        for t in others:
            know(t, r).start()
        want_ref[r] = mine_ref[...]

    def launch(i):
        for h in range(halves):
            for t in others:
                across(i, h, t, r).start()
        mine(i).start()

    launch(0)
    launch(1)
    if first:
        keys_ref[...] = sort_hosts(columns, blocks, raw_ref[...])
        spread.begin()
    else:
        peers, lines, _ = lists_ref.shape
        groups = seeds // lines
        turns = (columns - 1) * halves - 1
        load = -(-peers // turns)

        def find(q, _):
            keys = lists_ref[q].astype(jnp.int32) & (blocks * size - 1)
            for g, spots in enumerate(find_ranks(groups, blocks, keys)):
                rank_ref[q, g * lines : (g + 1) * lines, :] = spots
            return 0

    pieces = min(8, (columns - 1) * halves)
    for i in range(columns):
        mine(i).wait()
        side = jnp.where(targets[i] > z, 0, 1)
        joined = jnp.where(targets[i] > z, z > 0, z < columns - 1)
        cols = jnp.zeros((blocks, size), F32)
        for h in range(halves):
            for t in others:
                across(i, h, t, t).wait_recv()
            if h == 0:
                def weigh(q, cols):
                    tail = landed[i, q, tail_at : spans[0][1], :].astype(jnp.int32)
                    for c in range(cap):
                        word = tail[c : c + 1, :]
                        hit = block_iota == (word & (blocks - 1))
                        scale = jnp.exp2((word >> bits).astype(F32) - WORD)
                        table[q * cap + c] = jnp.where(
                            hit, jnp.broadcast_to(scale, (blocks, size)), F32(0)
                        )
                        if first:
                            f, high, low = (
                                tail[cap + 3 * c + k : cap + 3 * c + k + 1, :].astype(F32) for k in range(3)
                            )
                            col = (high + low * F32(2.0**-WORD)) * jnp.exp2(f - WORD)
                            cols = cols + jnp.where(hit, jnp.broadcast_to(col, (blocks, size)), F32(0))
                    return cols

                cols = lax.fori_loop(0, rows, weigh, cols, unroll=4)

            first_row = spans[h][0]

            def strip(k, _):
                at = pl.multiple_of(k * 16, 16)

                def add(q, sums):
                    sums = list(sums)
                    for c in range(cap):
                        spot = pl.multiple_of(first_row + c * part + at, 16)
                        value = to_float(landed[i, q, pl.ds(spot, 16), :])
                        for b in range(blocks):
                            sums[b] = sums[b] + value * table[q * cap + c, b : b + 1, :]
                    return tuple(sums)

                sums = lax.fori_loop(0, rows, add, (jnp.zeros((16, size), F32),) * blocks)
                for b in range(blocks):
                    partial[b, pl.ds(at, 16), :] = sums[b]
                return 0

            lax.fori_loop(0, part // 16, strip, 0)

            def join(way):
                chain(i, h, way).wait_recv()
                exps[...] = jnp.exp2(to_float(inbox[way, targets[i], h, data : data + blocks, :]) - WORD)

                def one(b, _):
                    got = to_float(inbox[way, targets[i], h, pl.ds(pl.multiple_of(b * part, part), part), :])
                    partial[b] += got * exps[pl.ds(b, 1), :]
                    return 0

                lax.fori_loop(0, blocks, one, 0, unroll=4)

            def join_cols(way):
                f, high, low = (
                    to_float(inbox[way, targets[i], h, data + (k + 1) * blocks : data + (k + 2) * blocks, :])
                    for k in range(3)
                )
                colsum[...] += (high + low * F32(2.0**-WORD)) * jnp.exp2(f - WORD)

            if first and h == 0:
                colsum = weight_ref
                colsum[...] = cols
            if i < columns - 1:
                @pl.when(joined)
                def _():
                    join(side)
                    if first and h == 0:
                        join_cols(side)

                def peak(b, _):
                    exps[pl.ds(b, 1), :] = jnp.max(jnp.abs(partial[b]), axis=0, keepdims=True)
                    return 0

                def squeeze(b, _):
                    packed[i, h, pl.ds(pl.multiple_of(b * part, part), part), :] = to_int16(
                        to_words(partial[b] * gains[pl.ds(b, 1), :])
                    )
                    return 0

                lax.fori_loop(0, blocks, peak, 0, unroll=8)
                exps[...] = exponent_of(exps[...])
                gains[...] = jnp.exp2(WORD - exps[...])
                lax.fori_loop(0, blocks, squeeze, 0, unroll=8)
                packed[i, h, data : data + blocks, :] = to_int16(exps[...])
                if first and h == 0:
                    col = colsum[...]
                    f = exponent_of(jnp.abs(col))
                    scaled = col * jnp.exp2(WORD - f)
                    high = to_words(scaled)
                    for k, row in enumerate((f, high, to_words((scaled - high) * F32(2.0**WORD)))):
                        packed[i, h, data + (k + 1) * blocks : data + (k + 2) * blocks, :] = to_int16(row)
                chain(i, h, side).start()
            else:
                for way, there in ((0, z > 0), (1, z < columns - 1)):
                    @pl.when(there)
                    def _():
                        join(way)
                        if first and h == 0:
                            join_cols(way)

                def finish(b, _):
                    inflow_ref[b, h * part : (h + 1) * part, :] = partial[b]
                    return 0

                lax.fori_loop(0, blocks, finish, 0, unroll=4)
                if first and h == 0:
                    colsum[...] += F32(1)
            step = i * halves + h
            if first and step < columns - 1:
                spread.hop(step + 1)
            if h == min(columns, halves) - 1 and i + 2 < columns:
                launch(i + 2)
            if first and step == (columns - 2) * halves:
                spread.collect()
            if not first and 0 <= step - halves < turns:
                begin, end = (min(peers, k * load) for k in (step - halves, step - halves + 1))
                lax.fori_loop(begin, end, find, 0, unroll=3 if (end - begin) % 3 == 0 else 2)
            if first and 0 <= step - halves < pieces:
                count_seeds(columns, cores_ref, tally, step - halves, pieces)
            if first and step == halves + pieces:
                spread_seeds(cores_ref.shape[1], tally, spam_ref)

    if first:
        for t in others:
            know(t, r).wait_send()
            know(t, t).wait_recv()
        spread.finish()
    for i in range(columns):
        for h in range(halves):
            for t in others:
                across(i, h, t, r).wait_send()
            if i < columns - 1:
                chain(i, h, jnp.where(targets[i] > z, 0, 1)).wait_send()


def trust_kernel(inflow, good_ref, spam_ref, weight_ref, keys_ref, trust_ref, shield_ref, vals_ref):
    blocks, seeds, size = inflow.shape
    lines = keys_ref.shape[0]
    groups = seeds // lines
    keys = keys_ref[...].astype(jnp.int32) & (blocks * size - 1)
    lanes = keys // blocks
    block = keys & (blocks - 1)
    part = lax.broadcasted_iota(jnp.int32, (lines, size), 1) // (size // groups)

    def one(b, vals):
        trust = F32(0.85) * inflow[b] + F32(0.15) * good_ref[b]
        trust_ref[pl.ds(pl.multiple_of(b * size, size), size), :] = jnp.transpose(trust)
        shield = F32(1) / (F32(1) + trust)
        shield_ref[b] = shield
        share = (shield * spam_ref[b] / weight_ref[pl.ds(b, 1), :]).astype(BF16).astype(F32)
        for g in range(groups):
            got = take(share[g * lines : (g + 1) * lines, :], lanes)
            vals = jnp.where((block == b) & (part == g), got, vals)
        return vals

    vals = lax.fori_loop(0, blocks, one, jnp.zeros((lines, size), F32), unroll=2)
    vals_ref[...] = vals.astype(BF16)


def pull_kernel(last, *refs):
    if last:
        src_ref, slot_ref, fetched_ref, spam_ref, tiles_ref, out_ref, acc = refs
    else:
        (src_ref, slot_ref, block_ref, lists_ref, vals_ref, rank_ref, spam_ref, shield_ref, weight_ref,
         tiles_ref, out_ref, acc, fetched_ref, codes, bounds, sem) = refs
    step = pl.program_id(0)
    per_step = tiles_ref.shape[0]
    size = acc.shape[2]

    @pl.when(step == 0)
    def _():
        acc[...] = jnp.zeros_like(acc)
        if not last:
            blocks = acc.shape[0]
            codes[...] = lists_ref[:, 0, :].astype(jnp.int32) // (blocks * size)
            copy = pltpu.make_async_copy(codes, bounds, sem)
            copy.start()
            copy.wait()
            expand(
                block_ref.shape[0] // lists_ref.shape[0], block_ref, lists_ref, vals_ref, rank_ref,
                blocks, bounds, fetched_ref,
            )

    def some(g, _):
        products = []
        for k in range(GROUP):
            n = step * per_step + g * GROUP + k
            products.append(
                lax.dot_general(
                    fetched_ref[slot_ref[n]], tiles_ref[g * GROUP + k], (((1,), (1,)), ((), ())),
                    preferred_element_type=F32,
                )
            )
        for k in range(GROUP):
            acc[src_ref[step * per_step + g * GROUP + k]] += products[k]
        return 0

    lax.fori_loop(0, per_step // GROUP, some, 0)

    @pl.when(step == pl.num_programs(0) - 1)
    def _():
        def distrust(b):
            return F32(0.85) * acc[b] + F32(0.15) * spam_ref[b]

        if last:
            def one(b, _):
                out_ref[pl.ds(pl.multiple_of(b * size, size), size), :] = jnp.transpose(distrust(b))
                return 0

            lax.fori_loop(0, acc.shape[0], one, 0)
        else:
            shares(shield_ref, weight_ref, distrust, out_ref)


def start_kernel(columns, good_ref, spam_ref, count_ref, list_ref, tally):
    list_ref[...] = jnp.transpose(spam_ref[...].astype(F32)).astype(jnp.int32)
    count_seeds(columns, good_ref, tally)
    spread_seeds(good_ref.shape[1], tally, count_ref)


def body(columns, tiles, tile_src, tile_slot, slot_block, out_degree, good_seeds, spam_cores):
    tile_count, size, _ = tiles.shape
    here = lambda x: pltpu.with_memory_space_constraint(x, pltpu.HBM)
    hosts = out_degree.shape[0]
    blocks = hosts // size
    seeds = good_seeds.shape[0]
    slots = slot_block.shape[0]
    peers = lax.axis_size(AXES)
    cap = slots // peers
    tail = -(-4 * cap // 16) * 16
    steps = 8
    shape = jax.ShapeDtypeStruct
    vector = (blocks, seeds, size)
    degree = out_degree.reshape(blocks, 1, size)

    rows = peers // columns
    part = seeds // HALVES
    count = spam_cores.shape[1]
    groups = seeds // count
    lines = seeds // groups
    good, spam_list = pl.pallas_call(
        functools.partial(start_kernel, columns),
        out_shape=(shape(vector, F32), shape(spam_cores.shape, jnp.int32)),
        in_specs=[VM, VM],
        out_specs=(VM, VM),
        scratch_shapes=[pltpu.VMEM((seeds, blocks, size), F32)],
        compiler_params=PLAIN,
        cost_estimate=pl.CostEstimate(
            flops=2 * seeds * good_seeds.size * (blocks + size), transcendentals=0,
            bytes_accessed=24 << 20,
        ),
    )(here(good_seeds), here(spam_cores.T))

    tile_spec = pl.BlockSpec((tile_count // steps, size, size), lambda i: (i, 0, 0))
    words = shape((peers, cap * size + tail, size), jnp.int16)
    outgoing = pl.pallas_call(
        functools.partial(push_kernel, True, cap, part),
        grid=(steps,),
        out_shape=words,
        in_specs=[SM, SM, SM, VM, VM, tile_spec],
        out_specs=VM,
        scratch_shapes=[
            pltpu.VMEM((slots, seeds + 16, size), F32),
            pltpu.VMEM((blocks, seeds + 16, size), BF16),
        ],
        compiler_params=PLAIN,
    )(here(tile_src), here(tile_slot), here(slot_block), good, here(degree), here(tiles))

    dma = pltpu.SemaphoreType.DMA
    spread_sems = [
        dma((columns,)), dma((columns,)), dma((rows, columns)), dma((rows, columns)),
        dma((rows, columns)), dma((rows, columns)),
    ]

    def reduce(first, words_in, *rest):
        long = blocks * part + blocks * (4 if first else 1)
        outs = (
            shape(vector, F32), shape((blocks, size), F32), shape(vector, F32),
            shape((rows, 1, slots), jnp.int32), shape((lines, size), jnp.int16),
            shape((peers, lines, size), jnp.int16),
        )
        if not first:
            outs = (shape(vector, F32), shape((peers, seeds, size), jnp.int32))
        return pl.pallas_call(
            functools.partial(reduce_kernel, first, rows, columns, cap),
            out_shape=outs,
            in_specs=[ANY, VM, VM, VM] if first else [ANY, VM],
            out_specs=(VM,) * len(outs),
            scratch_shapes=[
                pltpu.VMEM((columns, rows, cap * size + tail, size), jnp.int16),
                pltpu.VMEM((rows * cap, blocks, size), F32),
                pltpu.VMEM((blocks, part, size), F32),
                pltpu.VMEM((blocks, size), F32),
                pltpu.VMEM((blocks, size), F32),
                pltpu.VMEM((columns - 1, HALVES, long, size), jnp.int16),
                pltpu.VMEM((2, columns, HALVES, long, size), jnp.int16),
                dma((columns,)),
                dma((columns, HALVES, rows)),
                dma((columns, HALVES, rows)),
                dma((columns - 1, HALVES)),
                dma((2, columns, HALVES)),
                *([dma((rows,)), dma((rows,)), pltpu.VMEM((seeds, blocks, size), F32), *spread_sems] if first else []),
            ],
            compiler_params=pltpu.CompilerParams(
                collective_id=1 if first else 2, has_side_effects=True,
                vmem_limit_bytes=LIMIT,
            ),
        )(words_in, *rest)

    inflow, weight, spam, want, keys, lists = reduce(
        True, outgoing, spam_list, slot_block.reshape(1, slots), spam_cores.T
    )
    outgoing = pl.pallas_call(
        functools.partial(push_kernel, False, cap, part),
        grid=(steps,),
        out_shape=words,
        in_specs=[SM, SM, SM, VM, VM, VM, tile_spec],
        out_specs=VM,
        scratch_shapes=[
            pltpu.VMEM((slots, seeds, size), F32),
            pltpu.VMEM(vector, BF16),
        ],
        compiler_params=PLAIN,
    )(tile_src, tile_slot, slot_block, inflow, good, degree, tiles)
    inflow, ranks = reduce(False, outgoing, lists)
    fetch = pl.pallas_call(
        functools.partial(fetch_kernel, rows, columns, cap),
        out_shape=shape((slots, seeds, size), BF16),
        in_specs=[SM, VM],
        out_specs=VM,
        scratch_shapes=[
            *[pltpu.VMEM(vector, BF16)] * (2 * columns - 2),
            pltpu.VMEM((rows, columns * cap, seeds, size), BF16),
            pltpu.SemaphoreType.DMA((2 * columns - 2,)),
            pltpu.SemaphoreType.DMA((2 * columns - 2,)),
            pltpu.SemaphoreType.DMA((rows, columns)),
            pltpu.SemaphoreType.DMA((rows, columns)),
        ],
        compiler_params=pltpu.CompilerParams(collective_id=0, has_side_effects=True, vmem_limit_bytes=LIMIT),
    )
    trust, shield, vals = pl.pallas_call(
        trust_kernel,
        out_shape=(shape((hosts, seeds), F32), shape(vector, F32), shape((lines, size), BF16)),
        in_specs=[VM, VM, VM, VM, VM],
        out_specs=(VM, VM, VM),
        compiler_params=PLAIN,
    )(inflow, good, spam, weight, keys)
    vals = pl.pallas_call(
        functools.partial(value_kernel, rows, columns),
        out_shape=shape((peers, lines, size), BF16),
        in_specs=[VM],
        out_specs=VM,
        scratch_shapes=spread_sems,
        compiler_params=pltpu.CompilerParams(
            collective_id=3, has_side_effects=True, vmem_limit_bytes=LIMIT
        ),
    )(vals)
    share = pl.pallas_call(
        functools.partial(pull_kernel, False),
        grid=(steps,),
        out_shape=shape(vector, BF16),
        in_specs=[SM, SM, SM, VM, VM, VM, VM, VM, VM, tile_spec],
        out_specs=VM,
        scratch_shapes=[
            pltpu.VMEM(vector, F32),
            pltpu.VMEM((slots, seeds, size), BF16),
            pltpu.VMEM((peers, size), jnp.int32),
            pltpu.SMEM((peers, size), jnp.int32),
            pltpu.SemaphoreType.DMA,
        ],
        compiler_params=PLAIN,
    )(tile_src, tile_slot, slot_block, lists, vals, ranks, spam, shield, weight, tiles)
    fetched = fetch(want, share)
    distrust = pl.pallas_call(
        functools.partial(pull_kernel, True),
        grid=(steps,),
        out_shape=shape((hosts, seeds), F32),
        in_specs=[SM, SM, VM, VM, tile_spec],
        out_specs=VM,
        scratch_shapes=[pltpu.VMEM(vector, F32)],
        compiler_params=PLAIN,
    )(tile_src, tile_slot, fetched, spam, tiles)
    return trust, distrust


def solution(mesh):
    in_specs = (
        P(AXES, None, None),
        P(AXES),
        P(AXES),
        P(AXES),
        P(AXES),
        P(None, AXES),
        P(None, AXES),
    )
    out_specs = (P(AXES, None), P(AXES, None))
    return jax.shard_map(
        functools.partial(body, mesh.shape["col"]),
        mesh=mesh, in_specs=in_specs, out_specs=out_specs, check_vma=False,
    )
```

```python
import functools

import jax
import jax.numpy as jnp
from jax import lax
from jax.experimental import pallas as pl
from jax.experimental.pallas import tpu as pltpu
from jax.sharding import PartitionSpec as P

AXES = ("row", "col")
VM = pl.BlockSpec(memory_space=pltpu.VMEM)
SM = pl.BlockSpec(memory_space=pltpu.SMEM)
LIMIT = 28 << 20
ANY = pl.BlockSpec(memory_space=pl.ANY)
F32 = jnp.float32
BF16 = jnp.bfloat16
PLAIN = pltpu.CompilerParams(vmem_limit_bytes=LIMIT)
WORD = 15
GROUP = 64
HALVES = 4
LAYERS = 6
MORE = 2
MESH = pl.DeviceIdType.MESH


def count_seeds(columns, source, tally, step=0, pieces=1):
    seeds, blocks, size = tally.shape
    hosts = blocks * size
    base = (lax.axis_index("row") * columns + lax.axis_index("col")) * hosts
    count = source.shape[1]
    block_iota = lax.broadcasted_iota(jnp.int32, (blocks, count), 0) * size
    lane_iota = lax.broadcasted_iota(jnp.int32, (size, count), 0)

    def one(s, _):
        local = source[pl.ds(s, 1), :] - base
        shifted = local - block_iota
        inside = jnp.where((shifted >= 0) & (shifted < size), F32(1), F32(0)).astype(BF16)
        start = jnp.max(jnp.where(local >= block_iota, block_iota, 0), axis=0, keepdims=True)
        lane = jnp.where(lane_iota == local - start, F32(1), F32(0)).astype(BF16)
        tally[s] = lax.dot_general(
            inside, lane, (((1,), (1,)), ((), ())), preferred_element_type=F32
        )
        return 0

    share = seeds // pieces
    lax.fori_loop(step * share, (step + 1) * share, one, 0, unroll=16)


def spread_seeds(count, tally, target):
    blocks, _, size = target.shape
    factor = F32(blocks * size / count)
    for b in range(blocks):
        target[b] = tally[:, b, :] * factor


def exponent_of(peak):
    return jnp.floor(jnp.log2(jnp.maximum(peak, F32(2.0**-100)))) + F32(1)


def to_words(value):
    return jnp.clip(jnp.floor(value + F32(0.5)), F32(-32767), F32(32767))


def pack(first, cap, part, bits, acc, block_ref, out_ref):
    peers = out_ref.shape[0]
    size = acc.shape[2]
    halves = size // part
    tail = out_ref.shape[1] - cap * size

    def one(p, _):
        exps, cols = [], []
        for c in range(cap):
            n = p * cap + c
            value = acc[n, :size, :]
            e = exponent_of(jnp.max(jnp.abs(value), axis=0, keepdims=True))
            words = to_words(value * jnp.exp2(WORD - e)).astype(jnp.int32).astype(jnp.int16)
            for h in range(halves):
                at = (h * cap + c) * part + (tail if h else 0)
                out_ref[p, at : at + part, :] = words[h * part : (h + 1) * part, :]
            exps.append(e * F32(2**bits) + block_ref[n].astype(F32))
            if first:
                col = acc[n, size : size + 8, :][:1, :]
                f = exponent_of(jnp.abs(col))
                scaled = col * jnp.exp2(WORD - f)
                high = to_words(scaled)
                cols += [f, high, to_words((scaled - high) * F32(2.0**WORD))]
        rows = exps + cols
        if tail > len(rows):
            rows.append(jnp.zeros((tail - len(rows), size), F32))
        at = cap * part
        out_ref[p, at : at + tail, :] = jnp.concatenate(rows, axis=0).astype(jnp.int32).astype(jnp.int16)
        return 0

    lax.fori_loop(0, peers, one, 0, unroll=2)


def push_kernel(first, cap, part, *refs):
    if first:
        src_ref, slot_ref, block_ref, good_ref, degree_ref, tiles_ref, out_ref, acc, scaled = refs
    else:
        src_ref, slot_ref, block_ref, inflow, good_ref, degree_ref, tiles_ref, out_ref, acc, scaled = refs
    step = pl.program_id(0)
    blocks, seeds, size = good_ref.shape
    per_step = tiles_ref.shape[0]

    @pl.when(step == 0)
    def _():
        acc[...] = jnp.zeros_like(acc)
        def one(b, _):
            degree = degree_ref[b].astype(F32)
            trust = good_ref[b]
            if not first:
                trust = F32(0.85) * inflow[b] + F32(0.15) * trust
            scaled[b, :seeds, :] = (trust / degree).astype(BF16)
            if first:
                scaled[b, seeds:, :] = jnp.ones((scaled.shape[1] - seeds, size), BF16)
            return 0

        lax.fori_loop(0, blocks, one, 0)

    def some(g, _):
        products = []
        for k in range(GROUP):
            n = step * per_step + g * GROUP + k
            products.append(
                jnp.dot(scaled[src_ref[n]], tiles_ref[g * GROUP + k], preferred_element_type=F32)
            )
        for k in range(GROUP):
            acc[slot_ref[step * per_step + g * GROUP + k]] += products[k]
        return 0

    lax.fori_loop(0, per_step // GROUP, some, 0)

    @pl.when(step == pl.num_programs(0) - 1)
    def _():
        pack(first, cap, part, blocks.bit_length() - 1, acc, block_ref, out_ref)


def shares(shield_ref, weight_ref, start_of, share_ref):
    def one(b, _):
        weight = weight_ref[pl.ds(b, 1), :]
        share_ref[b] = jnp.transpose(shield_ref[b] * start_of(b) / weight).astype(BF16)
        return 0

    lax.fori_loop(0, share_ref.shape[0], one, 0, unroll=2)


def greet(devices):
    barrier = pltpu.get_barrier_semaphore()
    for device, there in devices:
        @pl.when(there)
        def _():
            pl.semaphore_signal(barrier, inc=1, device_id=device, device_id_type=MESH)
    pl.semaphore_wait(barrier, sum(jnp.where(there, 1, 0) for _, there in devices))


def fetch_kernel(rows, columns, cap, want_ref, share_ref, fetched_ref, *scratch):
    line = 2 * (columns - 1)
    held, (picked, line_send, line_recv, send, recv) = scratch[:line], scratch[line:]
    r, z = lax.axis_index("row"), lax.axis_index("col")
    others = [lax.rem(r + d, rows) for d in range(1, rows)]
    sides = (-1, 1)
    inside = {side: (z + side >= 0) & (z + side < columns) for side in sides}
    greet([((t, z), t >= 0) for t in others] + [((r, z + side), inside[side]) for side in sides])

    def place(side, d):
        return 2 * (d - 1) + (0 if side < 0 else 1)

    def pass_on(source, d, side):
        slot = place(-side, d)
        return pltpu.make_async_remote_copy(
            src_ref=source, dst_ref=held[slot],
            send_sem=line_send.at[slot], recv_sem=line_recv.at[slot],
            device_id=(r, z + side), device_id_type=MESH,
        )

    def serve(t, origin):
        return pltpu.make_async_remote_copy(
            src_ref=picked.at[t, pl.ds(origin * cap, cap)],
            dst_ref=fetched_ref.at[pl.ds((r * columns + origin) * cap, cap)],
            send_sem=send.at[t, origin], recv_sem=recv.at[r, origin],
            device_id=(t, z), device_id_type=MESH,
        )

    def spread(source, origin):
        before = None
        for t in others:
            for j in range(cap):
                picked[t, origin * cap + j] = source[want_ref[t, 0, (r * columns + origin) * cap + j]]
            if before is not None:
                serve(before, origin).start()
            before = t
        for j in range(cap):
            fetched_ref[(r * columns + origin) * cap + j] = source[want_ref[r, 0, (r * columns + origin) * cap + j]]
        serve(before, origin).start()

    for side in sides:
        @pl.when(inside[side])
        def _():
            pass_on(share_ref, 1, side).start()
    spread(share_ref, z)
    for d in range(1, columns):
        for side in sides:
            origin = z + side * d

            @pl.when((origin >= 0) & (origin < columns))
            def _():
                here = held[place(side, d)]
                pass_on(share_ref, d, -side).wait_recv()

                if d < columns - 1:
                    @pl.when(inside[-side])
                    def _():
                        pass_on(here, d + 1, -side).start()

                spread(here, origin)
    for origin in range(columns):
        for t in others:
            serve(t, origin).wait_send()
            pltpu.make_async_remote_copy(
                src_ref=picked.at[t, pl.ds(origin * cap, cap)],
                dst_ref=fetched_ref.at[pl.ds((t * columns + origin) * cap, cap)],
                send_sem=send.at[t, origin], recv_sem=recv.at[t, origin],
                device_id=(t, z), device_id_type=MESH,
            ).wait_recv()
    for d in range(columns - 1):
        for side in sides:
            origin = z - side * d

            @pl.when((origin >= 0) & (origin < columns) & inside[side])
            def _():
                pass_on(share_ref, d + 1, side).wait_send()


def take(table, index):
    return jnp.take_along_axis(table, index, axis=1, mode="promise_in_bounds")


def find_ranks(groups, blocks, keys):
    lines, size = keys.shape
    count = size // groups
    least = lax.broadcasted_iota(jnp.int32, (lines, size), 1) * blocks
    spots = [jnp.full((lines, size), count * g, jnp.int32) for g in range(groups)]
    step = count // 2
    while True:
        probes = [take(keys, spot + (max(step, 1) - 1)) for spot in spots]
        spots = [spot + jnp.where(probe < least, max(step, 1), 0) for spot, probe in zip(spots, probes)]
        if step == 0:
            return spots
        step //= 2


def ends_of(g, groups, spots):
    lines, size = spots.shape
    lane = lax.broadcasted_iota(jnp.int32, (lines, size), 1)
    after = pltpu.roll(spots, size - 1, 1)
    return jnp.where(lane == size - 1, (size // groups) * (g + 1), after)


def sort_hosts(columns, blocks, raw):
    count, seeds = raw.shape
    groups = seeds // count
    lines = seeds // groups
    base = (lax.axis_index("row") * columns + lax.axis_index("col")) * (blocks * seeds)
    local = (raw - base).astype(F32)
    stacked = jnp.concatenate(
        [local] + [pltpu.roll(local, seeds - g * lines, 1) for g in range(1, groups)], axis=0
    )
    hosts = jnp.transpose(stacked)[:lines, :].astype(jnp.int32)
    keys = ((hosts & (seeds - 1)) * blocks + hosts // seeds).astype(F32)
    lane = lax.broadcasted_iota(jnp.int32, keys.shape, 1)
    k = 2
    while k <= count:
        j = k // 2
        while j:
            other = take(keys, lane ^ j)
            rising = ((lane & k) == 0) | (k == count)
            lower = ((lane & j) == 0) == rising
            keys = jnp.where(lower, jnp.minimum(keys, other), jnp.maximum(keys, other))
            j //= 2
        k *= 2
    keys = keys.astype(jnp.int32)
    spots = find_ranks(groups, blocks, keys)
    most = functools.reduce(
        jnp.maximum, [ends_of(g, groups, spot) - spot for g, spot in enumerate(spots)]
    ).astype(F32)
    most = jnp.max(jnp.max(most, axis=1, keepdims=True), axis=0, keepdims=True).astype(jnp.int32)
    code = jnp.where(most > LAYERS, 1, 0) + jnp.where(most > LAYERS + MORE, 1, 0)
    return (keys + code * (blocks * seeds)).astype(jnp.int16)


class Spread:
    def __init__(self, rows, columns, own, out, sems):
        self.rows, self.columns, self.own, self.out = rows, columns, own, out
        self.line_send, self.line_recv, self.plane_send, self.plane_recv, self.pair_send, self.pair_recv = sems
        r, z = lax.axis_index("row"), lax.axis_index("col")
        self.r, self.z = r, z
        self.twin = r + 1 - 2 * lax.rem(r, 2)
        self.mates = [lax.rem(r + d, rows) for d in range(2, rows, 2)]
        self.others = [self.twin] + [lax.rem(self.twin + d, rows) for d in range(2, rows, 2)]
        self.peers = [lax.rem(z + d, columns) for d in range(1, columns)]

    def send(self, source, row, origin, sends, recvs, to):
        return pltpu.make_async_remote_copy(
            src_ref=source, dst_ref=self.out.at[row * self.columns + origin],
            send_sem=sends, recv_sem=recvs, device_id=to, device_id_type=MESH,
        )

    def place(self, row, origin):
        return self.out.at[row * self.columns + origin]

    def line(self, d, origin):
        return self.send(
            self.own, self.r, origin, self.line_send.at[d], self.line_recv.at[origin],
            (self.r, lax.rem(self.z + d, self.columns)),
        )

    def plane(self, source, t, row, origin):
        return self.send(
            source, row, origin, self.plane_send.at[t, origin], self.plane_recv.at[row, origin],
            (t, self.z),
        )

    def pair(self, source, row, origin):
        return self.send(
            source, row, origin, self.pair_send.at[row, origin], self.pair_recv.at[row, origin],
            (self.twin, self.z),
        )

    def across(self, source, origin):
        for t in self.mates:
            self.plane(source, t, self.r, origin).start()
        self.pair(source, self.r, origin).start()

    def begin(self):
        for d in range(1, self.columns):
            self.line(d, self.z).start()
        self.across(self.own, self.z)
        self.out[self.r * self.columns + self.z] = self.own[...]

    def hop(self, d):
        origin = lax.rem(self.z + d, self.columns)
        self.line(d, origin).wait_recv()
        self.across(self.place(self.r, origin), origin)

    def collect(self):
        for t in self.mates:
            for origin in range(self.columns):
                here = self.place(t, origin)
                self.plane(here, t, t, origin).wait_recv()
                self.pair(here, t, origin).start()

    def finish(self):
        for t in self.others:
            for origin in range(self.columns):
                self.pair(self.place(t, origin), t, origin).wait_recv()
        for d in range(1, self.columns):
            self.line(d, self.z).wait_send()
        for origin in range(self.columns):
            for t in self.mates:
                self.plane(self.own, t, self.r, origin).wait_send()
                self.pair(self.own, t, origin).wait_send()
            self.pair(self.own, self.r, origin).wait_send()


def value_kernel(rows, columns, own_ref, spam_ref, vals_ref, turned_ref, *sems):
    spread = Spread(rows, columns, own_ref, vals_ref, sems)
    greet(
        [((t, spread.z), t >= 0) for t in spread.mates + [spread.twin]]
        + [((spread.r, y), y >= 0) for y in spread.peers]
    )
    spread.begin()

    def turn(b, _):
        turned_ref[b] = jnp.transpose(spam_ref[b])
        return 0

    share = -(-spam_ref.shape[0] // columns)
    for d in range(columns):
        if d:
            spread.hop(d)
        first, end = (min(spam_ref.shape[0], k * share) for k in (d, d + 1))
        lax.fori_loop(first, end, turn, 0)
    spread.collect()
    spread.finish()


def expand(cap, block_ref, lists_ref, vals_ref, rank_ref, blocks, bounds, fetched):
    peers, lines, size = lists_ref.shape
    groups = fetched.shape[1] // lines
    tall = 16

    def paint(q, low, high, fresh):
        tags = [
            F32(1) + (block_ref[q * cap + c] + 1).astype(F32) * F32(2.0**-14) for c in range(cap)
        ]

        def some(i, _):
            at = pl.multiple_of(i * tall, tall)
            block = lists_ref[q, pl.ds(at, tall), :].astype(jnp.int32) & (blocks - 1)
            value = vals_ref[q, pl.ds(at, tall), :].astype(F32)
            marked = value * (F32(1) + (block + 1).astype(F32) * F32(2.0**-14))
            for g in range(groups):
                row = pl.multiple_of(g * lines + at, tall)
                spots = rank_ref[q, pl.ds(row, tall), :]
                ends = ends_of(g, groups, spots)

                def layer(j, outs):
                    spot = spots + j
                    live = spot < ends
                    got = jnp.where(live, take(marked, jnp.minimum(spot, size - 1)), F32(0))
                    plain = got.astype(BF16).astype(F32)
                    return tuple(
                        jnp.where(live & (plain * tag == got), plain, out) for tag, out in zip(tags, outs)
                    )

                if fresh:
                    outs = (jnp.zeros((tall, size), F32),) * cap
                else:
                    outs = tuple(
                        fetched[q * cap + c, pl.ds(row, tall), :].astype(F32) for c in range(cap)
                    )
                if high - low > LAYERS:
                    outs = lax.fori_loop(low, high, layer, outs)
                else:
                    for j in range(low, high):
                        outs = layer(j, outs)
                for c in range(cap):
                    fetched[q * cap + c, pl.ds(row, tall), :] = outs[c].astype(BF16)
            return 0

        lax.fori_loop(0, lines // tall, some, 0, unroll=4 if fresh else 1)

    def one(q, _):
        paint(q, 0, LAYERS, True)
        code = bounds[q, 0]

        @pl.when(code > 0)
        def _():
            paint(q, LAYERS, LAYERS + MORE, False)

        @pl.when(code > 1)
        def _():
            paint(q, LAYERS + MORE, size // groups, False)

        return 0

    lax.fori_loop(0, peers, one, 0)


def order_of(z, columns):
    table = []
    for plane in range(columns):
        line = []
        for k in range(columns):
            ahead = [t for t in (columns - 1 - k,) if t > plane]
            back = [t for t in (k,) if t < plane]
            line += ahead + back if 2 * plane < columns else back + ahead
        table.append(line + [plane])
    picks = []
    for i in range(columns):
        pick = z * 0
        for plane in range(columns):
            pick = pick + jnp.where(z == plane, table[plane][i], 0)
        picks.append(pick)
    return picks


def reduce_kernel(first, rows, columns, cap, words_ref, *refs):
    if first:
        cores_ref, mine_ref, raw_ref, inflow_ref, weight_ref, spam_ref, want_ref, keys_ref, lists_ref, *refs = refs
    else:
        lists_ref, inflow_ref, rank_ref, *refs = refs
    landed, table, partial, exps, gains, packed, inbox, own, send, recv, chain_send, chain_recv, *refs = refs
    r, z = lax.axis_index("row"), lax.axis_index("col")
    blocks, part, size = partial.shape
    seeds = inflow_ref.shape[1]
    halves = seeds // part
    bits = blocks.bit_length() - 1
    tail_at = cap * part
    spans = []
    for h in range(halves):
        start = spans[-1][0] + spans[-1][1] if spans else 0
        spans.append((start, cap * part + (landed.shape[2] - cap * seeds if h == 0 else 0)))
    data = blocks * part
    longs = [data + blocks * (4 if first and h == 0 else 1) for h in range(halves)]
    others = [lax.rem(r + d, rows) for d in range(1, rows)]
    targets = order_of(z, columns)
    block_iota = lax.broadcasted_iota(jnp.int32, (blocks, size), 0)
    greet(
        [((t, z), t >= 0) for t in others]
        + (
            [((r, lax.rem(z + d, columns)), z >= 0) for d in range(1, columns)] if first
            else [((r, z - 1), z > 0), ((r, z + 1), z < columns - 1)]
        )
    )

    def across(i, h, t, origin):
        at = pl.ds(*spans[h])
        return pltpu.make_async_remote_copy(
            src_ref=words_ref.at[t * columns + targets[i], at], dst_ref=landed.at[i, origin, at],
            send_sem=send.at[i, h, t], recv_sem=recv.at[i, h, origin],
            device_id=(t, z), device_id_type=MESH,
        )

    def mine(i):
        return pltpu.make_async_copy(
            words_ref.at[r * columns + targets[i]], landed.at[i, r], own.at[i]
        )

    def chain(i, h, side):
        at = pl.ds(0, longs[h])
        return pltpu.make_async_remote_copy(
            src_ref=packed.at[min(i, columns - 2), h, at], dst_ref=inbox.at[side, targets[i], h, at],
            send_sem=chain_send.at[min(i, columns - 2), h], recv_sem=chain_recv.at[side, targets[i], h],
            device_id=(r, z + 1 - 2 * side), device_id_type=MESH,
        )

    def to_int16(value):
        return value.astype(jnp.int32).astype(jnp.int16)

    def to_float(value):
        return value.astype(jnp.int32).astype(F32)

    if first:
        known_send, known_recv, tally, *sems = refs
        spread = Spread(rows, columns, keys_ref, lists_ref, sems)

        def know(t, origin):
            return pltpu.make_async_remote_copy(
                src_ref=mine_ref, dst_ref=want_ref.at[origin],
                send_sem=known_send.at[t], recv_sem=known_recv.at[origin],
                device_id=(t, z), device_id_type=MESH,
            )

        for t in others:
            know(t, r).start()
        want_ref[r] = mine_ref[...]

    def launch(i):
        for h in range(halves):
            for t in others:
                across(i, h, t, r).start()
        mine(i).start()

    launch(0)
    launch(1)
    if first:
        keys_ref[...] = sort_hosts(columns, blocks, raw_ref[...])
        spread.begin()
    else:
        peers, lines, _ = lists_ref.shape
        groups = seeds // lines
        turns = (columns - 1) * halves - 1
        load = -(-peers // turns)

        def find(q, _):
            keys = lists_ref[q].astype(jnp.int32) & (blocks * size - 1)
            for g, spots in enumerate(find_ranks(groups, blocks, keys)):
                rank_ref[q, g * lines : (g + 1) * lines, :] = spots
            return 0

    pieces = min(8, (columns - 1) * halves)
    for i in range(columns):
        mine(i).wait()
        side = jnp.where(targets[i] > z, 0, 1)
        joined = jnp.where(targets[i] > z, z > 0, z < columns - 1)
        cols = jnp.zeros((blocks, size), F32)
        for h in range(halves):
            for t in others:
                across(i, h, t, t).wait_recv()
            if h == 0:
                def weigh(q, cols):
                    tail = landed[i, q, tail_at : spans[0][1], :].astype(jnp.int32)
                    for c in range(cap):
                        word = tail[c : c + 1, :]
                        hit = block_iota == (word & (blocks - 1))
                        scale = jnp.exp2((word >> bits).astype(F32) - WORD)
                        table[q * cap + c] = jnp.where(
                            hit, jnp.broadcast_to(scale, (blocks, size)), F32(0)
                        )
                        if first:
                            f, high, low = (
                                tail[cap + 3 * c + k : cap + 3 * c + k + 1, :].astype(F32) for k in range(3)
                            )
                            col = (high + low * F32(2.0**-WORD)) * jnp.exp2(f - WORD)
                            cols = cols + jnp.where(hit, jnp.broadcast_to(col, (blocks, size)), F32(0))
                    return cols

                cols = lax.fori_loop(0, rows, weigh, cols, unroll=4)

            first_row = spans[h][0]

            def strip(k, _):
                at = pl.multiple_of(k * 16, 16)

                def add(q, sums):
                    sums = list(sums)
                    for c in range(cap):
                        spot = pl.multiple_of(first_row + c * part + at, 16)
                        value = to_float(landed[i, q, pl.ds(spot, 16), :])
                        for b in range(blocks):
                            sums[b] = sums[b] + value * table[q * cap + c, b : b + 1, :]
                    return tuple(sums)

                sums = lax.fori_loop(0, rows, add, (jnp.zeros((16, size), F32),) * blocks)
                for b in range(blocks):
                    partial[b, pl.ds(at, 16), :] = sums[b]
                return 0

            lax.fori_loop(0, part // 16, strip, 0)

            def join(way):
                chain(i, h, way).wait_recv()
                exps[...] = jnp.exp2(to_float(inbox[way, targets[i], h, data : data + blocks, :]) - WORD)

                def one(b, _):
                    got = to_float(inbox[way, targets[i], h, pl.ds(pl.multiple_of(b * part, part), part), :])
                    partial[b] += got * exps[pl.ds(b, 1), :]
                    return 0

                lax.fori_loop(0, blocks, one, 0, unroll=4)

            def join_cols(way):
                f, high, low = (
                    to_float(inbox[way, targets[i], h, data + (k + 1) * blocks : data + (k + 2) * blocks, :])
                    for k in range(3)
                )
                colsum[...] += (high + low * F32(2.0**-WORD)) * jnp.exp2(f - WORD)

            if first and h == 0:
                colsum = weight_ref
                colsum[...] = cols
            if i < columns - 1:
                @pl.when(joined)
                def _():
                    join(side)
                    if first and h == 0:
                        join_cols(side)

                def peak(b, _):
                    exps[pl.ds(b, 1), :] = jnp.max(jnp.abs(partial[b]), axis=0, keepdims=True)
                    return 0

                def squeeze(b, _):
                    packed[i, h, pl.ds(pl.multiple_of(b * part, part), part), :] = to_int16(
                        to_words(partial[b] * gains[pl.ds(b, 1), :])
                    )
                    return 0

                lax.fori_loop(0, blocks, peak, 0, unroll=8)
                exps[...] = exponent_of(exps[...])
                gains[...] = jnp.exp2(WORD - exps[...])
                lax.fori_loop(0, blocks, squeeze, 0, unroll=8)
                packed[i, h, data : data + blocks, :] = to_int16(exps[...])
                if first and h == 0:
                    col = colsum[...]
                    f = exponent_of(jnp.abs(col))
                    scaled = col * jnp.exp2(WORD - f)
                    high = to_words(scaled)
                    for k, row in enumerate((f, high, to_words((scaled - high) * F32(2.0**WORD)))):
                        packed[i, h, data + (k + 1) * blocks : data + (k + 2) * blocks, :] = to_int16(row)
                chain(i, h, side).start()
            else:
                for way, there in ((0, z > 0), (1, z < columns - 1)):
                    @pl.when(there)
                    def _():
                        join(way)
                        if first and h == 0:
                            join_cols(way)

                def finish(b, _):
                    inflow_ref[b, h * part : (h + 1) * part, :] = partial[b]
                    return 0

                lax.fori_loop(0, blocks, finish, 0, unroll=4)
                if first and h == 0:
                    colsum[...] += F32(1)
            step = i * halves + h
            if first and step < columns - 1:
                spread.hop(step + 1)
            if h == min(columns, halves) - 1 and i + 2 < columns:
                launch(i + 2)
            if first and step == (columns - 2) * halves:
                spread.collect()
            if not first and 0 <= step - halves < turns:
                begin, end = (min(peers, k * load) for k in (step - halves, step - halves + 1))
                lax.fori_loop(begin, end, find, 0, unroll=3 if (end - begin) % 3 == 0 else 2)
            if first and 0 <= step - halves < pieces:
                count_seeds(columns, cores_ref, tally, step - halves, pieces)
            if first and step == halves + pieces:
                spread_seeds(cores_ref.shape[1], tally, spam_ref)

    if first:
        for t in others:
            know(t, r).wait_send()
            know(t, t).wait_recv()
        spread.finish()
    for i in range(columns):
        for h in range(halves):
            for t in others:
                across(i, h, t, r).wait_send()
            if i < columns - 1:
                chain(i, h, jnp.where(targets[i] > z, 0, 1)).wait_send()


def trust_kernel(inflow, good_ref, spam_ref, weight_ref, keys_ref, trust_ref, shield_ref, vals_ref):
    blocks, seeds, size = inflow.shape
    lines = keys_ref.shape[0]
    groups = seeds // lines
    keys = keys_ref[...].astype(jnp.int32) & (blocks * size - 1)
    lanes = keys // blocks
    block = keys & (blocks - 1)
    part = lax.broadcasted_iota(jnp.int32, (lines, size), 1) // (size // groups)

    def one(b, vals):
        trust = F32(0.85) * inflow[b] + F32(0.15) * good_ref[b]
        trust_ref[pl.ds(pl.multiple_of(b * size, size), size), :] = jnp.transpose(trust)
        shield = F32(1) / (F32(1) + trust)
        shield_ref[b] = shield
        share = (shield * spam_ref[b] / weight_ref[pl.ds(b, 1), :]).astype(BF16).astype(F32)
        for g in range(groups):
            got = take(share[g * lines : (g + 1) * lines, :], lanes)
            vals = jnp.where((block == b) & (part == g), got, vals)
        return vals

    vals = lax.fori_loop(0, blocks, one, jnp.zeros((lines, size), F32), unroll=2)
    vals_ref[...] = vals.astype(BF16)


def pull_kernel(last, *refs):
    if last:
        src_ref, slot_ref, fetched_ref, spam_ref, tiles_ref, out_ref, acc = refs
    else:
        (src_ref, slot_ref, block_ref, lists_ref, vals_ref, rank_ref, spam_ref, shield_ref, weight_ref,
         tiles_ref, out_ref, acc, fetched_ref, codes, bounds, sem) = refs
    step = pl.program_id(0)
    per_step = tiles_ref.shape[0]
    size = acc.shape[2]

    @pl.when(step == 0)
    def _():
        acc[...] = jnp.zeros_like(acc)
        if not last:
            blocks = acc.shape[0]
            codes[...] = lists_ref[:, 0, :].astype(jnp.int32) // (blocks * size)
            copy = pltpu.make_async_copy(codes, bounds, sem)
            copy.start()
            copy.wait()
            expand(
                block_ref.shape[0] // lists_ref.shape[0], block_ref, lists_ref, vals_ref, rank_ref,
                blocks, bounds, fetched_ref,
            )

    def some(g, _):
        products = []
        for k in range(GROUP):
            n = step * per_step + g * GROUP + k
            tile, got = tiles_ref[g * GROUP + k], fetched_ref[slot_ref[n]]
            if last:
                products.append(jnp.dot(tile, got, preferred_element_type=F32))
            else:
                products.append(
                    lax.dot_general(got, tile, (((1,), (1,)), ((), ())), preferred_element_type=F32)
                )
        for k in range(GROUP):
            acc[src_ref[step * per_step + g * GROUP + k]] += products[k]
        return 0

    lax.fori_loop(0, per_step // GROUP, some, 0)

    @pl.when(step == pl.num_programs(0) - 1)
    def _():
        def distrust(b):
            return F32(0.85) * acc[b] + F32(0.15) * spam_ref[b]

        if last:
            def one(b, _):
                out_ref[pl.ds(pl.multiple_of(b * size, size), size), :] = distrust(b)
                return 0

            lax.fori_loop(0, acc.shape[0], one, 0, unroll=2)
        else:
            shares(shield_ref, weight_ref, distrust, out_ref)


def start_kernel(columns, good_ref, spam_ref, tiles_ref, count_ref, list_ref, near_ref, tally, sem):
    load = pltpu.make_async_copy(tiles_ref, near_ref, sem)
    load.start()
    list_ref[...] = jnp.transpose(spam_ref[...].astype(F32)).astype(jnp.int32)
    count_seeds(columns, good_ref, tally)
    spread_seeds(good_ref.shape[1], tally, count_ref)
    load.wait()


def body(columns, tiles, tile_src, tile_slot, slot_block, out_degree, good_seeds, spam_cores):
    tile_count, size, _ = tiles.shape
    here = lambda x: pltpu.with_memory_space_constraint(x, pltpu.HBM)
    hosts = out_degree.shape[0]
    blocks = hosts // size
    seeds = good_seeds.shape[0]
    slots = slot_block.shape[0]
    peers = lax.axis_size(AXES)
    cap = slots // peers
    tail = -(-4 * cap // 16) * 16
    steps = 1
    shape = jax.ShapeDtypeStruct
    vector = (blocks, seeds, size)
    degree = out_degree.reshape(blocks, 1, size)

    rows = peers // columns
    part = seeds // HALVES
    count = spam_cores.shape[1]
    groups = seeds // count
    lines = seeds // groups
    good, spam_list, tiles = pl.pallas_call(
        functools.partial(start_kernel, columns),
        out_shape=(
            shape(vector, F32), shape(spam_cores.shape, jnp.int32), shape(tiles.shape, BF16),
        ),
        in_specs=[VM, VM, ANY],
        out_specs=(VM, VM, VM),
        scratch_shapes=[pltpu.VMEM((seeds, blocks, size), F32), pltpu.SemaphoreType.DMA],
        compiler_params=PLAIN,
        cost_estimate=pl.CostEstimate(
            flops=2 * seeds * good_seeds.size * (blocks + size), transcendentals=0,
            bytes_accessed=24 << 20,
        ),
    )(here(good_seeds), here(spam_cores.T), here(tiles))

    tile_spec = VM
    words = shape((peers, cap * size + tail, size), jnp.int16)
    outgoing = pl.pallas_call(
        functools.partial(push_kernel, True, cap, part),
        grid=(steps,),
        out_shape=words,
        in_specs=[SM, SM, SM, VM, VM, tile_spec],
        out_specs=VM,
        scratch_shapes=[
            pltpu.VMEM((slots, seeds + 16, size), F32),
            pltpu.VMEM((blocks, seeds + 16, size), BF16),
        ],
        compiler_params=PLAIN,
    )(here(tile_src), here(tile_slot), here(slot_block), good, here(degree), tiles)

    dma = pltpu.SemaphoreType.DMA
    spread_sems = [
        dma((columns,)), dma((columns,)), dma((rows, columns)), dma((rows, columns)),
        dma((rows, columns)), dma((rows, columns)),
    ]

    def reduce(first, words_in, *rest):
        long = blocks * part + blocks * (4 if first else 1)
        outs = (
            shape(vector, F32), shape((blocks, size), F32), shape(vector, F32),
            shape((rows, 1, slots), jnp.int32), shape((lines, size), jnp.int16),
            shape((peers, lines, size), jnp.int16),
        )
        if not first:
            outs = (shape(vector, F32), shape((peers, seeds, size), jnp.int32))
        return pl.pallas_call(
            functools.partial(reduce_kernel, first, rows, columns, cap),
            out_shape=outs,
            in_specs=[ANY, VM, VM, VM] if first else [ANY, VM],
            out_specs=(VM,) * len(outs),
            scratch_shapes=[
                pltpu.VMEM((columns, rows, cap * size + tail, size), jnp.int16),
                pltpu.VMEM((rows * cap, blocks, size), F32),
                pltpu.VMEM((blocks, part, size), F32),
                pltpu.VMEM((blocks, size), F32),
                pltpu.VMEM((blocks, size), F32),
                pltpu.VMEM((columns - 1, HALVES, long, size), jnp.int16),
                pltpu.VMEM((2, columns, HALVES, long, size), jnp.int16),
                dma((columns,)),
                dma((columns, HALVES, rows)),
                dma((columns, HALVES, rows)),
                dma((columns - 1, HALVES)),
                dma((2, columns, HALVES)),
                *([dma((rows,)), dma((rows,)), pltpu.VMEM((seeds, blocks, size), F32), *spread_sems] if first else []),
            ],
            compiler_params=pltpu.CompilerParams(
                collective_id=1 if first else 2, has_side_effects=True,
                vmem_limit_bytes=LIMIT,
            ),
        )(words_in, *rest)

    inflow, weight, spam, want, keys, lists = reduce(
        True, outgoing, spam_list, slot_block.reshape(1, slots), spam_cores.T
    )
    outgoing = pl.pallas_call(
        functools.partial(push_kernel, False, cap, part),
        grid=(steps,),
        out_shape=words,
        in_specs=[SM, SM, SM, VM, VM, VM, tile_spec],
        out_specs=VM,
        scratch_shapes=[
            pltpu.VMEM((slots, seeds, size), F32),
            pltpu.VMEM(vector, BF16),
        ],
        compiler_params=PLAIN,
    )(tile_src, tile_slot, slot_block, inflow, good, degree, tiles)
    inflow, ranks = reduce(False, outgoing, lists)
    fetch = pl.pallas_call(
        functools.partial(fetch_kernel, rows, columns, cap),
        out_shape=shape((slots, seeds, size), BF16),
        in_specs=[SM, VM],
        out_specs=VM,
        scratch_shapes=[
            *[pltpu.VMEM(vector, BF16)] * (2 * columns - 2),
            pltpu.VMEM((rows, columns * cap, seeds, size), BF16),
            pltpu.SemaphoreType.DMA((2 * columns - 2,)),
            pltpu.SemaphoreType.DMA((2 * columns - 2,)),
            pltpu.SemaphoreType.DMA((rows, columns)),
            pltpu.SemaphoreType.DMA((rows, columns)),
        ],
        compiler_params=pltpu.CompilerParams(collective_id=0, has_side_effects=True, vmem_limit_bytes=LIMIT),
    )
    trust, shield, vals = pl.pallas_call(
        trust_kernel,
        out_shape=(shape((hosts, seeds), F32), shape(vector, F32), shape((lines, size), BF16)),
        in_specs=[VM, VM, VM, VM, VM],
        out_specs=(VM, VM, VM),
        compiler_params=PLAIN,
    )(inflow, good, spam, weight, keys)
    vals, turned = pl.pallas_call(
        functools.partial(value_kernel, rows, columns),
        out_shape=(shape((peers, lines, size), BF16), shape(vector, F32)),
        in_specs=[VM, VM],
        out_specs=(VM, VM),
        scratch_shapes=spread_sems,
        compiler_params=pltpu.CompilerParams(
            collective_id=3, has_side_effects=True, vmem_limit_bytes=LIMIT
        ),
    )(vals, spam)
    share = pl.pallas_call(
        functools.partial(pull_kernel, False),
        grid=(steps,),
        out_shape=shape(vector, BF16),
        in_specs=[SM, SM, SM, VM, VM, VM, VM, VM, VM, tile_spec],
        out_specs=VM,
        scratch_shapes=[
            pltpu.VMEM(vector, F32),
            pltpu.VMEM((slots, seeds, size), BF16),
            pltpu.VMEM((peers, size), jnp.int32),
            pltpu.SMEM((peers, size), jnp.int32),
            pltpu.SemaphoreType.DMA,
        ],
        compiler_params=PLAIN,
    )(tile_src, tile_slot, slot_block, lists, vals, ranks, spam, shield, weight, tiles)
    fetched = fetch(want, share)
    distrust = pl.pallas_call(
        functools.partial(pull_kernel, True),
        grid=(steps,),
        out_shape=shape((hosts, seeds), F32),
        in_specs=[SM, SM, VM, VM, tile_spec],
        out_specs=VM,
        scratch_shapes=[pltpu.VMEM(vector, F32)],
        compiler_params=PLAIN,
    )(tile_src, tile_slot, fetched, turned, tiles)
    return trust, distrust


def solution(mesh):
    in_specs = (
        P(AXES, None, None),
        P(AXES),
        P(AXES),
        P(AXES),
        P(AXES),
        P(None, AXES),
        P(None, AXES),
    )
    out_specs = (P(AXES, None), P(AXES, None))
    return jax.shard_map(
        functools.partial(body, mesh.shape["col"]),
        mesh=mesh, in_specs=in_specs, out_specs=out_specs, check_vma=False,
    )
```

```python
import functools

import jax
import jax.numpy as jnp
from jax import lax
from jax.experimental import pallas as pl
from jax.experimental.pallas import tpu as pltpu
from jax.sharding import PartitionSpec as P

AXES = ("row", "col")
VM = pl.BlockSpec(memory_space=pltpu.VMEM)
SM = pl.BlockSpec(memory_space=pltpu.SMEM)
LIMIT = 28 << 20
ANY = pl.BlockSpec(memory_space=pl.ANY)
F32 = jnp.float32
BF16 = jnp.bfloat16
PLAIN = pltpu.CompilerParams(vmem_limit_bytes=LIMIT)
WORD = 15
GROUP = 64
HALVES = 4
PARTS = 2
LAYERS = 6
MORE = 2
MESH = pl.DeviceIdType.MESH


def count_seeds(columns, source, tally, step=0, pieces=1):
    seeds, blocks, size = tally.shape
    hosts = blocks * size
    base = (lax.axis_index("row") * columns + lax.axis_index("col")) * hosts
    count = source.shape[1]
    block_iota = lax.broadcasted_iota(jnp.int32, (blocks, count), 0) * size
    lane_iota = lax.broadcasted_iota(jnp.int32, (size, count), 0)

    def one(s, _):
        local = source[pl.ds(s, 1), :] - base
        shifted = local - block_iota
        inside = jnp.where((shifted >= 0) & (shifted < size), F32(1), F32(0)).astype(BF16)
        start = jnp.max(jnp.where(local >= block_iota, block_iota, 0), axis=0, keepdims=True)
        lane = jnp.where(lane_iota == local - start, F32(1), F32(0)).astype(BF16)
        tally[s] = lax.dot_general(
            inside, lane, (((1,), (1,)), ((), ())), preferred_element_type=F32
        )
        return 0

    share = seeds // pieces
    lax.fori_loop(step * share, (step + 1) * share, one, 0, unroll=16)


def spread_seeds(count, tally, target):
    blocks, _, size = target.shape
    factor = F32(blocks * size / count)
    for b in range(blocks):
        target[b] = tally[:, b, :] * factor


def exponent_of(peak):
    return jnp.floor(jnp.log2(jnp.maximum(peak, F32(2.0**-100)))) + F32(1)


def to_words(value):
    return jnp.clip(jnp.floor(value + F32(0.5)), F32(-32767), F32(32767))


def pack(first, cap, part, bits, acc, block_ref, out_ref):
    peers = out_ref.shape[0]
    size = acc.shape[2]
    halves = size // part
    tail = out_ref.shape[1] - cap * size

    def one(p, _):
        exps, cols = [], []
        for c in range(cap):
            n = p * cap + c
            value = acc[n, :size, :]
            e = exponent_of(jnp.max(jnp.abs(value), axis=0, keepdims=True))
            words = to_words(value * jnp.exp2(WORD - e)).astype(jnp.int32).astype(jnp.int16)
            for h in range(halves):
                at = (h * cap + c) * part + (tail if h else 0)
                out_ref[p, at : at + part, :] = words[h * part : (h + 1) * part, :]
            exps.append(e * F32(2**bits) + block_ref[n].astype(F32))
            if first:
                col = acc[n, size : size + 8, :][:1, :]
                f = exponent_of(jnp.abs(col))
                scaled = col * jnp.exp2(WORD - f)
                high = to_words(scaled)
                cols += [f, high, to_words((scaled - high) * F32(2.0**WORD))]
        rows = exps + cols
        if tail > len(rows):
            rows.append(jnp.zeros((tail - len(rows), size), F32))
        at = cap * part
        out_ref[p, at : at + tail, :] = jnp.concatenate(rows, axis=0).astype(jnp.int32).astype(jnp.int16)
        return 0

    lax.fori_loop(0, peers, one, 0, unroll=2)


def push_kernel(first, cap, part, *refs):
    if first:
        src_ref, slot_ref, block_ref, good_ref, degree_ref, tiles_ref, out_ref, acc, scaled = refs
    else:
        src_ref, slot_ref, block_ref, inflow, good_ref, degree_ref, tiles_ref, out_ref, acc, scaled = refs
    step = pl.program_id(0)
    blocks, seeds, size = good_ref.shape
    per_step = tiles_ref.shape[0]

    @pl.when(step == 0)
    def _():
        acc[...] = jnp.zeros_like(acc)
        def one(b, _):
            degree = degree_ref[b].astype(F32)
            trust = good_ref[b]
            if not first:
                trust = F32(0.85) * inflow[b] + F32(0.15) * trust
            scaled[b, :seeds, :] = (trust / degree).astype(BF16)
            if first:
                scaled[b, seeds:, :] = jnp.ones((scaled.shape[1] - seeds, size), BF16)
            return 0

        lax.fori_loop(0, blocks, one, 0)

    def some(g, _):
        products = []
        for k in range(GROUP):
            n = step * per_step + g * GROUP + k
            products.append(
                jnp.dot(scaled[src_ref[n]], tiles_ref[g * GROUP + k], preferred_element_type=F32)
            )
        for k in range(GROUP):
            acc[slot_ref[step * per_step + g * GROUP + k]] += products[k]
        return 0

    lax.fori_loop(0, per_step // GROUP, some, 0)

    @pl.when(step == pl.num_programs(0) - 1)
    def _():
        pack(first, cap, part, blocks.bit_length() - 1, acc, block_ref, out_ref)


def shares(shield_ref, weight_ref, start_of, share_ref):
    def one(b, _):
        weight = weight_ref[pl.ds(b, 1), :]
        share_ref[b] = jnp.transpose(shield_ref[b] * start_of(b) / weight).astype(BF16)
        return 0

    lax.fori_loop(0, share_ref.shape[0], one, 0, unroll=2)


def greet(devices):
    barrier = pltpu.get_barrier_semaphore()
    for device, there in devices:
        @pl.when(there)
        def _():
            pl.semaphore_signal(barrier, inc=1, device_id=device, device_id_type=MESH)
    pl.semaphore_wait(barrier, sum(jnp.where(there, 1, 0) for _, there in devices))


def fetch_kernel(rows, columns, cap, want_ref, share_ref, fetched_ref, *scratch):
    line = 2 * (columns - 1)
    held, (picked, line_send, line_recv, send, recv) = scratch[: line * PARTS], scratch[line * PARTS :]
    r, z = lax.axis_index("row"), lax.axis_index("col")
    others = [lax.rem(r + d, rows) for d in range(1, rows)]
    sides = (-1, 1)
    inside = {side: (z + side >= 0) & (z + side < columns) for side in sides}
    tall = share_ref.shape[1] // PARTS
    greet([((t, z), t >= 0) for t in others] + [((r, z + side), inside[side]) for side in sides])

    def place(side, d, k):
        return (2 * (d - 1) + (0 if side < 0 else 1)) * PARTS + k

    def pass_on(source, d, side, k):
        slot = place(-side, d, k)
        return pltpu.make_async_remote_copy(
            src_ref=source, dst_ref=held[slot],
            send_sem=line_send.at[slot], recv_sem=line_recv.at[slot],
            device_id=(r, z + side), device_id_type=MESH,
        )

    def own(k):
        return share_ref.at[:, pl.ds(k * tall, tall)]

    def serve(t, origin, k, source, sender):
        span = pl.ds(k * tall, tall)
        return pltpu.make_async_remote_copy(
            src_ref=picked.at[t, pl.ds(origin * cap, cap), span],
            dst_ref=fetched_ref.at[pl.ds((source * columns + origin) * cap, cap), span],
            send_sem=send.at[t, origin * PARTS + k], recv_sem=recv.at[sender, origin * PARTS + k],
            device_id=(t, z), device_id_type=MESH,
        )

    def spread(source, origin, k):
        span = slice(k * tall, (k + 1) * tall)

        def pick(t, j):
            n = want_ref[t, 0, (r * columns + origin) * cap + j]
            return source[n, span, :] if source.shape[1] > tall else source[n]

        before = None
        for t in others:
            for j in range(cap):
                picked[t, origin * cap + j, span, :] = pick(t, j)
            if before is not None:
                serve(before, origin, k, r, r).start()
            before = t
        for j in range(cap):
            fetched_ref[(r * columns + origin) * cap + j, span, :] = pick(r, j)
        serve(before, origin, k, r, r).start()

    for k in range(PARTS):
        for side in sides:
            @pl.when(inside[side])
            def _():
                pass_on(own(k), 1, side, k).start()
    for k in range(PARTS):
        spread(share_ref, z, k)
    for d in range(1, columns):
        for k in range(PARTS):
            for side in sides:
                origin = z + side * d

                @pl.when((origin >= 0) & (origin < columns))
                def _():
                    here = held[place(side, d, k)]
                    pass_on(here, d, -side, k).wait_recv()

                    if d < columns - 1:
                        @pl.when(inside[-side])
                        def _():
                            pass_on(here, d + 1, -side, k).start()

                    spread(here, origin, k)
    for origin in range(columns):
        for k in range(PARTS):
            for t in others:
                serve(t, origin, k, r, r).wait_send()
                serve(t, origin, k, t, t).wait_recv()
    for d in range(columns - 1):
        for k in range(PARTS):
            for side in sides:
                origin = z - side * d

                @pl.when((origin >= 0) & (origin < columns) & inside[side])
                def _():
                    pass_on(held[0], d + 1, side, k).wait_send()


def take(table, index):
    return jnp.take_along_axis(table, index, axis=1, mode="promise_in_bounds")


def find_ranks(groups, blocks, keys):
    lines, size = keys.shape
    count = size // groups
    least = lax.broadcasted_iota(jnp.int32, (lines, size), 1) * blocks
    spots = [jnp.full((lines, size), count * g, jnp.int32) for g in range(groups)]
    step = count // 2
    while True:
        probes = [take(keys, spot + (max(step, 1) - 1)) for spot in spots]
        spots = [spot + jnp.where(probe < least, max(step, 1), 0) for spot, probe in zip(spots, probes)]
        if step == 0:
            return spots
        step //= 2


def ends_of(g, groups, spots):
    lines, size = spots.shape
    lane = lax.broadcasted_iota(jnp.int32, (lines, size), 1)
    after = pltpu.roll(spots, size - 1, 1)
    return jnp.where(lane == size - 1, (size // groups) * (g + 1), after)


def sort_hosts(columns, blocks, raw):
    count, seeds = raw.shape
    groups = seeds // count
    lines = seeds // groups
    base = (lax.axis_index("row") * columns + lax.axis_index("col")) * (blocks * seeds)
    local = (raw - base).astype(F32)
    stacked = jnp.concatenate(
        [local] + [pltpu.roll(local, seeds - g * lines, 1) for g in range(1, groups)], axis=0
    )
    hosts = jnp.transpose(stacked)[:lines, :].astype(jnp.int32)
    keys = ((hosts & (seeds - 1)) * blocks + hosts // seeds).astype(F32)
    lane = lax.broadcasted_iota(jnp.int32, keys.shape, 1)
    k = 2
    while k <= count:
        j = k // 2
        while j:
            other = take(keys, lane ^ j)
            rising = ((lane & k) == 0) | (k == count)
            lower = ((lane & j) == 0) == rising
            keys = jnp.where(lower, jnp.minimum(keys, other), jnp.maximum(keys, other))
            j //= 2
        k *= 2
    keys = keys.astype(jnp.int32)
    spots = find_ranks(groups, blocks, keys)
    most = functools.reduce(
        jnp.maximum, [ends_of(g, groups, spot) - spot for g, spot in enumerate(spots)]
    ).astype(F32)
    most = jnp.max(jnp.max(most, axis=1, keepdims=True), axis=0, keepdims=True).astype(jnp.int32)
    code = jnp.where(most > LAYERS, 1, 0) + jnp.where(most > LAYERS + MORE, 1, 0)
    return (keys + code * (blocks * seeds)).astype(jnp.int16)


class Spread:
    def __init__(self, rows, columns, own, out, sems):
        self.rows, self.columns, self.own, self.out = rows, columns, own, out
        self.line_send, self.line_recv, self.plane_send, self.plane_recv, self.pair_send, self.pair_recv = sems
        r, z = lax.axis_index("row"), lax.axis_index("col")
        self.r, self.z = r, z
        self.twin = r + 1 - 2 * lax.rem(r, 2)
        self.mates = [lax.rem(r + d, rows) for d in range(2, rows, 2)]
        self.others = [self.twin] + [lax.rem(self.twin + d, rows) for d in range(2, rows, 2)]
        self.peers = [lax.rem(z + d, columns) for d in range(1, columns)]

    def send(self, source, row, origin, sends, recvs, to):
        return pltpu.make_async_remote_copy(
            src_ref=source, dst_ref=self.out.at[row * self.columns + origin],
            send_sem=sends, recv_sem=recvs, device_id=to, device_id_type=MESH,
        )

    def place(self, row, origin):
        return self.out.at[row * self.columns + origin]

    def line(self, d, origin):
        return self.send(
            self.own, self.r, origin, self.line_send.at[d], self.line_recv.at[origin],
            (self.r, lax.rem(self.z + d, self.columns)),
        )

    def plane(self, source, t, row, origin):
        return self.send(
            source, row, origin, self.plane_send.at[t, origin], self.plane_recv.at[row, origin],
            (t, self.z),
        )

    def pair(self, source, row, origin):
        return self.send(
            source, row, origin, self.pair_send.at[row, origin], self.pair_recv.at[row, origin],
            (self.twin, self.z),
        )

    def across(self, source, origin):
        for t in self.mates:
            self.plane(source, t, self.r, origin).start()
        self.pair(source, self.r, origin).start()

    def begin(self):
        for d in range(1, self.columns):
            self.line(d, self.z).start()
        self.across(self.own, self.z)
        self.out[self.r * self.columns + self.z] = self.own[...]

    def hop(self, d):
        origin = lax.rem(self.z + d, self.columns)
        self.line(d, origin).wait_recv()
        self.across(self.place(self.r, origin), origin)

    def collect(self):
        for t in self.mates:
            for origin in range(self.columns):
                here = self.place(t, origin)
                self.plane(here, t, t, origin).wait_recv()
                self.pair(here, t, origin).start()

    def finish(self):
        for t in self.others:
            for origin in range(self.columns):
                self.pair(self.place(t, origin), t, origin).wait_recv()
        for d in range(1, self.columns):
            self.line(d, self.z).wait_send()
        for origin in range(self.columns):
            for t in self.mates:
                self.plane(self.own, t, self.r, origin).wait_send()
                self.pair(self.own, t, origin).wait_send()
            self.pair(self.own, self.r, origin).wait_send()


def value_kernel(rows, columns, own_ref, spam_ref, vals_ref, turned_ref, *sems):
    spread = Spread(rows, columns, own_ref, vals_ref, sems)
    greet(
        [((t, spread.z), t >= 0) for t in spread.mates + [spread.twin]]
        + [((spread.r, y), y >= 0) for y in spread.peers]
    )
    spread.begin()

    def turn(b, _):
        turned_ref[b] = jnp.transpose(spam_ref[b])
        return 0

    share = -(-spam_ref.shape[0] // columns)
    for d in range(columns):
        if d:
            spread.hop(d)
        first, end = (min(spam_ref.shape[0], k * share) for k in (d, d + 1))
        lax.fori_loop(first, end, turn, 0)
    spread.collect()
    spread.finish()


def expand(cap, block_ref, lists_ref, vals_ref, rank_ref, blocks, bounds, fetched):
    peers, lines, size = lists_ref.shape
    groups = fetched.shape[1] // lines
    tall = 16

    def paint(q, low, high, fresh):
        tags = [
            F32(1) + (block_ref[q * cap + c] + 1).astype(F32) * F32(2.0**-14) for c in range(cap)
        ]

        def some(i, _):
            at = pl.multiple_of(i * tall, tall)
            block = lists_ref[q, pl.ds(at, tall), :].astype(jnp.int32) & (blocks - 1)
            value = vals_ref[q, pl.ds(at, tall), :].astype(F32)
            marked = value * (F32(1) + (block + 1).astype(F32) * F32(2.0**-14))
            for g in range(groups):
                row = pl.multiple_of(g * lines + at, tall)
                spots = rank_ref[q, pl.ds(row, tall), :]
                ends = ends_of(g, groups, spots)

                def layer(j, outs):
                    spot = spots + j
                    live = spot < ends
                    got = jnp.where(live, take(marked, jnp.minimum(spot, size - 1)), F32(0))
                    plain = got.astype(BF16).astype(F32)
                    return tuple(
                        jnp.where(live & (plain * tag == got), plain, out) for tag, out in zip(tags, outs)
                    )

                if fresh:
                    outs = (jnp.zeros((tall, size), F32),) * cap
                else:
                    outs = tuple(
                        fetched[q * cap + c, pl.ds(row, tall), :].astype(F32) for c in range(cap)
                    )
                if high - low > LAYERS:
                    outs = lax.fori_loop(low, high, layer, outs)
                else:
                    for j in range(low, high):
                        outs = layer(j, outs)
                for c in range(cap):
                    fetched[q * cap + c, pl.ds(row, tall), :] = outs[c].astype(BF16)
            return 0

        lax.fori_loop(0, lines // tall, some, 0, unroll=4 if fresh else 1)

    def one(q, _):
        paint(q, 0, LAYERS, True)
        code = bounds[q, 0]

        @pl.when(code > 0)
        def _():
            paint(q, LAYERS, LAYERS + MORE, False)

        @pl.when(code > 1)
        def _():
            paint(q, LAYERS + MORE, size // groups, False)

        return 0

    lax.fori_loop(0, peers, one, 0)


def order_of(z, columns):
    table = []
    for plane in range(columns):
        line = []
        for k in range(columns):
            ahead = [t for t in (columns - 1 - k,) if t > plane]
            back = [t for t in (k,) if t < plane]
            line += ahead + back if 2 * plane < columns else back + ahead
        table.append(line + [plane])
    picks = []
    for i in range(columns):
        pick = z * 0
        for plane in range(columns):
            pick = pick + jnp.where(z == plane, table[plane][i], 0)
        picks.append(pick)
    return picks


def reduce_kernel(first, rows, columns, cap, words_ref, *refs):
    if first:
        cores_ref, mine_ref, raw_ref, inflow_ref, weight_ref, spam_ref, want_ref, keys_ref, lists_ref, *refs = refs
    else:
        lists_ref, inflow_ref, rank_ref, *refs = refs
    landed, table, partial, exps, gains, packed, inbox, own, send, recv, chain_send, chain_recv, *refs = refs
    r, z = lax.axis_index("row"), lax.axis_index("col")
    blocks, part, size = partial.shape
    seeds = inflow_ref.shape[1]
    halves = seeds // part
    bits = blocks.bit_length() - 1
    tail_at = cap * part
    spans = []
    for h in range(halves):
        start = spans[-1][0] + spans[-1][1] if spans else 0
        spans.append((start, cap * part + (landed.shape[2] - cap * seeds if h == 0 else 0)))
    data = blocks * part
    longs = [data + blocks * (4 if first and h == 0 else 1) for h in range(halves)]
    others = [lax.rem(r + d, rows) for d in range(1, rows)]
    targets = order_of(z, columns)
    block_iota = lax.broadcasted_iota(jnp.int32, (blocks, size), 0)
    greet(
        [((t, z), t >= 0) for t in others]
        + (
            [((r, lax.rem(z + d, columns)), z >= 0) for d in range(1, columns)] if first
            else [((r, z - 1), z > 0), ((r, z + 1), z < columns - 1)]
        )
    )

    def across(i, h, t, origin):
        at = pl.ds(*spans[h])
        return pltpu.make_async_remote_copy(
            src_ref=words_ref.at[t * columns + targets[i], at], dst_ref=landed.at[i, origin, at],
            send_sem=send.at[i, h, t], recv_sem=recv.at[i, h, origin],
            device_id=(t, z), device_id_type=MESH,
        )

    def mine(i):
        return pltpu.make_async_copy(
            words_ref.at[r * columns + targets[i]], landed.at[i, r], own.at[i]
        )

    def chain(i, h, side):
        at = pl.ds(0, longs[h])
        return pltpu.make_async_remote_copy(
            src_ref=packed.at[min(i, columns - 2), h, at], dst_ref=inbox.at[side, targets[i], h, at],
            send_sem=chain_send.at[min(i, columns - 2), h], recv_sem=chain_recv.at[side, targets[i], h],
            device_id=(r, z + 1 - 2 * side), device_id_type=MESH,
        )

    def to_int16(value):
        return value.astype(jnp.int32).astype(jnp.int16)

    def to_float(value):
        return value.astype(jnp.int32).astype(F32)

    if first:
        known_send, known_recv, tally, *sems = refs
        spread = Spread(rows, columns, keys_ref, lists_ref, sems)

        def know(t, origin):
            return pltpu.make_async_remote_copy(
                src_ref=mine_ref, dst_ref=want_ref.at[origin],
                send_sem=known_send.at[t], recv_sem=known_recv.at[origin],
                device_id=(t, z), device_id_type=MESH,
            )

        for t in others:
            know(t, r).start()
        want_ref[r] = mine_ref[...]

    def launch(i):
        for h in range(halves):
            for t in others:
                across(i, h, t, r).start()
        mine(i).start()

    launch(0)
    launch(1)
    if first:
        keys_ref[...] = sort_hosts(columns, blocks, raw_ref[...])
        spread.begin()
    else:
        peers, lines, _ = lists_ref.shape
        groups = seeds // lines
        turns = (columns - 1) * halves - 1
        load = -(-peers // turns)

        def find(q, _):
            keys = lists_ref[q].astype(jnp.int32) & (blocks * size - 1)
            for g, spots in enumerate(find_ranks(groups, blocks, keys)):
                rank_ref[q, g * lines : (g + 1) * lines, :] = spots
            return 0

    pieces = min(8, (columns - 1) * halves)
    for i in range(columns):
        mine(i).wait()
        side = jnp.where(targets[i] > z, 0, 1)
        joined = jnp.where(targets[i] > z, z > 0, z < columns - 1)
        cols = jnp.zeros((blocks, size), F32)
        for h in range(halves):
            for t in others:
                across(i, h, t, t).wait_recv()
            if h == 0:
                def weigh(q, cols):
                    tail = landed[i, q, tail_at : spans[0][1], :].astype(jnp.int32)
                    for c in range(cap):
                        word = tail[c : c + 1, :]
                        hit = block_iota == (word & (blocks - 1))
                        scale = jnp.exp2((word >> bits).astype(F32) - WORD)
                        table[q * cap + c] = jnp.where(
                            hit, jnp.broadcast_to(scale, (blocks, size)), F32(0)
                        )
                        if first:
                            f, high, low = (
                                tail[cap + 3 * c + k : cap + 3 * c + k + 1, :].astype(F32) for k in range(3)
                            )
                            col = (high + low * F32(2.0**-WORD)) * jnp.exp2(f - WORD)
                            cols = cols + jnp.where(hit, jnp.broadcast_to(col, (blocks, size)), F32(0))
                    return cols

                cols = lax.fori_loop(0, rows, weigh, cols, unroll=4)

            first_row = spans[h][0]

            def strip(k, _):
                at = pl.multiple_of(k * 16, 16)

                def add(q, sums):
                    sums = list(sums)
                    for c in range(cap):
                        spot = pl.multiple_of(first_row + c * part + at, 16)
                        value = to_float(landed[i, q, pl.ds(spot, 16), :])
                        for b in range(blocks):
                            sums[b] = sums[b] + value * table[q * cap + c, b : b + 1, :]
                    return tuple(sums)

                sums = lax.fori_loop(0, rows, add, (jnp.zeros((16, size), F32),) * blocks)
                for b in range(blocks):
                    partial[b, pl.ds(at, 16), :] = sums[b]
                return 0

            lax.fori_loop(0, part // 16, strip, 0)

            def join(way):
                chain(i, h, way).wait_recv()
                exps[...] = jnp.exp2(to_float(inbox[way, targets[i], h, data : data + blocks, :]) - WORD)

                def one(b, _):
                    got = to_float(inbox[way, targets[i], h, pl.ds(pl.multiple_of(b * part, part), part), :])
                    partial[b] += got * exps[pl.ds(b, 1), :]
                    return 0

                lax.fori_loop(0, blocks, one, 0, unroll=4)

            def join_cols(way):
                f, high, low = (
                    to_float(inbox[way, targets[i], h, data + (k + 1) * blocks : data + (k + 2) * blocks, :])
                    for k in range(3)
                )
                colsum[...] += (high + low * F32(2.0**-WORD)) * jnp.exp2(f - WORD)

            if first and h == 0:
                colsum = weight_ref
                colsum[...] = cols
            if i < columns - 1:
                @pl.when(joined)
                def _():
                    join(side)
                    if first and h == 0:
                        join_cols(side)

                def peak(b, _):
                    exps[pl.ds(b, 1), :] = jnp.max(jnp.abs(partial[b]), axis=0, keepdims=True)
                    return 0

                def squeeze(b, _):
                    packed[i, h, pl.ds(pl.multiple_of(b * part, part), part), :] = to_int16(
                        to_words(partial[b] * gains[pl.ds(b, 1), :])
                    )
                    return 0

                lax.fori_loop(0, blocks, peak, 0, unroll=8)
                exps[...] = exponent_of(exps[...])
                gains[...] = jnp.exp2(WORD - exps[...])
                lax.fori_loop(0, blocks, squeeze, 0, unroll=8)
                packed[i, h, data : data + blocks, :] = to_int16(exps[...])
                if first and h == 0:
                    col = colsum[...]
                    f = exponent_of(jnp.abs(col))
                    scaled = col * jnp.exp2(WORD - f)
                    high = to_words(scaled)
                    for k, row in enumerate((f, high, to_words((scaled - high) * F32(2.0**WORD)))):
                        packed[i, h, data + (k + 1) * blocks : data + (k + 2) * blocks, :] = to_int16(row)
                chain(i, h, side).start()
            else:
                for way, there in ((0, z > 0), (1, z < columns - 1)):
                    @pl.when(there)
                    def _():
                        join(way)
                        if first and h == 0:
                            join_cols(way)

                def finish(b, _):
                    inflow_ref[b, h * part : (h + 1) * part, :] = partial[b]
                    return 0

                lax.fori_loop(0, blocks, finish, 0, unroll=4)
                if first and h == 0:
                    colsum[...] += F32(1)
            step = i * halves + h
            if first and step < columns - 1:
                spread.hop(step + 1)
            if h == min(columns, halves) - 1 and i + 2 < columns:
                launch(i + 2)
            if first and step == (columns - 2) * halves:
                spread.collect()
            if not first and 0 <= step - halves < turns:
                begin, end = (min(peers, k * load) for k in (step - halves, step - halves + 1))
                lax.fori_loop(begin, end, find, 0, unroll=3 if (end - begin) % 3 == 0 else 2)
            if first and 0 <= step - halves < pieces:
                count_seeds(columns, cores_ref, tally, step - halves, pieces)
            if first and step == halves + pieces:
                spread_seeds(cores_ref.shape[1], tally, spam_ref)

    if first:
        for t in others:
            know(t, r).wait_send()
            know(t, t).wait_recv()
        spread.finish()
    for i in range(columns):
        for h in range(halves):
            for t in others:
                across(i, h, t, r).wait_send()
            if i < columns - 1:
                chain(i, h, jnp.where(targets[i] > z, 0, 1)).wait_send()


def trust_kernel(inflow, good_ref, spam_ref, weight_ref, keys_ref, trust_ref, shield_ref, vals_ref):
    blocks, seeds, size = inflow.shape
    lines = keys_ref.shape[0]
    groups = seeds // lines
    keys = keys_ref[...].astype(jnp.int32) & (blocks * size - 1)
    lanes = keys // blocks
    block = keys & (blocks - 1)
    part = lax.broadcasted_iota(jnp.int32, (lines, size), 1) // (size // groups)

    def one(b, vals):
        trust = F32(0.85) * inflow[b] + F32(0.15) * good_ref[b]
        trust_ref[pl.ds(pl.multiple_of(b * size, size), size), :] = jnp.transpose(trust)
        shield = F32(1) / (F32(1) + trust)
        shield_ref[b] = shield
        share = (shield * spam_ref[b] / weight_ref[pl.ds(b, 1), :]).astype(BF16).astype(F32)
        for g in range(groups):
            got = take(share[g * lines : (g + 1) * lines, :], lanes)
            vals = jnp.where((block == b) & (part == g), got, vals)
        return vals

    vals = lax.fori_loop(0, blocks, one, jnp.zeros((lines, size), F32), unroll=2)
    vals_ref[...] = vals.astype(BF16)


def pull_kernel(last, *refs):
    if last:
        src_ref, slot_ref, fetched_ref, spam_ref, tiles_ref, out_ref, acc = refs
    else:
        (src_ref, slot_ref, block_ref, lists_ref, vals_ref, rank_ref, spam_ref, shield_ref, weight_ref,
         tiles_ref, out_ref, acc, fetched_ref, codes, bounds, sem) = refs
    step = pl.program_id(0)
    per_step = tiles_ref.shape[0]
    size = acc.shape[2]

    @pl.when(step == 0)
    def _():
        acc[...] = jnp.zeros_like(acc)
        if not last:
            blocks = acc.shape[0]
            codes[...] = lists_ref[:, 0, :].astype(jnp.int32) // (blocks * size)
            copy = pltpu.make_async_copy(codes, bounds, sem)
            copy.start()
            copy.wait()
            expand(
                block_ref.shape[0] // lists_ref.shape[0], block_ref, lists_ref, vals_ref, rank_ref,
                blocks, bounds, fetched_ref,
            )

    def some(g, _):
        products = []
        for k in range(GROUP):
            n = step * per_step + g * GROUP + k
            tile, got = tiles_ref[g * GROUP + k], fetched_ref[slot_ref[n]]
            if last:
                products.append(jnp.dot(tile, got, preferred_element_type=F32))
            else:
                products.append(
                    lax.dot_general(got, tile, (((1,), (1,)), ((), ())), preferred_element_type=F32)
                )
        for k in range(GROUP):
            acc[src_ref[step * per_step + g * GROUP + k]] += products[k]
        return 0

    lax.fori_loop(0, per_step // GROUP, some, 0)

    @pl.when(step == pl.num_programs(0) - 1)
    def _():
        def distrust(b):
            return F32(0.85) * acc[b] + F32(0.15) * spam_ref[b]

        if last:
            def one(b, _):
                out_ref[pl.ds(pl.multiple_of(b * size, size), size), :] = distrust(b)
                return 0

            lax.fori_loop(0, acc.shape[0], one, 0, unroll=2)
        else:
            shares(shield_ref, weight_ref, distrust, out_ref)


def start_kernel(columns, good_ref, spam_ref, tiles_ref, count_ref, list_ref, near_ref, tally, sem):
    load = pltpu.make_async_copy(tiles_ref, near_ref, sem)
    load.start()
    list_ref[...] = jnp.transpose(spam_ref[...].astype(F32)).astype(jnp.int32)
    count_seeds(columns, good_ref, tally)
    spread_seeds(good_ref.shape[1], tally, count_ref)
    load.wait()


def body(columns, tiles, tile_src, tile_slot, slot_block, out_degree, good_seeds, spam_cores):
    tile_count, size, _ = tiles.shape
    here = lambda x: pltpu.with_memory_space_constraint(x, pltpu.HBM)
    hosts = out_degree.shape[0]
    blocks = hosts // size
    seeds = good_seeds.shape[0]
    slots = slot_block.shape[0]
    peers = lax.axis_size(AXES)
    cap = slots // peers
    tail = -(-4 * cap // 16) * 16
    steps = 1
    shape = jax.ShapeDtypeStruct
    vector = (blocks, seeds, size)
    degree = out_degree.reshape(blocks, 1, size)

    rows = peers // columns
    part = seeds // HALVES
    count = spam_cores.shape[1]
    groups = seeds // count
    lines = seeds // groups
    good, spam_list, tiles = pl.pallas_call(
        functools.partial(start_kernel, columns),
        out_shape=(
            shape(vector, F32), shape(spam_cores.shape, jnp.int32), shape(tiles.shape, BF16),
        ),
        in_specs=[VM, VM, ANY],
        out_specs=(VM, VM, VM),
        scratch_shapes=[pltpu.VMEM((seeds, blocks, size), F32), pltpu.SemaphoreType.DMA],
        compiler_params=PLAIN,
        cost_estimate=pl.CostEstimate(
            flops=2 * seeds * good_seeds.size * (blocks + size), transcendentals=0,
            bytes_accessed=24 << 20,
        ),
    )(here(good_seeds), here(spam_cores.T), here(tiles))

    tile_spec = VM
    words = shape((peers, cap * size + tail, size), jnp.int16)
    outgoing = pl.pallas_call(
        functools.partial(push_kernel, True, cap, part),
        grid=(steps,),
        out_shape=words,
        in_specs=[SM, SM, SM, VM, VM, tile_spec],
        out_specs=VM,
        scratch_shapes=[
            pltpu.VMEM((slots, seeds + 16, size), F32),
            pltpu.VMEM((blocks, seeds + 16, size), BF16),
        ],
        compiler_params=PLAIN,
    )(here(tile_src), here(tile_slot), here(slot_block), good, here(degree), tiles)

    dma = pltpu.SemaphoreType.DMA
    spread_sems = [
        dma((columns,)), dma((columns,)), dma((rows, columns)), dma((rows, columns)),
        dma((rows, columns)), dma((rows, columns)),
    ]

    def reduce(first, words_in, *rest):
        long = blocks * part + blocks * (4 if first else 1)
        outs = (
            shape(vector, F32), shape((blocks, size), F32), shape(vector, F32),
            shape((rows, 1, slots), jnp.int32), shape((lines, size), jnp.int16),
            shape((peers, lines, size), jnp.int16),
        )
        if not first:
            outs = (shape(vector, F32), shape((peers, seeds, size), jnp.int32))
        return pl.pallas_call(
            functools.partial(reduce_kernel, first, rows, columns, cap),
            out_shape=outs,
            in_specs=[ANY, VM, VM, VM] if first else [ANY, VM],
            out_specs=(VM,) * len(outs),
            scratch_shapes=[
                pltpu.VMEM((columns, rows, cap * size + tail, size), jnp.int16),
                pltpu.VMEM((rows * cap, blocks, size), F32),
                pltpu.VMEM((blocks, part, size), F32),
                pltpu.VMEM((blocks, size), F32),
                pltpu.VMEM((blocks, size), F32),
                pltpu.VMEM((columns - 1, HALVES, long, size), jnp.int16),
                pltpu.VMEM((2, columns, HALVES, long, size), jnp.int16),
                dma((columns,)),
                dma((columns, HALVES, rows)),
                dma((columns, HALVES, rows)),
                dma((columns - 1, HALVES)),
                dma((2, columns, HALVES)),
                *([dma((rows,)), dma((rows,)), pltpu.VMEM((seeds, blocks, size), F32), *spread_sems] if first else []),
            ],
            compiler_params=pltpu.CompilerParams(
                collective_id=1 if first else 2, has_side_effects=True,
                vmem_limit_bytes=LIMIT,
            ),
        )(words_in, *rest)

    inflow, weight, spam, want, keys, lists = reduce(
        True, outgoing, spam_list, slot_block.reshape(1, slots), spam_cores.T
    )
    outgoing = pl.pallas_call(
        functools.partial(push_kernel, False, cap, part),
        grid=(steps,),
        out_shape=words,
        in_specs=[SM, SM, SM, VM, VM, VM, tile_spec],
        out_specs=VM,
        scratch_shapes=[
            pltpu.VMEM((slots, seeds, size), F32),
            pltpu.VMEM(vector, BF16),
        ],
        compiler_params=PLAIN,
    )(tile_src, tile_slot, slot_block, inflow, good, degree, tiles)
    inflow, ranks = reduce(False, outgoing, lists)
    fetch = pl.pallas_call(
        functools.partial(fetch_kernel, rows, columns, cap),
        out_shape=shape((slots, seeds, size), BF16),
        in_specs=[SM, VM],
        out_specs=VM,
        scratch_shapes=[
            *[pltpu.VMEM((blocks, size // PARTS, seeds), BF16)] * ((2 * columns - 2) * PARTS),
            pltpu.VMEM((rows, columns * cap, size, seeds), BF16),
            pltpu.SemaphoreType.DMA(((2 * columns - 2) * PARTS,)),
            pltpu.SemaphoreType.DMA(((2 * columns - 2) * PARTS,)),
            pltpu.SemaphoreType.DMA((rows, columns * PARTS)),
            pltpu.SemaphoreType.DMA((rows, columns * PARTS)),
        ],
        compiler_params=pltpu.CompilerParams(collective_id=0, has_side_effects=True, vmem_limit_bytes=LIMIT),
    )
    trust, shield, vals = pl.pallas_call(
        trust_kernel,
        out_shape=(shape((hosts, seeds), F32), shape(vector, F32), shape((lines, size), BF16)),
        in_specs=[VM, VM, VM, VM, VM],
        out_specs=(VM, VM, VM),
        compiler_params=PLAIN,
    )(inflow, good, spam, weight, keys)
    vals, turned = pl.pallas_call(
        functools.partial(value_kernel, rows, columns),
        out_shape=(shape((peers, lines, size), BF16), shape(vector, F32)),
        in_specs=[VM, VM],
        out_specs=(VM, VM),
        scratch_shapes=spread_sems,
        compiler_params=pltpu.CompilerParams(
            collective_id=3, has_side_effects=True, vmem_limit_bytes=LIMIT
        ),
    )(vals, spam)
    share = pl.pallas_call(
        functools.partial(pull_kernel, False),
        grid=(steps,),
        out_shape=shape(vector, BF16),
        in_specs=[SM, SM, SM, VM, VM, VM, VM, VM, VM, tile_spec],
        out_specs=VM,
        scratch_shapes=[
            pltpu.VMEM(vector, F32),
            pltpu.VMEM((slots, seeds, size), BF16),
            pltpu.VMEM((peers, size), jnp.int32),
            pltpu.SMEM((peers, size), jnp.int32),
            pltpu.SemaphoreType.DMA,
        ],
        compiler_params=PLAIN,
    )(tile_src, tile_slot, slot_block, lists, vals, ranks, spam, shield, weight, tiles)
    fetched = fetch(want, share)
    distrust = pl.pallas_call(
        functools.partial(pull_kernel, True),
        grid=(steps,),
        out_shape=shape((hosts, seeds), F32),
        in_specs=[SM, SM, VM, VM, tile_spec],
        out_specs=VM,
        scratch_shapes=[pltpu.VMEM(vector, F32)],
        compiler_params=PLAIN,
    )(tile_src, tile_slot, fetched, turned, tiles)
    return trust, distrust


def solution(mesh):
    in_specs = (
        P(AXES, None, None),
        P(AXES),
        P(AXES),
        P(AXES),
        P(AXES),
        P(None, AXES),
        P(None, AXES),
    )
    out_specs = (P(AXES, None), P(AXES, None))
    return jax.shard_map(
        functools.partial(body, mesh.shape["col"]),
        mesh=mesh, in_specs=in_specs, out_specs=out_specs, check_vma=False,
    )
```

```python
import functools

import jax
import jax.numpy as jnp
from jax import lax
from jax.experimental import pallas as pl
from jax.experimental.pallas import tpu as pltpu
from jax.sharding import PartitionSpec as P

AXES = ("row", "col")
VM = pl.BlockSpec(memory_space=pltpu.VMEM)
SM = pl.BlockSpec(memory_space=pltpu.SMEM)
LIMIT = 28 << 20
ANY = pl.BlockSpec(memory_space=pl.ANY)
F32 = jnp.float32
BF16 = jnp.bfloat16
PLAIN = pltpu.CompilerParams(vmem_limit_bytes=LIMIT)
WORD = 15
GROUP = 64
HALVES = 4
PARTS = 2
LAYERS = 6
MORE = 2
MESH = pl.DeviceIdType.MESH


def count_seeds(columns, source, tally, step=0, pieces=1):
    seeds, blocks, size = tally.shape
    hosts = blocks * size
    base = (lax.axis_index("row") * columns + lax.axis_index("col")) * hosts
    count = source.shape[1]
    block_iota = lax.broadcasted_iota(jnp.int32, (blocks, count), 0) * size
    lane_iota = lax.broadcasted_iota(jnp.int32, (size, count), 0)

    def one(s, _):
        local = source[pl.ds(s, 1), :] - base
        shifted = local - block_iota
        inside = jnp.where((shifted >= 0) & (shifted < size), F32(1), F32(0)).astype(BF16)
        start = jnp.max(jnp.where(local >= block_iota, block_iota, 0), axis=0, keepdims=True)
        lane = jnp.where(lane_iota == local - start, F32(1), F32(0)).astype(BF16)
        tally[s] = lax.dot_general(
            inside, lane, (((1,), (1,)), ((), ())), preferred_element_type=F32
        )
        return 0

    share = seeds // pieces
    lax.fori_loop(step * share, (step + 1) * share, one, 0, unroll=16)


def spread_seeds(count, tally, target):
    blocks, _, size = target.shape
    factor = F32(blocks * size / count)
    for b in range(blocks):
        target[b] = tally[:, b, :] * factor


def exponent_of(peak):
    return jnp.floor(jnp.log2(jnp.maximum(peak, F32(2.0**-100)))) + F32(1)


def to_words(value):
    return jnp.clip(jnp.floor(value + F32(0.5)), F32(-32767), F32(32767))


def pack(first, cap, part, bits, acc, block_ref, out_ref):
    peers = out_ref.shape[0]
    size = acc.shape[2]
    halves = size // part
    tail = out_ref.shape[1] - cap * size

    def one(p, _):
        exps, cols = [], []
        for c in range(cap):
            n = p * cap + c
            value = acc[n, :size, :]
            e = exponent_of(jnp.max(jnp.abs(value), axis=0, keepdims=True))
            words = to_words(value * jnp.exp2(WORD - e)).astype(jnp.int32).astype(jnp.int16)
            for h in range(halves):
                at = (h * cap + c) * part + (tail if h else 0)
                out_ref[p, at : at + part, :] = words[h * part : (h + 1) * part, :]
            exps.append(e * F32(2**bits) + block_ref[n].astype(F32))
            if first:
                col = acc[n, size : size + 8, :][:1, :]
                f = exponent_of(jnp.abs(col))
                scaled = col * jnp.exp2(WORD - f)
                high = to_words(scaled)
                cols += [f, high, to_words((scaled - high) * F32(2.0**WORD))]
        rows = exps + cols
        if tail > len(rows):
            rows.append(jnp.zeros((tail - len(rows), size), F32))
        at = cap * part
        out_ref[p, at : at + tail, :] = jnp.concatenate(rows, axis=0).astype(jnp.int32).astype(jnp.int16)
        return 0

    lax.fori_loop(0, peers, one, 0, unroll=4)


def push_kernel(first, cap, part, *refs):
    if first:
        src_ref, slot_ref, block_ref, good_ref, degree_ref, tiles_ref, out_ref, acc, scaled = refs
    else:
        src_ref, slot_ref, block_ref, inflow, good_ref, degree_ref, tiles_ref, out_ref, acc, scaled = refs
    step = pl.program_id(0)
    blocks, seeds, size = good_ref.shape
    per_step = tiles_ref.shape[0]

    @pl.when(step == 0)
    def _():
        acc[...] = jnp.zeros_like(acc)
        def one(b, _):
            degree = degree_ref[b].astype(F32)
            trust = good_ref[b]
            if not first:
                trust = F32(0.85) * inflow[b] + F32(0.15) * trust
            scaled[b, :seeds, :] = (trust / degree).astype(BF16)
            if first:
                scaled[b, seeds:, :] = jnp.ones((scaled.shape[1] - seeds, size), BF16)
            return 0

        lax.fori_loop(0, blocks, one, 0)

    def some(g, _):
        products = []
        for k in range(GROUP):
            n = step * per_step + g * GROUP + k
            products.append(
                jnp.dot(scaled[src_ref[n]], tiles_ref[g * GROUP + k], preferred_element_type=F32)
            )
        for k in range(GROUP):
            acc[slot_ref[step * per_step + g * GROUP + k]] += products[k]
        return 0

    lax.fori_loop(0, per_step // GROUP, some, 0)

    @pl.when(step == pl.num_programs(0) - 1)
    def _():
        pack(first, cap, part, blocks.bit_length() - 1, acc, block_ref, out_ref)


def shares(shield_ref, weight_ref, start_of, share_ref):
    def one(b, _):
        weight = weight_ref[pl.ds(b, 1), :]
        share_ref[b] = jnp.transpose(shield_ref[b] * start_of(b) / weight).astype(BF16)
        return 0

    lax.fori_loop(0, share_ref.shape[0], one, 0, unroll=2)


def greet(devices):
    barrier = pltpu.get_barrier_semaphore()
    for device, there in devices:
        @pl.when(there)
        def _():
            pl.semaphore_signal(barrier, inc=1, device_id=device, device_id_type=MESH)
    pl.semaphore_wait(barrier, sum(jnp.where(there, 1, 0) for _, there in devices))


def fetch_kernel(rows, columns, cap, want_ref, share_ref, fetched_ref, *scratch):
    line = 2 * (columns - 1)
    held, (picked, line_send, line_recv, send, recv) = scratch[: line * PARTS], scratch[line * PARTS :]
    r, z = lax.axis_index("row"), lax.axis_index("col")
    others = [lax.rem(r + d, rows) for d in range(1, rows)]
    sides = (-1, 1)
    inside = {side: (z + side >= 0) & (z + side < columns) for side in sides}
    tall = share_ref.shape[1] // PARTS
    greet([((t, z), t >= 0) for t in others] + [((r, z + side), inside[side]) for side in sides])

    def place(side, d, k):
        return (2 * (d - 1) + (0 if side < 0 else 1)) * PARTS + k

    def pass_on(source, d, side, k):
        slot = place(-side, d, k)
        return pltpu.make_async_remote_copy(
            src_ref=source, dst_ref=held[slot],
            send_sem=line_send.at[slot], recv_sem=line_recv.at[slot],
            device_id=(r, z + side), device_id_type=MESH,
        )

    def own(k):
        return share_ref.at[:, pl.ds(k * tall, tall)]

    def serve(t, origin, k, source, sender):
        span = pl.ds(k * tall, tall)
        return pltpu.make_async_remote_copy(
            src_ref=picked.at[t, pl.ds(origin * cap, cap), span],
            dst_ref=fetched_ref.at[pl.ds((source * columns + origin) * cap, cap), span],
            send_sem=send.at[t, origin * PARTS + k], recv_sem=recv.at[sender, origin * PARTS + k],
            device_id=(t, z), device_id_type=MESH,
        )

    def spread(source, origin, k):
        span = slice(k * tall, (k + 1) * tall)

        def pick(t, j):
            n = want_ref[t, 0, (r * columns + origin) * cap + j]
            return source[n, span, :] if source.shape[1] > tall else source[n]

        before = None
        for t in others:
            for j in range(cap):
                picked[t, origin * cap + j, span, :] = pick(t, j)
            if before is not None:
                serve(before, origin, k, r, r).start()
            before = t
        for j in range(cap):
            fetched_ref[(r * columns + origin) * cap + j, span, :] = pick(r, j)
        serve(before, origin, k, r, r).start()

    for k in range(PARTS):
        for side in sides:
            @pl.when(inside[side])
            def _():
                pass_on(own(k), 1, side, k).start()
    for k in range(PARTS):
        spread(share_ref, z, k)
    for d in range(1, columns):
        for k in range(PARTS):
            for side in sides:
                origin = z + side * d

                @pl.when((origin >= 0) & (origin < columns))
                def _():
                    here = held[place(side, d, k)]
                    pass_on(here, d, -side, k).wait_recv()

                    if d < columns - 1:
                        @pl.when(inside[-side])
                        def _():
                            pass_on(here, d + 1, -side, k).start()

                    spread(here, origin, k)
    for origin in range(columns):
        for k in range(PARTS):
            for t in others:
                serve(t, origin, k, r, r).wait_send()
                serve(t, origin, k, t, t).wait_recv()
    for d in range(columns - 1):
        for k in range(PARTS):
            for side in sides:
                origin = z - side * d

                @pl.when((origin >= 0) & (origin < columns) & inside[side])
                def _():
                    pass_on(held[0], d + 1, side, k).wait_send()


def take(table, index):
    return jnp.take_along_axis(table, index, axis=1, mode="promise_in_bounds")


def find_ranks(groups, blocks, keys):
    lines, size = keys.shape
    count = size // groups
    least = lax.broadcasted_iota(jnp.int32, (lines, size), 1) * blocks
    spots = [jnp.full((lines, size), count * g, jnp.int32) for g in range(groups)]
    step = count // 2
    while True:
        probes = [take(keys, spot + (max(step, 1) - 1)) for spot in spots]
        spots = [spot + jnp.where(probe < least, max(step, 1), 0) for spot, probe in zip(spots, probes)]
        if step == 0:
            return spots
        step //= 2


def ends_of(g, groups, spots):
    lines, size = spots.shape
    lane = lax.broadcasted_iota(jnp.int32, (lines, size), 1)
    after = pltpu.roll(spots, size - 1, 1)
    return jnp.where(lane == size - 1, (size // groups) * (g + 1), after)


def sort_hosts(columns, blocks, raw):
    count, seeds = raw.shape
    groups = seeds // count
    lines = seeds // groups
    base = (lax.axis_index("row") * columns + lax.axis_index("col")) * (blocks * seeds)
    local = (raw - base).astype(F32)
    stacked = jnp.concatenate(
        [local] + [pltpu.roll(local, seeds - g * lines, 1) for g in range(1, groups)], axis=0
    )
    hosts = jnp.transpose(stacked)[:lines, :].astype(jnp.int32)
    keys = ((hosts & (seeds - 1)) * blocks + hosts // seeds).astype(F32)
    lane = lax.broadcasted_iota(jnp.int32, keys.shape, 1)
    k = 2
    while k <= count:
        j = k // 2
        while j:
            other = take(keys, lane ^ j)
            rising = ((lane & k) == 0) | (k == count)
            lower = ((lane & j) == 0) == rising
            keys = jnp.where(lower, jnp.minimum(keys, other), jnp.maximum(keys, other))
            j //= 2
        k *= 2
    keys = keys.astype(jnp.int32)
    spots = find_ranks(groups, blocks, keys)
    most = functools.reduce(
        jnp.maximum, [ends_of(g, groups, spot) - spot for g, spot in enumerate(spots)]
    ).astype(F32)
    most = jnp.max(jnp.max(most, axis=1, keepdims=True), axis=0, keepdims=True).astype(jnp.int32)
    code = jnp.where(most > LAYERS, 1, 0) + jnp.where(most > LAYERS + MORE, 1, 0)
    return (keys + code * (blocks * seeds)).astype(jnp.int16)


class Spread:
    def __init__(self, rows, columns, own, out, sems):
        self.rows, self.columns, self.own, self.out = rows, columns, own, out
        self.line_send, self.line_recv, self.plane_send, self.plane_recv, self.pair_send, self.pair_recv = sems
        r, z = lax.axis_index("row"), lax.axis_index("col")
        self.r, self.z = r, z
        self.twin = r + 1 - 2 * lax.rem(r, 2)
        self.mates = [lax.rem(r + d, rows) for d in range(2, rows, 2)]
        self.others = [self.twin] + [lax.rem(self.twin + d, rows) for d in range(2, rows, 2)]
        self.peers = [lax.rem(z + d, columns) for d in range(1, columns)]

    def send(self, source, row, origin, sends, recvs, to):
        return pltpu.make_async_remote_copy(
            src_ref=source, dst_ref=self.out.at[row * self.columns + origin],
            send_sem=sends, recv_sem=recvs, device_id=to, device_id_type=MESH,
        )

    def place(self, row, origin):
        return self.out.at[row * self.columns + origin]

    def line(self, d, origin):
        return self.send(
            self.own, self.r, origin, self.line_send.at[d], self.line_recv.at[origin],
            (self.r, lax.rem(self.z + d, self.columns)),
        )

    def plane(self, source, t, row, origin):
        return self.send(
            source, row, origin, self.plane_send.at[t, origin], self.plane_recv.at[row, origin],
            (t, self.z),
        )

    def pair(self, source, row, origin):
        return self.send(
            source, row, origin, self.pair_send.at[row, origin], self.pair_recv.at[row, origin],
            (self.twin, self.z),
        )

    def across(self, source, origin):
        for t in self.mates:
            self.plane(source, t, self.r, origin).start()
        self.pair(source, self.r, origin).start()

    def begin(self):
        for d in range(1, self.columns):
            self.line(d, self.z).start()
        self.across(self.own, self.z)
        self.out[self.r * self.columns + self.z] = self.own[...]

    def hop(self, d):
        origin = lax.rem(self.z + d, self.columns)
        self.line(d, origin).wait_recv()
        self.across(self.place(self.r, origin), origin)

    def collect(self):
        for t in self.mates:
            for origin in range(self.columns):
                here = self.place(t, origin)
                self.plane(here, t, t, origin).wait_recv()
                self.pair(here, t, origin).start()

    def finish(self):
        for t in self.others:
            for origin in range(self.columns):
                self.pair(self.place(t, origin), t, origin).wait_recv()
        for d in range(1, self.columns):
            self.line(d, self.z).wait_send()
        for origin in range(self.columns):
            for t in self.mates:
                self.plane(self.own, t, self.r, origin).wait_send()
                self.pair(self.own, t, origin).wait_send()
            self.pair(self.own, self.r, origin).wait_send()


def value_kernel(rows, columns, own_ref, spam_ref, vals_ref, turned_ref, *sems):
    spread = Spread(rows, columns, own_ref, vals_ref, sems)
    greet(
        [((t, spread.z), t >= 0) for t in spread.mates + [spread.twin]]
        + [((spread.r, y), y >= 0) for y in spread.peers]
    )
    spread.begin()

    def turn(b, _):
        turned_ref[b] = jnp.transpose(spam_ref[b])
        return 0

    share = -(-spam_ref.shape[0] // columns)
    for d in range(columns):
        if d:
            spread.hop(d)
        first, end = (min(spam_ref.shape[0], k * share) for k in (d, d + 1))
        lax.fori_loop(first, end, turn, 0)
    spread.collect()
    spread.finish()


def expand(cap, block_ref, lists_ref, vals_ref, rank_ref, blocks, bounds, fetched):
    peers, lines, size = lists_ref.shape
    groups = fetched.shape[1] // lines
    tall = 32

    def paint(q, low, high, fresh):
        tags = [
            F32(1) + (block_ref[q * cap + c] + 1).astype(F32) * F32(2.0**-14) for c in range(cap)
        ]

        def some(i, _):
            at = pl.multiple_of(i * tall, tall)
            block = lists_ref[q, pl.ds(at, tall), :].astype(jnp.int32) & (blocks - 1)
            value = vals_ref[q, pl.ds(at, tall), :].astype(F32)
            marked = value * (F32(1) + (block + 1).astype(F32) * F32(2.0**-14))
            for g in range(groups):
                row = pl.multiple_of(g * lines + at, tall)
                spots = rank_ref[q, pl.ds(row, tall), :]
                ends = ends_of(g, groups, spots)

                def layer(j, outs):
                    spot = spots + j
                    live = spot < ends
                    got = jnp.where(live, take(marked, jnp.minimum(spot, size - 1)), F32(0))
                    plain = got.astype(BF16).astype(F32)
                    return tuple(
                        jnp.where(live & (plain * tag == got), plain, out) for tag, out in zip(tags, outs)
                    )

                if fresh:
                    outs = (jnp.zeros((tall, size), F32),) * cap
                else:
                    outs = tuple(
                        fetched[q * cap + c, pl.ds(row, tall), :].astype(F32) for c in range(cap)
                    )
                if high - low > LAYERS:
                    outs = lax.fori_loop(low, high, layer, outs)
                else:
                    for j in range(low, high):
                        outs = layer(j, outs)
                for c in range(cap):
                    fetched[q * cap + c, pl.ds(row, tall), :] = outs[c].astype(BF16)
            return 0

        lax.fori_loop(0, lines // tall, some, 0, unroll=2 if fresh else 1)

    def one(q, _):
        paint(q, 0, LAYERS, True)
        code = bounds[q, 0]

        @pl.when(code > 0)
        def _():
            paint(q, LAYERS, LAYERS + MORE, False)

        @pl.when(code > 1)
        def _():
            paint(q, LAYERS + MORE, size // groups, False)

        return 0

    lax.fori_loop(0, peers, one, 0)


def order_of(z, columns):
    table = []
    for plane in range(columns):
        line = []
        for k in range(columns):
            ahead = [t for t in (columns - 1 - k,) if t > plane]
            back = [t for t in (k,) if t < plane]
            line += ahead + back if 2 * plane < columns else back + ahead
        table.append(line + [plane])
    picks = []
    for i in range(columns):
        pick = z * 0
        for plane in range(columns):
            pick = pick + jnp.where(z == plane, table[plane][i], 0)
        picks.append(pick)
    return picks


def reduce_kernel(first, rows, columns, cap, words_ref, *refs):
    if first:
        cores_ref, mine_ref, raw_ref, inflow_ref, weight_ref, spam_ref, want_ref, keys_ref, lists_ref, *refs = refs
    else:
        lists_ref, inflow_ref, rank_ref, *refs = refs
    landed, table, partial, exps, gains, packed, inbox, own, send, recv, chain_send, chain_recv, *refs = refs
    r, z = lax.axis_index("row"), lax.axis_index("col")
    blocks, part, size = partial.shape
    seeds = inflow_ref.shape[1]
    halves = seeds // part
    bits = blocks.bit_length() - 1
    tail_at = cap * part
    spans = []
    for h in range(halves):
        start = spans[-1][0] + spans[-1][1] if spans else 0
        spans.append((start, cap * part + (landed.shape[2] - cap * seeds if h == 0 else 0)))
    data = blocks * part
    longs = [data + blocks * (4 if first and h == 0 else 1) for h in range(halves)]
    others = [lax.rem(r + d, rows) for d in range(1, rows)]
    targets = order_of(z, columns)
    block_iota = lax.broadcasted_iota(jnp.int32, (blocks, size), 0)
    greet(
        [((t, z), t >= 0) for t in others]
        + (
            [((r, lax.rem(z + d, columns)), z >= 0) for d in range(1, columns)] if first
            else [((r, z - 1), z > 0), ((r, z + 1), z < columns - 1)]
        )
    )

    def across(i, h, t, origin):
        at = pl.ds(*spans[h])
        return pltpu.make_async_remote_copy(
            src_ref=words_ref.at[t * columns + targets[i], at], dst_ref=landed.at[i, origin, at],
            send_sem=send.at[i, h, t], recv_sem=recv.at[i, h, origin],
            device_id=(t, z), device_id_type=MESH,
        )

    def mine(i):
        return pltpu.make_async_copy(
            words_ref.at[r * columns + targets[i]], landed.at[i, r], own.at[i]
        )

    def chain(i, h, side):
        at = pl.ds(0, longs[h])
        return pltpu.make_async_remote_copy(
            src_ref=packed.at[min(i, columns - 2), h, at], dst_ref=inbox.at[side, targets[i], h, at],
            send_sem=chain_send.at[min(i, columns - 2), h], recv_sem=chain_recv.at[side, targets[i], h],
            device_id=(r, z + 1 - 2 * side), device_id_type=MESH,
        )

    def to_int16(value):
        return value.astype(jnp.int32).astype(jnp.int16)

    def to_float(value):
        return value.astype(jnp.int32).astype(F32)

    if first:
        known_send, known_recv, tally, *sems = refs
        spread = Spread(rows, columns, keys_ref, lists_ref, sems)

        def know(t, origin):
            return pltpu.make_async_remote_copy(
                src_ref=mine_ref, dst_ref=want_ref.at[origin],
                send_sem=known_send.at[t], recv_sem=known_recv.at[origin],
                device_id=(t, z), device_id_type=MESH,
            )

        for t in others:
            know(t, r).start()
        want_ref[r] = mine_ref[...]

    def launch(i):
        for h in range(halves):
            for t in others:
                across(i, h, t, r).start()
        mine(i).start()

    launch(0)
    launch(1)
    if first:
        keys_ref[...] = sort_hosts(columns, blocks, raw_ref[...])
        spread.begin()
    else:
        peers, lines, _ = lists_ref.shape
        groups = seeds // lines
        turns = (columns - 1) * halves - 1
        load = -(-peers // turns)

        def find(q, _):
            keys = lists_ref[q].astype(jnp.int32) & (blocks * size - 1)
            for g, spots in enumerate(find_ranks(groups, blocks, keys)):
                rank_ref[q, g * lines : (g + 1) * lines, :] = spots
            return 0

    pieces = min(8, (columns - 1) * halves)
    for i in range(columns):
        mine(i).wait()
        side = jnp.where(targets[i] > z, 0, 1)
        joined = jnp.where(targets[i] > z, z > 0, z < columns - 1)
        cols = jnp.zeros((blocks, size), F32)
        for h in range(halves):
            for t in others:
                across(i, h, t, t).wait_recv()
            if h == 0:
                def weigh(q, cols):
                    tail = landed[i, q, tail_at : spans[0][1], :].astype(jnp.int32)
                    for c in range(cap):
                        word = tail[c : c + 1, :]
                        hit = block_iota == (word & (blocks - 1))
                        scale = jnp.exp2((word >> bits).astype(F32) - WORD)
                        table[q * cap + c] = jnp.where(
                            hit, jnp.broadcast_to(scale, (blocks, size)), F32(0)
                        )
                        if first:
                            f, high, low = (
                                tail[cap + 3 * c + k : cap + 3 * c + k + 1, :].astype(F32) for k in range(3)
                            )
                            col = (high + low * F32(2.0**-WORD)) * jnp.exp2(f - WORD)
                            cols = cols + jnp.where(hit, jnp.broadcast_to(col, (blocks, size)), F32(0))
                    return cols

                cols = lax.fori_loop(0, rows, weigh, cols, unroll=4)

            first_row = spans[h][0]

            def strip(k, _):
                at = pl.multiple_of(k * 16, 16)

                def add(q, sums):
                    sums = list(sums)
                    for c in range(cap):
                        spot = pl.multiple_of(first_row + c * part + at, 16)
                        value = to_float(landed[i, q, pl.ds(spot, 16), :])
                        for b in range(blocks):
                            sums[b] = sums[b] + value * table[q * cap + c, b : b + 1, :]
                    return tuple(sums)

                sums = lax.fori_loop(0, rows, add, (jnp.zeros((16, size), F32),) * blocks)
                for b in range(blocks):
                    partial[b, pl.ds(at, 16), :] = sums[b]
                return 0

            lax.fori_loop(0, part // 16, strip, 0)

            def join(way):
                chain(i, h, way).wait_recv()
                exps[...] = jnp.exp2(to_float(inbox[way, targets[i], h, data : data + blocks, :]) - WORD)

                def one(b, _):
                    got = to_float(inbox[way, targets[i], h, pl.ds(pl.multiple_of(b * part, part), part), :])
                    partial[b] += got * exps[pl.ds(b, 1), :]
                    return 0

                lax.fori_loop(0, blocks, one, 0, unroll=4)

            def join_cols(way):
                f, high, low = (
                    to_float(inbox[way, targets[i], h, data + (k + 1) * blocks : data + (k + 2) * blocks, :])
                    for k in range(3)
                )
                colsum[...] += (high + low * F32(2.0**-WORD)) * jnp.exp2(f - WORD)

            if first and h == 0:
                colsum = weight_ref
                colsum[...] = cols
            if i < columns - 1:
                @pl.when(joined)
                def _():
                    join(side)
                    if first and h == 0:
                        join_cols(side)

                def peak(b, _):
                    exps[pl.ds(b, 1), :] = jnp.max(jnp.abs(partial[b]), axis=0, keepdims=True)
                    return 0

                def squeeze(b, _):
                    packed[i, h, pl.ds(pl.multiple_of(b * part, part), part), :] = to_int16(
                        to_words(partial[b] * gains[pl.ds(b, 1), :])
                    )
                    return 0

                lax.fori_loop(0, blocks, peak, 0, unroll=8)
                exps[...] = exponent_of(exps[...])
                gains[...] = jnp.exp2(WORD - exps[...])
                lax.fori_loop(0, blocks, squeeze, 0, unroll=8)
                packed[i, h, data : data + blocks, :] = to_int16(exps[...])
                if first and h == 0:
                    col = colsum[...]
                    f = exponent_of(jnp.abs(col))
                    scaled = col * jnp.exp2(WORD - f)
                    high = to_words(scaled)
                    for k, row in enumerate((f, high, to_words((scaled - high) * F32(2.0**WORD)))):
                        packed[i, h, data + (k + 1) * blocks : data + (k + 2) * blocks, :] = to_int16(row)
                chain(i, h, side).start()
            else:
                for way, there in ((0, z > 0), (1, z < columns - 1)):
                    @pl.when(there)
                    def _():
                        join(way)
                        if first and h == 0:
                            join_cols(way)

                def finish(b, _):
                    inflow_ref[b, h * part : (h + 1) * part, :] = partial[b]
                    return 0

                lax.fori_loop(0, blocks, finish, 0, unroll=4)
                if first and h == 0:
                    colsum[...] += F32(1)
            step = i * halves + h
            if first and step < columns - 1:
                spread.hop(step + 1)
            if h == min(columns, halves) - 1 and i + 2 < columns:
                launch(i + 2)
            if first and step == (columns - 2) * halves:
                spread.collect()
            if not first and 0 <= step - halves < turns:
                begin, end = (min(peers, k * load) for k in (step - halves, step - halves + 1))
                lax.fori_loop(begin, end, find, 0, unroll=3 if (end - begin) % 3 == 0 else 2)
            if first and 0 <= step - halves < pieces:
                count_seeds(columns, cores_ref, tally, step - halves, pieces)
            if first and step == halves + pieces:
                spread_seeds(cores_ref.shape[1], tally, spam_ref)

    if first:
        for t in others:
            know(t, r).wait_send()
            know(t, t).wait_recv()
        spread.finish()
    for i in range(columns):
        for h in range(halves):
            for t in others:
                across(i, h, t, r).wait_send()
            if i < columns - 1:
                chain(i, h, jnp.where(targets[i] > z, 0, 1)).wait_send()


def trust_kernel(inflow, good_ref, spam_ref, weight_ref, keys_ref, trust_ref, shield_ref, vals_ref):
    blocks, seeds, size = inflow.shape
    lines = keys_ref.shape[0]
    groups = seeds // lines
    keys = keys_ref[...].astype(jnp.int32) & (blocks * size - 1)
    lanes = keys // blocks
    block = keys & (blocks - 1)
    part = lax.broadcasted_iota(jnp.int32, (lines, size), 1) // (size // groups)

    def one(b, vals):
        trust = F32(0.85) * inflow[b] + F32(0.15) * good_ref[b]
        trust_ref[pl.ds(pl.multiple_of(b * size, size), size), :] = jnp.transpose(trust)
        shield = F32(1) / (F32(1) + trust)
        shield_ref[b] = shield
        share = (shield * spam_ref[b] / weight_ref[pl.ds(b, 1), :]).astype(BF16).astype(F32)
        for g in range(groups):
            got = take(share[g * lines : (g + 1) * lines, :], lanes)
            vals = jnp.where((block == b) & (part == g), got, vals)
        return vals

    vals = lax.fori_loop(0, blocks, one, jnp.zeros((lines, size), F32), unroll=2)
    vals_ref[...] = vals.astype(BF16)


def pull_kernel(last, *refs):
    if last:
        src_ref, slot_ref, fetched_ref, spam_ref, tiles_ref, out_ref, acc = refs
    else:
        (src_ref, slot_ref, block_ref, lists_ref, vals_ref, rank_ref, spam_ref, shield_ref, weight_ref,
         tiles_ref, out_ref, acc, fetched_ref, codes, bounds, sem) = refs
    step = pl.program_id(0)
    per_step = tiles_ref.shape[0]
    size = acc.shape[2]

    @pl.when(step == 0)
    def _():
        acc[...] = jnp.zeros_like(acc)
        if not last:
            blocks = acc.shape[0]
            codes[...] = lists_ref[:, 0, :].astype(jnp.int32) // (blocks * size)
            copy = pltpu.make_async_copy(codes, bounds, sem)
            copy.start()
            copy.wait()
            expand(
                block_ref.shape[0] // lists_ref.shape[0], block_ref, lists_ref, vals_ref, rank_ref,
                blocks, bounds, fetched_ref,
            )

    def some(g, _):
        products = []
        for k in range(GROUP):
            n = step * per_step + g * GROUP + k
            tile, got = tiles_ref[g * GROUP + k], fetched_ref[slot_ref[n]]
            if last:
                products.append(jnp.dot(tile, got, preferred_element_type=F32))
            else:
                products.append(
                    lax.dot_general(got, tile, (((1,), (1,)), ((), ())), preferred_element_type=F32)
                )
        for k in range(GROUP):
            acc[src_ref[step * per_step + g * GROUP + k]] += products[k]
        return 0

    lax.fori_loop(0, per_step // GROUP, some, 0)

    @pl.when(step == pl.num_programs(0) - 1)
    def _():
        def distrust(b):
            return F32(0.85) * acc[b] + F32(0.15) * spam_ref[b]

        if last:
            def one(b, _):
                out_ref[pl.ds(pl.multiple_of(b * size, size), size), :] = distrust(b)
                return 0

            lax.fori_loop(0, acc.shape[0], one, 0, unroll=2)
        else:
            shares(shield_ref, weight_ref, distrust, out_ref)


def start_kernel(columns, good_ref, spam_ref, tiles_ref, count_ref, list_ref, near_ref, tally, sem):
    load = pltpu.make_async_copy(tiles_ref, near_ref, sem)
    load.start()
    list_ref[...] = jnp.transpose(spam_ref[...].astype(F32)).astype(jnp.int32)
    count_seeds(columns, good_ref, tally)
    spread_seeds(good_ref.shape[1], tally, count_ref)
    load.wait()


def body(columns, tiles, tile_src, tile_slot, slot_block, out_degree, good_seeds, spam_cores):
    tile_count, size, _ = tiles.shape
    here = lambda x: pltpu.with_memory_space_constraint(x, pltpu.HBM)
    hosts = out_degree.shape[0]
    blocks = hosts // size
    seeds = good_seeds.shape[0]
    slots = slot_block.shape[0]
    peers = lax.axis_size(AXES)
    cap = slots // peers
    tail = -(-4 * cap // 16) * 16
    steps = 1
    shape = jax.ShapeDtypeStruct
    vector = (blocks, seeds, size)
    degree = out_degree.reshape(blocks, 1, size)

    rows = peers // columns
    part = seeds // HALVES
    count = spam_cores.shape[1]
    groups = seeds // count
    lines = seeds // groups
    good, spam_list, tiles = pl.pallas_call(
        functools.partial(start_kernel, columns),
        out_shape=(
            shape(vector, F32), shape(spam_cores.shape, jnp.int32), shape(tiles.shape, BF16),
        ),
        in_specs=[VM, VM, ANY],
        out_specs=(VM, VM, VM),
        scratch_shapes=[pltpu.VMEM((seeds, blocks, size), F32), pltpu.SemaphoreType.DMA],
        compiler_params=PLAIN,
        cost_estimate=pl.CostEstimate(
            flops=2 * seeds * good_seeds.size * (blocks + size), transcendentals=0,
            bytes_accessed=24 << 20,
        ),
    )(here(good_seeds), here(spam_cores.T), here(tiles))

    tile_spec = VM
    words = shape((peers, cap * size + tail, size), jnp.int16)
    outgoing = pl.pallas_call(
        functools.partial(push_kernel, True, cap, part),
        grid=(steps,),
        out_shape=words,
        in_specs=[SM, SM, SM, VM, VM, tile_spec],
        out_specs=VM,
        scratch_shapes=[
            pltpu.VMEM((slots, seeds + 16, size), F32),
            pltpu.VMEM((blocks, seeds + 16, size), BF16),
        ],
        compiler_params=PLAIN,
    )(here(tile_src), here(tile_slot), here(slot_block), good, here(degree), tiles)

    dma = pltpu.SemaphoreType.DMA
    spread_sems = [
        dma((columns,)), dma((columns,)), dma((rows, columns)), dma((rows, columns)),
        dma((rows, columns)), dma((rows, columns)),
    ]

    def reduce(first, words_in, *rest):
        long = blocks * part + blocks * (4 if first else 1)
        outs = (
            shape(vector, F32), shape((blocks, size), F32), shape(vector, F32),
            shape((rows, 1, slots), jnp.int32), shape((lines, size), jnp.int16),
            shape((peers, lines, size), jnp.int16),
        )
        if not first:
            outs = (shape(vector, F32), shape((peers, seeds, size), jnp.int32))
        return pl.pallas_call(
            functools.partial(reduce_kernel, first, rows, columns, cap),
            out_shape=outs,
            in_specs=[ANY, VM, VM, VM] if first else [ANY, VM],
            out_specs=(VM,) * len(outs),
            scratch_shapes=[
                pltpu.VMEM((columns, rows, cap * size + tail, size), jnp.int16),
                pltpu.VMEM((rows * cap, blocks, size), F32),
                pltpu.VMEM((blocks, part, size), F32),
                pltpu.VMEM((blocks, size), F32),
                pltpu.VMEM((blocks, size), F32),
                pltpu.VMEM((columns - 1, HALVES, long, size), jnp.int16),
                pltpu.VMEM((2, columns, HALVES, long, size), jnp.int16),
                dma((columns,)),
                dma((columns, HALVES, rows)),
                dma((columns, HALVES, rows)),
                dma((columns - 1, HALVES)),
                dma((2, columns, HALVES)),
                *([dma((rows,)), dma((rows,)), pltpu.VMEM((seeds, blocks, size), F32), *spread_sems] if first else []),
            ],
            compiler_params=pltpu.CompilerParams(
                collective_id=1 if first else 2, has_side_effects=True,
                vmem_limit_bytes=LIMIT,
            ),
        )(words_in, *rest)

    inflow, weight, spam, want, keys, lists = reduce(
        True, outgoing, spam_list, slot_block.reshape(1, slots), spam_cores.T
    )
    outgoing = pl.pallas_call(
        functools.partial(push_kernel, False, cap, part),
        grid=(steps,),
        out_shape=words,
        in_specs=[SM, SM, SM, VM, VM, VM, tile_spec],
        out_specs=VM,
        scratch_shapes=[
            pltpu.VMEM((slots, seeds, size), F32),
            pltpu.VMEM(vector, BF16),
        ],
        compiler_params=PLAIN,
    )(tile_src, tile_slot, slot_block, inflow, good, degree, tiles)
    inflow, ranks = reduce(False, outgoing, lists)
    fetch = pl.pallas_call(
        functools.partial(fetch_kernel, rows, columns, cap),
        out_shape=shape((slots, seeds, size), BF16),
        in_specs=[SM, VM],
        out_specs=VM,
        scratch_shapes=[
            *[pltpu.VMEM((blocks, size // PARTS, seeds), BF16)] * ((2 * columns - 2) * PARTS),
            pltpu.VMEM((rows, columns * cap, size, seeds), BF16),
            pltpu.SemaphoreType.DMA(((2 * columns - 2) * PARTS,)),
            pltpu.SemaphoreType.DMA(((2 * columns - 2) * PARTS,)),
            pltpu.SemaphoreType.DMA((rows, columns * PARTS)),
            pltpu.SemaphoreType.DMA((rows, columns * PARTS)),
        ],
        compiler_params=pltpu.CompilerParams(collective_id=0, has_side_effects=True, vmem_limit_bytes=LIMIT),
    )
    trust, shield, vals = pl.pallas_call(
        trust_kernel,
        out_shape=(shape((hosts, seeds), F32), shape(vector, F32), shape((lines, size), BF16)),
        in_specs=[VM, VM, VM, VM, VM],
        out_specs=(VM, VM, VM),
        compiler_params=PLAIN,
    )(inflow, good, spam, weight, keys)
    vals, turned = pl.pallas_call(
        functools.partial(value_kernel, rows, columns),
        out_shape=(shape((peers, lines, size), BF16), shape(vector, F32)),
        in_specs=[VM, VM],
        out_specs=(VM, VM),
        scratch_shapes=spread_sems,
        compiler_params=pltpu.CompilerParams(
            collective_id=3, has_side_effects=True, vmem_limit_bytes=LIMIT
        ),
    )(vals, spam)
    share = pl.pallas_call(
        functools.partial(pull_kernel, False),
        grid=(steps,),
        out_shape=shape(vector, BF16),
        in_specs=[SM, SM, SM, VM, VM, VM, VM, VM, VM, tile_spec],
        out_specs=VM,
        scratch_shapes=[
            pltpu.VMEM(vector, F32),
            pltpu.VMEM((slots, seeds, size), BF16),
            pltpu.VMEM((peers, size), jnp.int32),
            pltpu.SMEM((peers, size), jnp.int32),
            pltpu.SemaphoreType.DMA,
        ],
        compiler_params=PLAIN,
    )(tile_src, tile_slot, slot_block, lists, vals, ranks, spam, shield, weight, tiles)
    fetched = fetch(want, share)
    distrust = pl.pallas_call(
        functools.partial(pull_kernel, True),
        grid=(steps,),
        out_shape=shape((hosts, seeds), F32),
        in_specs=[SM, SM, VM, VM, tile_spec],
        out_specs=VM,
        scratch_shapes=[pltpu.VMEM(vector, F32)],
        compiler_params=PLAIN,
    )(tile_src, tile_slot, fetched, turned, tiles)
    return trust, distrust


def solution(mesh):
    in_specs = (
        P(AXES, None, None),
        P(AXES),
        P(AXES),
        P(AXES),
        P(AXES),
        P(None, AXES),
        P(None, AXES),
    )
    out_specs = (P(AXES, None), P(AXES, None))
    return jax.shard_map(
        functools.partial(body, mesh.shape["col"]),
        mesh=mesh, in_specs=in_specs, out_specs=out_specs, check_vma=False,
    )
```
